32 devices in a mesh: dp: 4 (over y, x), expert: 8 (over z, core).
Axes of the slice: x: 2, y: 2, z: 4, core: 2. Of those that a mesh axis runs over, the one named last changes fastest.
Arguments:
- tokens: bfloat16 [32768, 768], P(('dp', 'expert')), may hold values from -6 to 6
- routes: int32 [32768, 1], P(('dp', 'expert')), may hold values from 0 to 15
- slot_order: int32 [32768], P(('dp', 'expert')), may hold values from 0 to 1023, as said below
- prefix_len: int32 [32], P(('dp', 'expert')), may hold values from 102 to 512
- ln1_gain: float32 [768], replicated, may hold values from 0.5 to 1.5
- ln1_bias: float32 [768], replicated, may hold values from -0.6 to 0.6
- mixer_weight: bfloat16 [768, 3072], P(None, ('dp', 'expert')), may hold values from -0.3125 to 0.3125
- ln2_gain: float32 [768], replicated, may hold values from 0.5 to 1.5
- ln2_bias: float32 [768], replicated, may hold values from -0.6 to 0.6
- router_weight: bfloat16 [768, 16], replicated, may hold values from -0.15625 to 0.15625
- expert_in: bfloat16 [16, 3072, 768], P('expert', 'dp'), may hold values from -0.21875 to 0.21875
- expert_out: bfloat16 [16, 3072, 768], P('expert', 'dp'), may hold values from -0.3125 to 0.3125
- cotangent: bfloat16 [32768, 768], P(('dp', 'expert')), may hold values from -6 to 6
Outputs:
- mixed_out: bfloat16 [32768, 768], P(('dp', 'expert'))
- tokens_grad: float32 [32768, 768], P(('dp', 'expert'))
- ln1_gain_grad: float32 [768], replicated
- ln1_bias_grad: float32 [768], replicated
- mixer_grad: float32 [768, 3072], P(None, ('dp', 'expert'))
- ln2_gain_grad: float32 [768], replicated
- ln2_bias_grad: float32 [768], replicated
- router_grad: float32 [768, 16], replicated
- expert_in_grad: float32 [16, 3072, 768], P('expert', 'dp')
- expert_out_grad: float32 [16, 3072, 768], P('expert', 'dp')
- balance: float32 [], replicated
The draws below stay inside these ranges and needn't reach their ends.
Inputs may be any that keep to these rules, and one draw needn't show every extreme that they name: `routes`: every expert is named by some token. `slot_order`: within each aligned block of 1024 tokens every value appears once.
All inputs are finite; a program needn't handle non-finite values.
Results may differ from the reference program's by a relative error of at most 0.015.
The reference program's roundings to bfloat16 on the way count: a program that leaves them out, or rounds other values in their place, can miss the bound.
Values may be sent and summed in bfloat16 or wider, within the bound.
A program may use at most 256 MiB of HBM per device.

```python
from functools import partial
import jax
import jax.numpy as jnp
from jax import lax

D = 768
HEADS = 12
HEAD_DIM = 64
FF = 3072
SEQ = 1024
TOK_DEV = 1024
TOKENS = 32768
SEQS = 32
EXPERTS = 16
CAP = 64
N_DP = 4
N_EXPERT = 8


def draw_slot_order(key, part):
    block_keys = jax.random.split(key, TOKENS // TOK_DEV)
    orders = jax.vmap(lambda block_key: jax.random.permutation(block_key, TOK_DEV))(block_keys)
    return orders.reshape(TOKENS).astype(jnp.int32)


def draw_prefix_len(key, part):
    first_key, second_key, third_key = jax.random.split(key, 3)
    lengths = jax.random.randint(first_key, (SEQS,), SEQ // 10, SEQ // 2 + 1)
    longest = jax.random.randint(second_key, (), 0, SEQS)
    shortest = (longest + jax.random.randint(third_key, (), 1, SEQS)) % SEQS
    lengths = lengths.at[longest].set(SEQ // 2).at[shortest].set(SEQ // 10)
    return lengths.astype(jnp.int32)


def with_spikes(drawn, stream_key, source, target, shards_of, factor):
    def block_of(position):
        return (jnp.arange(drawn.shape[position]) // (drawn.shape[position] // shards_of)).reshape((-1,) + (1,) * (drawn.ndim - 1 - position))

    near = jax.random.permutation(stream_key, shards_of)[block_of(target)]
    other_side = (block_of(target) + shards_of // 2) % shards_of
    return jnp.where((block_of(source) == near) | (block_of(source) == other_side), factor * drawn, drawn)


def block_levels(stream_key, dims, shards, smallest, top_value):
    loudness = 1.0
    for position, blocks in shards:
        draws = jax.random.uniform(jax.random.fold_in(jax.random.fold_in(stream_key, 6), position), (blocks,), jnp.float32, smallest / len(shards), top_value / len(shards))
        loudness = loudness * jnp.repeat(jnp.exp(draws), dims[position] // blocks).reshape((-1,) + (1,) * (len(dims) - 1 - position))
    return loudness


def choose_distinct(rng, rows, count, top, lift):
    sequence = jax.random.permutation(jax.random.fold_in(rng, 1), count)
    pull = sequence
    for power in range(3):
        pull = pull * pull // count
    pull = pull * lift // count
    chance = jax.random.randint(jax.random.fold_in(rng, 2), (rows, count), 0, 4096) + pull
    holders = jax.random.permutation(jax.random.fold_in(rng, 3), rows)[jnp.arange(count) % rows]
    chance = jnp.where(jnp.arange(rows)[:, None] == holders[None, :], 1 << 14, chance)
    merit = chance * count + jnp.arange(count)
    return lax.top_k(merit.astype(jnp.int32), top)[1].astype(jnp.int32)


def scatter_about(own_key, dims, scale, limit, shards=(), kind=jnp.bfloat16):
    drawn = jax.random.normal(own_key, dims, jnp.float32) * scale
    if len(shards) > 0:
        drawn = block_levels(own_key, dims, shards, -0.22, 0.18) * drawn
    return jnp.clip(drawn, min=-limit, max=limit).astype(kind)


def bell_draw_with(key, dims, scale, limit, pieces, heavy, kind=jnp.bfloat16):
    values = scale * jax.random.normal(key, dims, jnp.float32)
    if pieces:
        values = values * block_levels(key, dims, pieces, -0.22, 0.18)
    return jnp.clip(with_spikes(values, jax.random.fold_in(key, 3), *heavy), -limit, limit).astype(kind)


def setup_inputs(seed: int = 0) -> dict:
    arg_keys = jax.random.split(jax.random.key(seed), 14)
    return {
        "tokens": scatter_about(arg_keys[0], (TOKENS, D), 1.0, 6.0, ((0, 32),)),
        "routes": choose_distinct(arg_keys[1], TOKENS, EXPERTS, 1, 512),
        "slot_order": draw_slot_order(jax.random.fold_in(arg_keys[13], 71), 0),
        "prefix_len": draw_prefix_len(jax.random.fold_in(arg_keys[13], 71), 0),
        "ln1_gain": jnp.clip(1.0 + 0.1 * jax.random.normal(arg_keys[4], (D,), jnp.float32), 0.5, 1.5),
        "ln1_bias": scatter_about(arg_keys[5], (D,), 0.1, 0.6, (), jnp.float32),
        "mixer_weight": scatter_about(arg_keys[6], (D, 4 * D), (D // 2) ** -0.5, 0.3125, ((1, 32),)),
        "ln2_gain": jnp.clip(1.0 + 0.1 * jax.random.normal(arg_keys[7], (D,), jnp.float32), 0.5, 1.5),
        "ln2_bias": scatter_about(arg_keys[8], (D,), 0.1, 0.6, (), jnp.float32),
        "router_weight": scatter_about(arg_keys[9], (D, EXPERTS), (2 * D) ** -0.5, 0.15625),
        "expert_in": scatter_about(arg_keys[10], (EXPERTS, FF, D), D ** -0.5, 0.21875, ((0, 8), (1, 4))),
        "expert_out": scatter_about(arg_keys[11], (EXPERTS, FF, D), (FF // 8) ** -0.5, 0.3125, ((0, 8), (1, 4))),
        "cotangent": bell_draw_with(arg_keys[12], (TOKENS, D), 1.0, 6.0, ((0, 32),), (0, 1, 32, 2.75)),
    }


epsilon = 1e-05
masked_score = -1000000000.0

@jax.custom_vjp
def low(v):
    return lax.optimization_barrier(v.astype(jnp.bfloat16)).astype(jnp.float32)

@jax.custom_vjp
def low_back(v):
    return v

def low_keep(v):
    return (low(v), None)

def low_pass(kept, grad):
    return (grad,)

def back_keep(v):
    return (v, None)

def back_low(kept, grad):
    return (low(grad),)
low.defvjp(low_keep, low_pass)
low_back.defvjp(back_keep, back_low)

def highest_dot(first_op, second_op):
    return jnp.dot(first_op, second_op, precision=lax.Precision.HIGHEST, preferred_element_type=jnp.float32)

def layer_norm(values, gain_vec, offset):
    center = values - lax.optimization_barrier(jnp.mean(values, axis=-1, keepdims=True))
    spread = lax.optimization_barrier(jnp.mean(center * center, axis=-1, keepdims=True))
    return center * lax.rsqrt(spread + epsilon) * gain_vec + offset

def attend_sequence(packed):
    query_rows, key_rows, value_rows, prefix = packed
    heads_query = query_rows.reshape(SEQ, HEADS, HEAD_DIM)
    heads_key = key_rows.reshape(SEQ, HEADS, HEAD_DIM)
    heads_value = value_rows.reshape(SEQ, HEADS, HEAD_DIM)
    scores = jnp.einsum('qhd,khd->hqk', heads_query, heads_key, precision=lax.Precision.HIGHEST) * HEAD_DIM ** (-0.5)
    scores = low_back(scores)
    places = jnp.arange(SEQ)
    visible = (places[None, :] <= places[:, None]) | (places[None, :] < prefix)
    scores = jnp.where(visible[None], scores, masked_score)
    maxima = lax.optimization_barrier(jnp.max(scores, axis=-1, keepdims=True))
    weights = jnp.exp(scores - maxima)
    probabilities = low(weights / lax.optimization_barrier(jnp.sum(weights, axis=-1, keepdims=True)))
    heads_out = jnp.einsum('hqk,khd->qhd', probabilities, heads_value, precision=lax.Precision.HIGHEST)
    return heads_out.reshape(SEQ, HEADS * HEAD_DIM)

def expert_apply(packed):
    expert_rows, weight_in, weight_out = packed
    pre_act = low_back(jnp.einsum('ncd,fd->ncf', expert_rows, weight_in, precision=lax.Precision.HIGHEST))
    activated = low(jax.nn.gelu(pre_act, approximate=False))
    return low_back(low(jnp.einsum('ncf,fd->ncd', activated, weight_out, precision=lax.Precision.HIGHEST)))

def group_forward(weights_pack, packed):
    ln1_gain, ln1_bias, mixer_weight, ln2_gain, ln2_bias, router_weight, expert_in, expert_out = weights_pack
    group_rows, group_prefix, group_hot, group_slot, group_weight = packed
    model_width = group_rows.shape[1]
    normed = low(layer_norm(group_rows, ln1_gain, ln1_bias))
    projected = low_back(low(highest_dot(normed, mixer_weight[:, :3 * model_width])))
    seq_total = group_rows.shape[0] // SEQ
    queries = projected[:, :model_width].reshape(seq_total, SEQ, model_width)
    key_part = projected[:, model_width:2 * model_width].reshape(seq_total, SEQ, model_width)
    value_part = projected[:, 2 * model_width:].reshape(seq_total, SEQ, model_width)
    attended = lax.map(jax.checkpoint(attend_sequence), (queries, key_part, value_part, group_prefix))
    attended = low_back(low(attended.reshape(-1, model_width)))
    middle = group_rows + low_back(highest_dot(attended, mixer_weight[:, 3 * model_width:]))
    normed2 = low(layer_norm(middle, ln2_gain, ln2_bias))
    chosen = lax.optimization_barrier(jnp.sum(low_back(highest_dot(normed2, router_weight)) * group_hot, axis=1))
    gate_value = jax.nn.sigmoid(chosen)
    block_count = group_rows.shape[0] // TOK_DEV
    blocks = normed2.reshape(block_count, TOK_DEV, model_width)
    slotted = jax.vmap(partial(jax.ops.segment_sum, num_segments=EXPERTS * CAP + 1))(blocks, group_slot)[:, :EXPERTS * CAP]
    per_expert = low_back(slotted.reshape(block_count, EXPERTS, CAP, model_width).transpose(1, 0, 2, 3))
    produced = lax.map(jax.checkpoint(expert_apply), (per_expert, expert_in, expert_out))
    back_rows = produced.transpose(1, 0, 2, 3).reshape(block_count, EXPERTS * CAP, model_width)
    back_rows = jnp.concatenate([back_rows, jnp.zeros((block_count, 1, model_width), back_rows.dtype)], axis=1)
    returned = jnp.take_along_axis(back_rows, group_slot[:, :, None], axis=1).reshape(-1, model_width)
    output = middle + gate_value[:, None] * returned
    return (output, jnp.sum(group_weight * gate_value))

def forward(constants, tokens, ln1_gain, ln1_bias, mixer_weight, ln2_gain, ln2_bias, router_weight, expert_in, expert_out):
    prefix_len, route_hot, slot_index, load_weight = constants
    weights_pack = (ln1_gain, ln1_bias, mixer_weight, ln2_gain, ln2_bias, router_weight, expert_in, expert_out)
    group_size = N_EXPERT * TOK_DEV

    def group_step(packed):
        return group_forward(weights_pack, packed)
    packed = (tokens.reshape(N_DP, group_size, -1), prefix_len.reshape(N_DP, -1), route_hot.reshape(N_DP, group_size, -1), slot_index.reshape(N_DP, N_EXPERT, TOK_DEV), load_weight.reshape(N_DP, group_size))
    outputs, balances = lax.map(jax.checkpoint(group_step), packed)
    return (outputs.reshape(TOKENS, -1), jnp.sum(balances))

def block_rank(packed):
    order_block, route_block = packed
    same_expert = route_block[:, None] == route_block[None, :]
    earlier = order_block[None, :] < order_block[:, None]
    return lax.optimization_barrier(jnp.sum((same_expert & earlier).astype(jnp.int32), axis=1))

def reference(tokens, routes, slot_order, prefix_len, ln1_gain, ln1_bias, mixer_weight, ln2_gain, ln2_bias, router_weight, expert_in, expert_out, cotangent):
    route_flat = routes[:, 0]
    route_hot = (route_flat[:, None] == jnp.arange(EXPERTS)[None, :]).astype(jnp.float32)
    counts = lax.optimization_barrier(jnp.sum(route_hot, axis=0))
    mean_load = TOKENS / EXPERTS
    load_weight = (lax.optimization_barrier(jnp.sum(route_hot * counts[None, :], axis=1)) - mean_load) / mean_load / TOKENS
    order_blocks = slot_order.reshape(N_DP * N_EXPERT, TOK_DEV)
    route_blocks = route_flat.reshape(N_DP * N_EXPERT, TOK_DEV)
    slot_rank = lax.map(block_rank, (order_blocks, route_blocks))
    slot_index = jnp.where(slot_rank < CAP, route_blocks * CAP + slot_rank, EXPERTS * CAP).astype(jnp.int32)
    constants = (prefix_len, route_hot, slot_index, load_weight)
    (output, balance), pullback = jax.vjp(partial(forward, constants), tokens.astype(jnp.float32), ln1_gain.astype(jnp.float32), ln1_bias.astype(jnp.float32), mixer_weight.astype(jnp.float32), ln2_gain.astype(jnp.float32), ln2_bias.astype(jnp.float32), router_weight.astype(jnp.float32), expert_in.astype(jnp.float32), expert_out.astype(jnp.float32))
    gradients = pullback((cotangent.astype(jnp.float32), jnp.ones_like(balance)))
    return (output.astype(jnp.bfloat16), gradients[0], gradients[1], gradients[2], gradients[3], gradients[4], gradients[5], gradients[6], gradients[7], gradients[8], balance)
```

```python
import functools

import jax
import jax.numpy as jnp
from jax import lax
from jax.experimental import pallas as pl
from jax.experimental.pallas import tpu as pltpu
from jax.sharding import PartitionSpec as P


epsilon = 1e-05
masked_score = -1000000000.0


def layer_norm(values, gain_vec, offset):
    center = values - jnp.mean(values, axis=-1, keepdims=True)
    spread = jnp.mean(center * center, axis=-1, keepdims=True)
    return center * lax.rsqrt(spread + epsilon) * gain_vec + offset


def exact_gelu(values):
    return jax.nn.gelu(values, approximate=False)


def contract_rows(first_op, second_op):
    return lax.dot_general(
        first_op, second_op, (((0,), (0,)), ((), ())), preferred_element_type=jnp.float32
    )


def times_transposed(first_op, second_op):
    return lax.dot_general(
        first_op, second_op, (((1,), (1,)), ((), ())), preferred_element_type=jnp.float32
    )


BF=jnp.bfloat16; F32=jnp.float32
NEG=-1e9
QB=256
def key_extent(i, n):
    return max((i+1)*QB, 512)

def nt(a,b): return lax.dot_general(a,b,(((1,),(1,)),((),())),preferred_element_type=F32)
def nn(a,b): return lax.dot_general(a,b,(((1,),(0,)),((),())),preferred_element_type=F32)

def fill_bias(bias_ref, prefix):
    kp=lax.broadcasted_iota(jnp.int32,(QB,QB),0); qp=lax.broadcasted_iota(jnp.int32,(QB,QB),1)
    causal=kp<=qp
    bias_ref[0]=jnp.where(causal|(kp<prefix),0.0,NEG)
    bias_ref[1]=jnp.where(kp+QB<prefix,0.0,NEG)+jnp.zeros((QB,QB),F32)
    bias_ref[2]=jnp.where(causal|(kp+QB<prefix),0.0,NEG)
    bias_ref[3]=jnp.where(causal,0.0,NEG)

def block_bias(j,i):
    if j==0 and i==0: return 0
    if j==1 and i==0: return 1
    if j==1 and i==1: return 2
    if j==i: return 3
    return None

def fwd_kernel(pre_ref,q_ref,k_ref,v_ref,o_ref,lse_ref,bias_ref):
    @pl.when(pl.program_id(0)==0)
    def _(): fill_bias(bias_ref,pre_ref[0])
    T=q_ref.shape[0]
    lane=lax.broadcasted_iota(jnp.int32,(1,128),1)
    vT=v_ref[...].T
    ones=jnp.ones((16,T),BF)
    for i in range(T//QB):
        K=key_extent(i,T)
        q=q_ref[i*QB:(i+1)*QB,:]*jnp.asarray(0.125,BF)
        outs=[]
        for h in range(2):
            qh=jnp.where((lane<64) if h==0 else (lane>=64), q, jnp.zeros_like(q))
            parts=[]
            for j in range(K//QB):
                s=nt(k_ref[j*QB:(j+1)*QB,:],qh)
                b=block_bias(j,i)
                if b is not None: s=s+bias_ref[b]
                parts.append(s)
            m=functools.reduce(jnp.maximum,[jnp.max(s,axis=0,keepdims=True) for s in parts])
            vh=jnp.concatenate([vT[h*64:(h+1)*64],ones],axis=0)
            acc=None
            for j,s in enumerate(parts):
                p=jnp.exp(s-m).astype(BF)
                c=nn(vh[:,j*QB:(j+1)*QB],p)
                acc=c if acc is None else acc+c
            l=acc[64:65]
            outs.append(acc[:64]*(1.0/l))
            lse_ref[0,h:h+1,i*QB:(i+1)*QB]=m+jnp.log(l)
        o_ref[i*QB:(i+1)*QB,:]=jnp.concatenate(outs,axis=0).T.astype(BF)

def attn_fwd(prefix,proj):
    T=proj.shape[0]; W=proj.shape[1]//3; n=W//128
    return pl.pallas_call(fwd_kernel,grid=(n,),
        in_specs=[pl.BlockSpec(memory_space=pltpu.SMEM)]+[pl.BlockSpec((T,128),functools.partial(lambda c,j:(0,c*n+j),c)) for c in range(3)],
        out_specs=[pl.BlockSpec((T,128),lambda j:(0,j)),pl.BlockSpec((1,2,T),lambda j:(j,0,0))],
        out_shape=[jax.ShapeDtypeStruct((T,W),BF),jax.ShapeDtypeStruct((n,2,T),F32)],
        scratch_shapes=[pltpu.VMEM((4,QB,QB),F32)],
        compiler_params=pltpu.CompilerParams(vmem_limit_bytes=60<<20),
        name="attn_fwd")(prefix,proj,proj,proj)

def bwd_kernel(pre_ref,q_ref,k_ref,v_ref,o_ref,g_ref,lse_ref,dq_ref,dk_ref,dv_ref,bias_ref,dk_acc,dv_acc):
    @pl.when(pl.program_id(0)==0)
    def _(): fill_bias(bias_ref,pre_ref[0])
    T=q_ref.shape[0]; nb=T//QB
    lane=lax.broadcasted_iota(jnp.int32,(1,128),1)
    kT=k_ref[...].T
    started=[False]*nb
    for i in range(nb-1,-1,-1):
        K=key_extent(i,T)
        rows=slice(i*QB,(i+1)*QB)
        q=q_ref[rows,:]*jnp.asarray(0.125,BF)
        g=g_ref[rows,:]
        dT=(g.astype(F32)*o_ref[rows,:].astype(F32)).T
        outs=[]
        for h in range(2):
            sel=(lane<64) if h==0 else (lane>=64)
            qh=jnp.where(sel,q,jnp.zeros_like(q)); gh=jnp.where(sel,g,jnp.zeros_like(g))
            lse=lse_ref[0,h:h+1,rows]
            delta=jnp.sum(dT[h*64:(h+1)*64],axis=0,keepdims=True)
            dq=None
            for j in range(K//QB):
                kr=slice(j*QB,(j+1)*QB)
                s=nt(k_ref[kr,:],qh)
                b=block_bias(j,i)
                if b is not None: s=s+bias_ref[b]
                p=jnp.exp(s-lse)
                dp=nt(v_ref[kr,:],gh)
                ds=(p*(dp-delta)).astype(BF)
                dv=nn(p.astype(BF),gh)
                dk=nn(ds,qh)
                first=(i==nb-1 and h==0)
                if first: dv_acc[kr,:]=dv; dk_acc[kr,:]=dk
                else:
                    dv_acc[kr,:]+=dv; dk_acc[kr,:]+=dk
                c=nn(kT[h*64:(h+1)*64,kr],ds)
                dq=c if dq is None else dq+c
            outs.append(dq)
        dq_ref[rows,:]=(jnp.concatenate(outs,axis=0).T*0.125).astype(BF)
    dk_ref[...]=dk_acc[...].astype(BF)
    dv_ref[...]=dv_acc[...].astype(BF)

def attn_bwd(prefix,proj,att,grad,lse):
    T=proj.shape[0]; W=proj.shape[1]//3; n=W//128
    cb=lambda: pl.BlockSpec((T,128),lambda j:(0,j))
    return pl.pallas_call(bwd_kernel,grid=(n,),
        in_specs=[pl.BlockSpec(memory_space=pltpu.SMEM)]+[pl.BlockSpec((T,128),functools.partial(lambda c,j:(0,c*n+j),c)) for c in range(3)]
          +[cb(),cb(),pl.BlockSpec((1,2,T),lambda j:(j,0,0))],
        out_specs=[cb()]*3,
        out_shape=[jax.ShapeDtypeStruct((T,W),BF)]*3,
        scratch_shapes=[pltpu.VMEM((4,QB,QB),F32),pltpu.VMEM((T,128),F32),pltpu.VMEM((T,128),F32)],
        compiler_params=pltpu.CompilerParams(vmem_limit_bytes=60<<20),
        name="attn_bwd")(prefix,proj,proj,proj,att,grad,lse)


def on_device(
    tokens,
    routes,
    slot_order,
    prefix_len,
    ln1_gain,
    ln1_bias,
    mixer_weight,
    ln2_gain,
    ln2_bias,
    router_weight,
    expert_in,
    expert_out,
    cotangent,
):
    model_width = tokens.shape[1]
    token_count = tokens.shape[0]
    expert_total = router_weight.shape[1]
    local_experts = expert_in.shape[0]
    capacity = token_count // expert_total
    owner_count = lax.axis_size("expert")
    full_mixer = lax.all_gather(mixer_weight, ("dp", "expert"), axis=1, tiled=True)
    inner_weight = full_mixer[:, : 3 * model_width]
    outer_weight = full_mixer[:, 3 * model_width :]
    inputs = tokens.astype(jnp.float32)
    normed, norm_pull = jax.vjp(layer_norm, inputs, ln1_gain, ln1_bias)
    normed_low = normed.astype(jnp.bfloat16)
    projected = jnp.dot(normed_low, inner_weight, preferred_element_type=jnp.float32).astype(
        jnp.bfloat16
    )
    attended, head_lse = attn_fwd(prefix_len, projected)
    middle = inputs + jnp.dot(attended, outer_weight, preferred_element_type=jnp.float32)
    normed2, norm2_pull = jax.vjp(layer_norm, middle, ln2_gain, ln2_bias)
    normed2_low = normed2.astype(jnp.bfloat16)
    route_flat = routes[:, 0]
    route_hot = route_flat[:, None] == jnp.arange(expert_total)[None, :]
    route_float = route_hot.astype(jnp.float32)
    logits = jnp.dot(normed2_low, router_weight, preferred_element_type=jnp.float32)
    chosen = jnp.sum(logits * route_float, axis=1)
    gate_value = jax.nn.sigmoid(chosen)
    counts = lax.psum(jnp.sum(route_float, axis=0), ("dp", "expert"))
    earlier = (slot_order[None, :] < slot_order[:, None]).astype(jnp.bfloat16)
    ahead_count = jnp.dot(
        earlier, route_hot.astype(jnp.bfloat16), preferred_element_type=jnp.float32
    )
    slot_rank = jnp.sum(ahead_count * route_float, axis=1).astype(jnp.int32)
    slot_index = route_flat * capacity + slot_rank
    is_kept = slot_rank < capacity
    slot_hot = (
        (slot_index[:, None] == jnp.arange(expert_total * capacity)[None, :]) & is_kept[:, None]
    ).astype(jnp.bfloat16)
    slotted = contract_rows(slot_hot, normed2_low).astype(jnp.bfloat16)
    outgoing = slotted.reshape(owner_count, local_experts * capacity, model_width)
    arrived = lax.all_to_all(outgoing, "expert", split_axis=0, concat_axis=0, tiled=True).reshape(
        owner_count, local_experts, capacity, model_width
    )
    full_in, full_out = (
        lax.all_gather(expert_in, "dp", axis=1, tiled=True),
        lax.all_gather(expert_out, "dp", axis=1, tiled=True),
    )
    pre_act = jnp.einsum("secd,efd->secf", arrived, full_in, preferred_element_type=jnp.float32)
    activated = exact_gelu(pre_act).astype(jnp.bfloat16)
    produced = jnp.einsum(
        "secf,efd->secd", activated, full_out, preferred_element_type=jnp.float32
    ).astype(jnp.bfloat16)
    returned_slots = lax.all_to_all(
        produced.reshape(owner_count, local_experts * capacity, model_width),
        "expert",
        split_axis=0,
        concat_axis=0,
        tiled=True,
    )
    returned = jnp.dot(
        slot_hot,
        returned_slots.reshape(expert_total * capacity, model_width),
        preferred_element_type=jnp.float32,
    )
    output = middle + gate_value[:, None] * returned
    mixed_out = output.astype(jnp.bfloat16)
    out_grad = cotangent.astype(jnp.float32)
    mean_load = jnp.sum(counts) / expert_total
    load_weight = (
        (jnp.sum(route_float * counts[None, :], axis=1) - mean_load) / mean_load / jnp.sum(counts)
    )
    balance_part = jnp.sum(load_weight * gate_value)
    gate_grad = jnp.sum(out_grad * returned, axis=1) + load_weight
    logit_grad = gate_grad * gate_value * (1.0 - gate_value)
    logit_full = (logit_grad[:, None] * route_float).astype(jnp.bfloat16)
    router_part = contract_rows(normed2_low, logit_full)
    normed2_grad = times_transposed(logit_full, router_weight)
    slot_grad = contract_rows(
        slot_hot, (gate_value[:, None] * out_grad).astype(jnp.bfloat16)
    ).astype(jnp.bfloat16)
    sent_grad = lax.all_to_all(
        slot_grad.reshape(owner_count, local_experts * capacity, model_width),
        "expert",
        split_axis=0,
        concat_axis=0,
        tiled=True,
    )
    sent_grad = sent_grad.reshape(owner_count, local_experts, capacity, model_width)
    act_grad = jnp.einsum("secd,efd->secf", sent_grad, full_out, preferred_element_type=jnp.float32)
    pre_grad = jax.vjp(exact_gelu, pre_act)[1](act_grad)[0].astype(jnp.bfloat16)
    out_part = jnp.einsum(
        "secf,secd->efd", activated, sent_grad, preferred_element_type=jnp.float32
    )
    in_part = jnp.einsum("secf,secd->efd", pre_grad, arrived, preferred_element_type=jnp.float32)
    slotted_grad = jnp.einsum(
        "secf,efd->secd", pre_grad, full_in, preferred_element_type=jnp.float32
    ).astype(jnp.bfloat16)
    expert_in_grad, expert_out_grad = (
        lax.psum_scatter(
            in_part.astype(jnp.bfloat16), "dp", scatter_dimension=1, tiled=True
        ).astype(jnp.float32),
        lax.psum_scatter(
            out_part.astype(jnp.bfloat16), "dp", scatter_dimension=1, tiled=True
        ).astype(jnp.float32),
    )
    back_grad = lax.all_to_all(
        slotted_grad.reshape(owner_count, local_experts * capacity, model_width),
        "expert",
        split_axis=0,
        concat_axis=0,
        tiled=True,
    )
    normed2_grad = normed2_grad + jnp.dot(
        slot_hot,
        back_grad.reshape(expert_total * capacity, model_width),
        preferred_element_type=jnp.float32,
    )
    middle_part, ln2_gain_part, ln2_bias_part = norm2_pull(normed2_grad)
    middle_grad = out_grad + middle_part
    attn_grad = middle_grad.astype(jnp.bfloat16)
    outer_grad = contract_rows(attended, attn_grad)
    attended_grad = times_transposed(attn_grad, outer_weight).astype(jnp.bfloat16)
    parts = attn_bwd(prefix_len, projected, attended, attended_grad, head_lse)
    inner_grad = jnp.concatenate([contract_rows(normed_low, part) for part in parts], axis=1)
    normed_grad = sum(
        times_transposed(part, inner_weight[:, c * model_width : (c + 1) * model_width])
        for c, part in enumerate(parts)
    )
    input_part, ln1_gain_part, ln1_bias_part = norm_pull(normed_grad)
    tokens_grad = middle_grad + input_part
    mixer_grad = lax.psum_scatter(
        jnp.concatenate([inner_grad, outer_grad], axis=1),
        ("dp", "expert"),
        scatter_dimension=1,
        tiled=True,
    )
    summed = lax.psum(
        (ln1_gain_part, ln1_bias_part, ln2_gain_part, ln2_bias_part, router_part, balance_part),
        ("dp", "expert"),
    )
    return (
        mixed_out,
        tokens_grad,
        summed[0],
        summed[1],
        mixer_grad,
        summed[2],
        summed[3],
        summed[4],
        expert_in_grad,
        expert_out_grad,
        summed[5],
    )


def solution(mesh):
    in_specs = (
        P(("dp", "expert"), None),
        P(("dp", "expert"), None),
        P(("dp", "expert")),
        P(("dp", "expert")),
        P(),
        P(),
        P(None, ("dp", "expert")),
        P(),
        P(),
        P(),
        P("expert", "dp", None),
        P("expert", "dp", None),
        P(("dp", "expert"), None),
    )
    out_specs = (
        P(("dp", "expert"), None),
        P(("dp", "expert"), None),
        P(),
        P(),
        P(None, ("dp", "expert")),
        P(),
        P(),
        P(),
        P("expert", "dp", None),
        P("expert", "dp", None),
        P(),
    )
    return jax.shard_map(
        on_device, mesh=mesh, in_specs=in_specs, out_specs=out_specs, check_vma=False
    )
```

```python
import functools

import jax
import jax.numpy as jnp
from jax import lax
from jax.experimental import pallas as pl
from jax.experimental.pallas import tpu as pltpu
from jax.sharding import PartitionSpec as P


epsilon = 1e-05


def layer_norm(values, gain_vec, offset):
    center = values - jnp.mean(values, axis=-1, keepdims=True)
    spread = jnp.mean(center * center, axis=-1, keepdims=True)
    return center * lax.rsqrt(spread + epsilon) * gain_vec + offset


def contract_rows(first_op, second_op):
    return lax.dot_general(
        first_op, second_op, (((0,), (0,)), ((), ())), preferred_element_type=jnp.float32
    )


def times_transposed(first_op, second_op):
    return lax.dot_general(
        first_op, second_op, (((1,), (1,)), ((), ())), preferred_element_type=jnp.float32
    )


BF=jnp.bfloat16; F32=jnp.float32
NEG=-1e9
QB=256
def key_extent(i, n):
    return max((i+1)*QB, 512)

def nt(a,b): return lax.dot_general(a,b,(((1,),(1,)),((),())),preferred_element_type=F32)
def nn(a,b): return lax.dot_general(a,b,(((1,),(0,)),((),())),preferred_element_type=F32)

def fill_bias(bias_ref, prefix):
    kp=lax.broadcasted_iota(jnp.int32,(QB,QB),0); qp=lax.broadcasted_iota(jnp.int32,(QB,QB),1)
    causal=kp<=qp
    bias_ref[0]=jnp.where(causal|(kp<prefix),0.0,NEG)
    bias_ref[1]=jnp.where(kp+QB<prefix,0.0,NEG)+jnp.zeros((QB,QB),F32)
    bias_ref[2]=jnp.where(causal|(kp+QB<prefix),0.0,NEG)
    bias_ref[3]=jnp.where(causal,0.0,NEG)

def block_bias(j,i):
    if j==0 and i==0: return 0
    if j==1 and i==0: return 1
    if j==1 and i==1: return 2
    if j==i: return 3
    return None

def fwd_kernel(pre_ref,q_ref,k_ref,v_ref,o_ref,lse_ref,bias_ref):
    @pl.when(pl.program_id(0)==0)
    def _(): fill_bias(bias_ref,pre_ref[0])
    T=q_ref.shape[0]
    lane=lax.broadcasted_iota(jnp.int32,(1,128),1)
    vT=v_ref[...].T
    ones=jnp.ones((16,T),BF)
    for i in range(T//QB):
        K=key_extent(i,T)
        q=q_ref[i*QB:(i+1)*QB,:]*jnp.asarray(0.125,BF)
        outs=[]
        for h in range(2):
            qh=jnp.where((lane<64) if h==0 else (lane>=64), q, jnp.zeros_like(q))
            parts=[]
            for j in range(K//QB):
                s=nt(k_ref[j*QB:(j+1)*QB,:],qh)
                b=block_bias(j,i)
                if b is not None: s=s+bias_ref[b]
                parts.append(s)
            m=functools.reduce(jnp.maximum,[jnp.max(s,axis=0,keepdims=True) for s in parts])
            vh=jnp.concatenate([vT[h*64:(h+1)*64],ones],axis=0)
            acc=None
            for j,s in enumerate(parts):
                p=jnp.exp(s-m).astype(BF)
                c=nn(vh[:,j*QB:(j+1)*QB],p)
                acc=c if acc is None else acc+c
            l=acc[64:65]
            outs.append(acc[:64]*(1.0/l))
            lse_ref[0,h:h+1,i*QB:(i+1)*QB]=m+jnp.log(l)
        o_ref[i*QB:(i+1)*QB,:]=jnp.concatenate(outs,axis=0).T.astype(BF)

def attn_fwd(prefix,proj):
    T=proj.shape[0]; W=proj.shape[1]//3; n=W//128
    return pl.pallas_call(fwd_kernel,grid=(n,),
        in_specs=[pl.BlockSpec(memory_space=pltpu.SMEM)]+[pl.BlockSpec((T,128),functools.partial(lambda c,j:(0,c*n+j),c)) for c in range(3)],
        out_specs=[pl.BlockSpec((T,128),lambda j:(0,j)),pl.BlockSpec((1,2,T),lambda j:(j,0,0))],
        out_shape=[jax.ShapeDtypeStruct((T,W),BF),jax.ShapeDtypeStruct((n,2,T),F32)],
        scratch_shapes=[pltpu.VMEM((4,QB,QB),F32)],
        compiler_params=pltpu.CompilerParams(vmem_limit_bytes=60<<20),
        name="attn_fwd")(prefix,proj,proj,proj)

def bwd_kernel(pre_ref,q_ref,k_ref,v_ref,o_ref,g_ref,lse_ref,dq_ref,dk_ref,dv_ref,bias_ref,dk_acc,dv_acc):
    @pl.when(pl.program_id(0)==0)
    def _(): fill_bias(bias_ref,pre_ref[0])
    T=q_ref.shape[0]; nb=T//QB
    lane=lax.broadcasted_iota(jnp.int32,(1,128),1)
    kT=k_ref[...].T
    started=[False]*nb
    for i in range(nb-1,-1,-1):
        K=key_extent(i,T)
        rows=slice(i*QB,(i+1)*QB)
        q=q_ref[rows,:]*jnp.asarray(0.125,BF)
        g=g_ref[rows,:]
        dT=(g.astype(F32)*o_ref[rows,:].astype(F32)).T
        outs=[]
        for h in range(2):
            sel=(lane<64) if h==0 else (lane>=64)
            qh=jnp.where(sel,q,jnp.zeros_like(q)); gh=jnp.where(sel,g,jnp.zeros_like(g))
            lse=lse_ref[0,h:h+1,rows]
            delta=jnp.sum(dT[h*64:(h+1)*64],axis=0,keepdims=True)
            dq=None
            for j in range(K//QB):
                kr=slice(j*QB,(j+1)*QB)
                s=nt(k_ref[kr,:],qh)
                b=block_bias(j,i)
                if b is not None: s=s+bias_ref[b]
                p=jnp.exp(s-lse)
                dp=nt(v_ref[kr,:],gh)
                ds=(p*(dp-delta)).astype(BF)
                dv=nn(p.astype(BF),gh)
                dk=nn(ds,qh)
                first=(i==nb-1 and h==0)
                if first: dv_acc[kr,:]=dv; dk_acc[kr,:]=dk
                else:
                    dv_acc[kr,:]+=dv; dk_acc[kr,:]+=dk
                c=nn(kT[h*64:(h+1)*64,kr],ds)
                dq=c if dq is None else dq+c
            outs.append(dq)
        dq_ref[rows,:]=(jnp.concatenate(outs,axis=0).T*0.125).astype(BF)
    dk_ref[...]=dk_acc[...].astype(BF)
    dv_ref[...]=dv_acc[...].astype(BF)

def attn_bwd(prefix,proj,att,grad,lse):
    T=proj.shape[0]; W=proj.shape[1]//3; n=W//128
    cb=lambda: pl.BlockSpec((T,128),lambda j:(0,j))
    return pl.pallas_call(bwd_kernel,grid=(n,),
        in_specs=[pl.BlockSpec(memory_space=pltpu.SMEM)]+[pl.BlockSpec((T,128),functools.partial(lambda c,j:(0,c*n+j),c)) for c in range(3)]
          +[cb(),cb(),pl.BlockSpec((1,2,T),lambda j:(j,0,0))],
        out_specs=[cb()]*3,
        out_shape=[jax.ShapeDtypeStruct((T,W),BF)]*3,
        scratch_shapes=[pltpu.VMEM((4,QB,QB),F32),pltpu.VMEM((T,128),F32),pltpu.VMEM((T,128),F32)],
        compiler_params=pltpu.CompilerParams(vmem_limit_bytes=60<<20),
        name="attn_bwd")(prefix,proj,proj,proj,att,grad,lse)

def tn(a,b): return lax.dot_general(a,b,(((0,),(0,)),((),())),preferred_element_type=F32)

ERF_TOP=3.832506856900711
ERF_NUM=(0.00022905065861350646,0.0034082910107109506,0.050955695062380861,0.18520832239976145,1.128379143519084)
ERF_DEN=(-1.1791602954361697e-7,0.000023547966471313185,0.0010179625278914885,0.014070470171167667,0.11098505178285362,0.49746925110067538,1.0)

def erf32(x):
    x=jnp.clip(x,-ERF_TOP,ERF_TOP); y=x*x
    n=ERF_NUM[0]
    for c in ERF_NUM[1:]: n=n*y+c
    d=ERF_DEN[0]
    for c in ERF_DEN[1:]: d=d*y+c
    return x*n/d

def expert_kernel(nr,nw,tiles,*refs):
    rw_ref=refs[0]; refs=refs[1:]
    x_refs,refs=refs[:nr],refs[nr:]
    c_refs,refs=refs[:nr],refs[nr:]
    wi_refs,refs=refs[:nw],refs[nw:]
    wo_refs,refs=refs[:nw],refs[nw:]
    p_refs,refs=refs[:nr],refs[nr:]
    d_refs,refs=refs[:nr],refs[nr:]
    gi_refs,refs=refs[:nw],refs[nw:]
    go_refs,refs=refs[:nw],refs[nw:]
    rg_ref,x_s,g_s,gate_s,p_acc,d_acc=refs
    step=pl.program_id(0)
    S,C,D=x_refs[0].shape; R=S*C
    @pl.when(step==0)
    def _():
        for r in range(nr):
            rows=slice(r*R,(r+1)*R)
            x=x_refs[r][...].reshape(R,D)
            gate=jax.nn.sigmoid(jnp.sum(x.astype(F32)*rw_ref[...],axis=1,keepdims=True))
            x_s[rows,:]=x
            g_s[rows,:]=(gate*c_refs[r][...].reshape(R,D).astype(F32)).astype(BF)
            gate_s[rows,:]=gate
        p_acc[...]=jnp.zeros_like(p_acc); d_acc[...]=jnp.zeros_like(d_acc)
    for w in range(nw):
        @pl.when(step//tiles==w)
        def _(w=w):
            wi=wi_refs[w][0]; wo=wo_refs[w][0]
            pre=nt(x_s[...],wi)
            da=nt(g_s[...],wo)
            phi=0.5+0.5*erf32(pre*0.7071067811865476)
            act=(pre*phi).astype(BF)
            dens=0.3989422804014327*jnp.exp(-0.5*pre*pre)
            dp=(da*(phi+pre*dens)).astype(BF)
            p_acc[...]+=nn(act,wo)
            d_acc[...]+=nn(dp,wi)
            gi_refs[w][...]=tn(dp,x_s[...]).astype(gi_refs[w].dtype)
            go_refs[w][...]=tn(act,g_s[...]).astype(go_refs[w].dtype)
    @pl.when(step==nw*tiles-1)
    def _():
        rg=jnp.zeros((1,D),F32)
        for r in range(nr):
            rows=slice(r*R,(r+1)*R)
            p=p_acc[rows,:]; gate=gate_s[rows,:]
            dot=jnp.sum(p*c_refs[r][...].reshape(R,D).astype(F32),axis=1,keepdims=True)
            lg=dot*(gate*(1.0-gate))
            p_refs[r][...]=p.reshape(S,C,D).astype(p_refs[r].dtype)
            d_refs[r][...]=(d_acc[rows,:]+lg*rw_ref[...]).reshape(S,C,D).astype(d_refs[r].dtype)
            rg=rg+jnp.sum(lg*x_s[rows,:].astype(F32),axis=0,keepdims=True)
        rg_ref[...]=rg

def run_expert(e,rw,xs,cs,wis,wos):
    nr,nw=len(xs),len(wis)
    S,C,D=xs[0].shape; Q=wis[0].shape[1]; R=nr*S*C
    tile=Q
    for t in (384,256,192,128):
        if Q%t==0: tile=t; break
    tiles=Q//tile
    whole=lambda shape: pl.BlockSpec(shape,lambda i:(0,)*len(shape))
    at=lambda w: (lambda i: jnp.clip(i-w*tiles,0,tiles-1))
    wspec=lambda w: pl.BlockSpec((1,tile,D),lambda i,f=at(w):(e,f(i),0))
    gspec=lambda w: pl.BlockSpec((tile,D),lambda i,f=at(w):(f(i),0))
    rows_spec=whole((S,C,D))
    kind=lambda k: F32 if k==0 else BF
    outs=pl.pallas_call(functools.partial(expert_kernel,nr,nw,tiles),grid=(nw*tiles,),
        in_specs=[whole((1,D))]+[rows_spec]*(2*nr)+[wspec(w) for w in range(nw)]*2,
        out_specs=[rows_spec]*(2*nr)+[gspec(w) for w in range(nw)]*2+[whole((1,D))],
        out_shape=[jax.ShapeDtypeStruct((S,C,D),kind(r)) for r in range(nr)]*2
          +[jax.ShapeDtypeStruct((Q,D),kind(w)) for w in range(nw)]*2+[jax.ShapeDtypeStruct((1,D),F32)],
        scratch_shapes=[pltpu.VMEM((R,D),BF),pltpu.VMEM((R,D),BF),pltpu.VMEM((R,1),F32),pltpu.VMEM((R,D),F32),pltpu.VMEM((R,D),F32)],
        compiler_params=pltpu.CompilerParams(vmem_limit_bytes=60<<20),
        cost_estimate=pl.CostEstimate(flops=12*R*nw*Q*D,bytes_accessed=nw*Q*D*10+R*D*10,transcendentals=R*nw*Q),
        name="expert")(rw,*xs,*cs,*wis,*wos)
    return outs[:nr],outs[nr:2*nr],outs[2*nr:2*nr+nw],outs[2*nr+nw:2*nr+2*nw],outs[-1]

def low_shift(n,nx,k): return [(i,i//nx*nx+(i%nx+k)%nx) for i in range(n)]
def high_shift(n,nx,k): return [(i,(i+k*nx)%n) for i in range(n)]


def on_device(
    tokens,
    routes,
    slot_order,
    prefix_len,
    ln1_gain,
    ln1_bias,
    mixer_weight,
    ln2_gain,
    ln2_bias,
    router_weight,
    expert_in,
    expert_out,
    cotangent,
):
    model_width = tokens.shape[1]
    token_count = tokens.shape[0]
    expert_total = router_weight.shape[1]
    local_experts = expert_in.shape[0]
    capacity = token_count // expert_total
    owner_count = lax.axis_size("expert")
    dp_count = lax.axis_size("dp")
    low = max(d for d in range(1, dp_count + 1) if dp_count % d == 0 and d * d <= dp_count)
    high = dp_count // low
    to_low = lambda a, k: lax.ppermute(a, "dp", low_shift(dp_count, low, k))
    to_high = lambda a, k: lax.ppermute(a, "dp", high_shift(dp_count, low, k))
    swap_owner = lambda a: lax.all_to_all(a, "expert", split_axis=0, concat_axis=0, tiled=True)
    ins = [expert_in] + [to_low(expert_in, k) for k in range(1, low)]
    outs = [expert_out] + [to_low(expert_out, k) for k in range(1, low)]
    route_flat = routes[:, 0]
    route_hot = route_flat[:, None] == jnp.arange(expert_total)[None, :]
    route_float = route_hot.astype(jnp.float32)
    counts = lax.psum(jnp.sum(route_float, axis=0), ("dp", "expert"))
    earlier = (slot_order[None, :] < slot_order[:, None]).astype(jnp.bfloat16)
    ahead_count = jnp.dot(
        earlier, route_hot.astype(jnp.bfloat16), preferred_element_type=jnp.float32
    )
    slot_rank = jnp.sum(ahead_count * route_float, axis=1).astype(jnp.int32)
    part_rows = owner_count * capacity
    slot_index = (
        route_flat % local_experts * part_rows + route_flat // local_experts * capacity + slot_rank
    )
    is_kept = slot_rank < capacity
    slot_hot = (
        (slot_index[:, None] == jnp.arange(expert_total * capacity)[None, :]) & is_kept[:, None]
    ).astype(jnp.bfloat16)
    cot_sets = []
    for e in range(local_experts):
        hot = slot_hot[:, e * part_rows : (e + 1) * part_rows]
        mine = swap_owner(
            contract_rows(hot, cotangent)
            .astype(jnp.bfloat16)
            .reshape(owner_count, capacity, model_width)
        )
        cot_sets.append([mine] + [to_high(mine, k) for k in range(1, high)])
    full_mixer = lax.all_gather(mixer_weight, ("dp", "expert"), axis=1, tiled=True)
    inner_weight = full_mixer[:, : 3 * model_width]
    outer_weight = full_mixer[:, 3 * model_width :]
    inputs = tokens.astype(jnp.float32)
    normed, norm_pull = jax.vjp(layer_norm, inputs, ln1_gain, ln1_bias)
    normed_low = normed.astype(jnp.bfloat16)
    projected = jnp.dot(normed_low, inner_weight, preferred_element_type=jnp.float32).astype(
        jnp.bfloat16
    )
    attended, head_lse = attn_fwd(prefix_len, projected)
    middle = inputs + jnp.dot(attended, outer_weight, preferred_element_type=jnp.float32)
    normed2, norm2_pull = jax.vjp(layer_norm, middle, ln2_gain, ln2_bias)
    normed2_low = normed2.astype(jnp.bfloat16)
    chosen = jnp.sum(
        jnp.dot(normed2_low, router_weight, preferred_element_type=jnp.float32) * route_float, axis=1
    )
    gate_value = jax.nn.sigmoid(chosen)
    first_expert = lax.axis_index("expert") * local_experts
    back_rows, produced_rows, in_grads, out_grads = [], [], [], []
    router_part = jnp.zeros((model_width, expert_total), jnp.float32)
    row_sets = []
    for e in range(local_experts):
        hot = slot_hot[:, e * part_rows : (e + 1) * part_rows]
        outgoing = contract_rows(hot, normed2_low).astype(jnp.bfloat16)
        mine = swap_owner(outgoing.reshape(owner_count, capacity, model_width))
        row_sets.append([mine] + [to_high(mine, k) for k in range(1, high)])
    for e in range(local_experts):
        column = (jnp.arange(expert_total) == first_expert + e).astype(jnp.float32)
        router_column = jnp.sum(router_weight.astype(jnp.float32) * column[None, :], axis=1)
        produced, slot_grad, in_part, out_part, router_row = run_expert(
            e, router_column[None, :], row_sets[e], cot_sets[e], ins, outs
        )
        total = slot_grad[0]
        for k in range(1, high):
            total = total + to_high(slot_grad[k], -k).astype(jnp.float32)
        back_rows.append(swap_owner(total.astype(jnp.bfloat16)))
        total = produced[0]
        for k in range(1, high):
            total = total + to_high(produced[k], -k).astype(jnp.float32)
        produced_rows.append(swap_owner(total.astype(jnp.bfloat16)))
        for parts, sums in ((in_part, in_grads), (out_part, out_grads)):
            total = parts[0]
            for k in range(1, low):
                total = total + to_low(parts[k], -k).astype(jnp.float32)
            sums.append(total)
        router_part = router_part + router_row[0][:, None] * column[None, :]
    expert_in_grad, expert_out_grad = jnp.stack(in_grads), jnp.stack(out_grads)
    out_grad = cotangent.astype(jnp.float32)
    mean_load = jnp.sum(counts) / expert_total
    load_weight = (
        (jnp.sum(route_float * counts[None, :], axis=1) - mean_load) / mean_load / jnp.sum(counts)
    )
    balance_part = jnp.sum(load_weight * gate_value)
    load_grad = load_weight * gate_value * (1.0 - gate_value)
    load_full = (load_grad[:, None] * route_float).astype(jnp.bfloat16)
    router_part = router_part + contract_rows(normed2_low, load_full)
    normed2_grad = times_transposed(load_full, router_weight) + jnp.dot(
        slot_hot,
        jnp.concatenate([r.reshape(part_rows, model_width) for r in back_rows]),
        preferred_element_type=jnp.float32,
    )
    returned = jnp.dot(
        slot_hot,
        jnp.concatenate([r.reshape(part_rows, model_width) for r in produced_rows]),
        preferred_element_type=jnp.float32,
    )
    mixed_out = (middle + gate_value[:, None] * returned).astype(jnp.bfloat16)
    middle_part, ln2_gain_part, ln2_bias_part = norm2_pull(normed2_grad)
    middle_grad = out_grad + middle_part
    attn_grad = middle_grad.astype(jnp.bfloat16)
    outer_grad = contract_rows(attended, attn_grad)
    attended_grad = times_transposed(attn_grad, outer_weight).astype(jnp.bfloat16)
    parts = attn_bwd(prefix_len, projected, attended, attended_grad, head_lse)
    inner_grad = jnp.concatenate([contract_rows(normed_low, part) for part in parts], axis=1)
    normed_grad = sum(
        times_transposed(part, inner_weight[:, c * model_width : (c + 1) * model_width])
        for c, part in enumerate(parts)
    )
    input_part, ln1_gain_part, ln1_bias_part = norm_pull(normed_grad)
    tokens_grad = middle_grad + input_part
    mixer_grad = lax.psum_scatter(
        jnp.concatenate([inner_grad, outer_grad], axis=1),
        ("dp", "expert"),
        scatter_dimension=1,
        tiled=True,
    )
    summed = lax.psum(
        (ln1_gain_part, ln1_bias_part, ln2_gain_part, ln2_bias_part, router_part, balance_part),
        ("dp", "expert"),
    )
    return (
        mixed_out,
        tokens_grad,
        summed[0],
        summed[1],
        mixer_grad,
        summed[2],
        summed[3],
        summed[4],
        expert_in_grad,
        expert_out_grad,
        summed[5],
    )


def solution(mesh):
    in_specs = (
        P(("dp", "expert"), None),
        P(("dp", "expert"), None),
        P(("dp", "expert")),
        P(("dp", "expert")),
        P(),
        P(),
        P(None, ("dp", "expert")),
        P(),
        P(),
        P(),
        P("expert", "dp", None),
        P("expert", "dp", None),
        P(("dp", "expert"), None),
    )
    out_specs = (
        P(("dp", "expert"), None),
        P(("dp", "expert"), None),
        P(),
        P(),
        P(None, ("dp", "expert")),
        P(),
        P(),
        P(),
        P("expert", "dp", None),
        P("expert", "dp", None),
        P(),
    )
    return jax.shard_map(
        on_device, mesh=mesh, in_specs=in_specs, out_specs=out_specs, check_vma=False
    )
```

```python
import functools

import jax
import jax.numpy as jnp
from jax import lax
from jax.experimental import pallas as pl
from jax.experimental.pallas import tpu as pltpu
from jax.sharding import PartitionSpec as P


epsilon = 1e-05


def layer_norm(values, gain_vec, offset):
    center = values - jnp.mean(values, axis=-1, keepdims=True)
    spread = jnp.mean(center * center, axis=-1, keepdims=True)
    return center * lax.rsqrt(spread + epsilon) * gain_vec + offset


def contract_rows(first_op, second_op):
    return lax.dot_general(
        first_op, second_op, (((0,), (0,)), ((), ())), preferred_element_type=jnp.float32
    )


def times_transposed(first_op, second_op):
    return lax.dot_general(
        first_op, second_op, (((1,), (1,)), ((), ())), preferred_element_type=jnp.float32
    )


BF=jnp.bfloat16; F32=jnp.float32
NEG=-1e9
QB=256
def key_extent(i, n):
    return max((i+1)*QB, 512)

def nt(a,b): return lax.dot_general(a,b,(((1,),(1,)),((),())),preferred_element_type=F32)
def nn(a,b): return lax.dot_general(a,b,(((1,),(0,)),((),())),preferred_element_type=F32)

def fill_bias(bias_ref, prefix):
    kp=lax.broadcasted_iota(jnp.int32,(QB,QB),0); qp=lax.broadcasted_iota(jnp.int32,(QB,QB),1)
    causal=kp<=qp
    bias_ref[0]=jnp.where(causal|(kp<prefix),0.0,NEG)
    bias_ref[1]=jnp.where(kp+QB<prefix,0.0,NEG)+jnp.zeros((QB,QB),F32)
    bias_ref[2]=jnp.where(causal|(kp+QB<prefix),0.0,NEG)
    bias_ref[3]=jnp.where(causal,0.0,NEG)

def block_bias(j,i):
    if j==0 and i==0: return 0
    if j==1 and i==0: return 1
    if j==1 and i==1: return 2
    if j==i: return 3
    return None

def fwd_kernel(pre_ref,q_ref,k_ref,v_ref,o_ref,lse_ref,bias_ref):
    @pl.when(pl.program_id(0)==0)
    def _(): fill_bias(bias_ref,pre_ref[0])
    T=q_ref.shape[0]
    lane=lax.broadcasted_iota(jnp.int32,(1,128),1)
    vT=v_ref[...].T
    ones=jnp.ones((16,T),BF)
    for i in range(T//QB):
        K=key_extent(i,T)
        q=q_ref[i*QB:(i+1)*QB,:]*jnp.asarray(0.125,BF)
        outs=[]
        for h in range(2):
            qh=jnp.where((lane<64) if h==0 else (lane>=64), q, jnp.zeros_like(q))
            parts=[]
            for j in range(K//QB):
                s=nt(k_ref[j*QB:(j+1)*QB,:],qh)
                b=block_bias(j,i)
                if b is not None: s=s+bias_ref[b]
                parts.append(s)
            m=functools.reduce(jnp.maximum,[jnp.max(s,axis=0,keepdims=True) for s in parts])
            vh=jnp.concatenate([vT[h*64:(h+1)*64],ones],axis=0)
            acc=None
            for j,s in enumerate(parts):
                p=jnp.exp(s-m).astype(BF)
                c=nn(vh[:,j*QB:(j+1)*QB],p)
                acc=c if acc is None else acc+c
            l=acc[64:65]
            outs.append(acc[:64]*(1.0/l))
            lse_ref[0,h:h+1,i*QB:(i+1)*QB]=m+jnp.log(l)
        o_ref[i*QB:(i+1)*QB,:]=jnp.concatenate(outs,axis=0).T.astype(BF)

def attn_fwd(prefix,proj):
    T=proj.shape[0]; W=proj.shape[1]//3; n=W//128
    return pl.pallas_call(fwd_kernel,grid=(n,),
        in_specs=[pl.BlockSpec(memory_space=pltpu.SMEM)]+[pl.BlockSpec((T,128),functools.partial(lambda c,j:(0,c*n+j),c)) for c in range(3)],
        out_specs=[pl.BlockSpec((T,128),lambda j:(0,j)),pl.BlockSpec((1,2,T),lambda j:(j,0,0))],
        out_shape=[jax.ShapeDtypeStruct((T,W),BF),jax.ShapeDtypeStruct((n,2,T),F32)],
        scratch_shapes=[pltpu.VMEM((4,QB,QB),F32)],
        compiler_params=pltpu.CompilerParams(vmem_limit_bytes=60<<20),
        name="attn_fwd")(prefix,proj,proj,proj)

def bwd_kernel(pre_ref,q_ref,k_ref,v_ref,o_ref,g_ref,lse_ref,dq_ref,dk_ref,dv_ref,bias_ref,dk_acc,dv_acc):
    @pl.when(pl.program_id(0)==0)
    def _(): fill_bias(bias_ref,pre_ref[0])
    T=q_ref.shape[0]; nb=T//QB
    lane=lax.broadcasted_iota(jnp.int32,(1,128),1)
    kT=k_ref[...].T
    started=[False]*nb
    for i in range(nb-1,-1,-1):
        K=key_extent(i,T)
        rows=slice(i*QB,(i+1)*QB)
        q=q_ref[rows,:]*jnp.asarray(0.125,BF)
        g=g_ref[rows,:]
        dT=(g.astype(F32)*o_ref[rows,:].astype(F32)).T
        outs=[]
        for h in range(2):
            sel=(lane<64) if h==0 else (lane>=64)
            qh=jnp.where(sel,q,jnp.zeros_like(q)); gh=jnp.where(sel,g,jnp.zeros_like(g))
            lse=lse_ref[0,h:h+1,rows]
            delta=jnp.sum(dT[h*64:(h+1)*64],axis=0,keepdims=True)
            dq=None
            for j in range(K//QB):
                kr=slice(j*QB,(j+1)*QB)
                s=nt(k_ref[kr,:],qh)
                b=block_bias(j,i)
                if b is not None: s=s+bias_ref[b]
                p=jnp.exp(s-lse)
                dp=nt(v_ref[kr,:],gh)
                ds=(p*(dp-delta)).astype(BF)
                dv=nn(p.astype(BF),gh)
                dk=nn(ds,qh)
                first=(i==nb-1 and h==0)
                if first: dv_acc[kr,:]=dv; dk_acc[kr,:]=dk
                else:
                    dv_acc[kr,:]+=dv; dk_acc[kr,:]+=dk
                c=nn(kT[h*64:(h+1)*64,kr],ds)
                dq=c if dq is None else dq+c
            outs.append(dq)
        dq_ref[rows,:]=(jnp.concatenate(outs,axis=0).T*0.125).astype(BF)
    dk_ref[...]=dk_acc[...].astype(BF)
    dv_ref[...]=dv_acc[...].astype(BF)

def attn_bwd(prefix,proj,att,grad,lse):
    T=proj.shape[0]; W=proj.shape[1]//3; n=W//128
    cb=lambda: pl.BlockSpec((T,128),lambda j:(0,j))
    return pl.pallas_call(bwd_kernel,grid=(n,),
        in_specs=[pl.BlockSpec(memory_space=pltpu.SMEM)]+[pl.BlockSpec((T,128),functools.partial(lambda c,j:(0,c*n+j),c)) for c in range(3)]
          +[cb(),cb(),pl.BlockSpec((1,2,T),lambda j:(j,0,0))],
        out_specs=[cb()]*3,
        out_shape=[jax.ShapeDtypeStruct((T,W),BF)]*3,
        scratch_shapes=[pltpu.VMEM((4,QB,QB),F32),pltpu.VMEM((T,128),F32),pltpu.VMEM((T,128),F32)],
        compiler_params=pltpu.CompilerParams(vmem_limit_bytes=60<<20),
        name="attn_bwd")(prefix,proj,proj,proj,att,grad,lse)

def tn(a,b): return lax.dot_general(a,b,(((0,),(0,)),((),())),preferred_element_type=F32)

ERF_TOP=3.832506856900711
ERF_NUM=(0.00022905065861350646,0.0034082910107109506,0.050955695062380861,0.18520832239976145,1.128379143519084)
ERF_DEN=(-1.1791602954361697e-7,0.000023547966471313185,0.0010179625278914885,0.014070470171167667,0.11098505178285362,0.49746925110067538,1.0)

def erf32(x):
    x=jnp.clip(x,-ERF_TOP,ERF_TOP); y=x*x
    n=ERF_NUM[0]
    for c in ERF_NUM[1:]: n=n*y+c
    d=ERF_DEN[0]
    for c in ERF_DEN[1:]: d=d*y+c
    return x*n/d

def expert_kernel(nr,nw,tiles,*refs):
    rw_ref=refs[0]; refs=refs[1:]
    x_refs,refs=refs[:nr],refs[nr:]
    c_refs,refs=refs[:nr],refs[nr:]
    wi_refs,refs=refs[:nw],refs[nw:]
    wo_refs,refs=refs[:nw],refs[nw:]
    p_refs,refs=refs[:nr],refs[nr:]
    d_refs,refs=refs[:nr],refs[nr:]
    gi_refs,refs=refs[:nw],refs[nw:]
    go_refs,refs=refs[:nw],refs[nw:]
    rg_ref,x_s,g_s,gate_s,p_acc,d_acc=refs
    step=pl.program_id(0)
    S,C,D=x_refs[0].shape; R=S*C
    @pl.when(step==0)
    def _():
        for r in range(nr):
            rows=slice(r*R,(r+1)*R)
            x=x_refs[r][...].reshape(R,D)
            gate=jax.nn.sigmoid(jnp.sum(x.astype(F32)*rw_ref[...],axis=1,keepdims=True))
            x_s[rows,:]=x
            g_s[rows,:]=(gate*c_refs[r][...].reshape(R,D).astype(F32)).astype(BF)
            gate_s[rows,:]=gate
        p_acc[...]=jnp.zeros_like(p_acc); d_acc[...]=jnp.zeros_like(d_acc)
    for w in range(nw):
        @pl.when(step//tiles==w)
        def _(w=w):
            wi=wi_refs[w][...]; wo=wo_refs[w][...]
            pre=nt(x_s[...],wi)
            da=nt(g_s[...],wo)
            phi=0.5+0.5*erf32(pre*0.7071067811865476)
            act=(pre*phi).astype(BF)
            dens=0.3989422804014327*jnp.exp(-0.5*pre*pre)
            dp=(da*(phi+pre*dens)).astype(BF)
            p_acc[...]+=nn(act,wo)
            d_acc[...]+=nn(dp,wi)
            gi_refs[w][...]=tn(dp,x_s[...]).astype(gi_refs[w].dtype)
            go_refs[w][...]=tn(act,g_s[...]).astype(go_refs[w].dtype)
    @pl.when(step==nw*tiles-1)
    def _():
        rg=jnp.zeros((1,D),F32)
        for r in range(nr):
            rows=slice(r*R,(r+1)*R)
            p=p_acc[rows,:]; gate=gate_s[rows,:]
            dot=jnp.sum(p*c_refs[r][...].reshape(R,D).astype(F32),axis=1,keepdims=True)
            lg=dot*(gate*(1.0-gate))
            p_refs[r][...]=p.reshape(S,C,D).astype(p_refs[r].dtype)
            d_refs[r][...]=(d_acc[rows,:]+lg*rw_ref[...]).reshape(S,C,D).astype(d_refs[r].dtype)
            rg=rg+jnp.sum(lg*x_s[rows,:].astype(F32),axis=0,keepdims=True)
        rg_ref[...]=rg

def run_expert(e,rw,xs,cs,wis,wos):
    nr,nw=len(xs),len(wis)
    S,C,D=xs[0].shape; Q=wis[0].shape[0]; R=nr*S*C
    tile=Q
    for t in (384,256,192,128):
        if Q%t==0: tile=t; break
    tiles=Q//tile
    whole=lambda shape: pl.BlockSpec(shape,lambda i:(0,)*len(shape))
    at=lambda w: (lambda i: jnp.clip(i-w*tiles,0,tiles-1))
    wspec=lambda w: pl.BlockSpec((tile,D),lambda i,f=at(w):(f(i),0))
    gspec=lambda w: pl.BlockSpec((tile,D),lambda i,f=at(w):(f(i),0))
    rows_spec=whole((S,C,D))
    kind=lambda k: F32 if k==0 else BF
    outs=pl.pallas_call(functools.partial(expert_kernel,nr,nw,tiles),grid=(nw*tiles,),
        in_specs=[whole((1,D))]+[rows_spec]*nr+[pl.BlockSpec((S,1,C,D),lambda i:(0,e,0,0))]*nr+[wspec(w) for w in range(nw)]*2,
        out_specs=[rows_spec]*(2*nr)+[gspec(w) for w in range(nw)]*2+[whole((1,D))],
        out_shape=[jax.ShapeDtypeStruct((S,C,D),kind(r)) for r in range(nr)]*2
          +[jax.ShapeDtypeStruct((Q,D),kind(w)) for w in range(nw)]*2+[jax.ShapeDtypeStruct((1,D),F32)],
        scratch_shapes=[pltpu.VMEM((R,D),BF),pltpu.VMEM((R,D),BF),pltpu.VMEM((R,1),F32),pltpu.VMEM((R,D),F32),pltpu.VMEM((R,D),F32)],
        compiler_params=pltpu.CompilerParams(vmem_limit_bytes=60<<20),
        cost_estimate=pl.CostEstimate(flops=12*R*nw*Q*D,bytes_accessed=nw*Q*D*10+R*D*10,transcendentals=R*nw*Q),
        name="expert")(rw,*xs,*cs,*wis,*wos)
    return outs[:nr],outs[nr:2*nr],outs[2*nr:2*nr+nw],outs[2*nr+nw:2*nr+2*nw],outs[-1]

MESH=pl.DeviceIdType.MESH

class Grid:
    def __init__(self):
        self.dp=lax.axis_size("dp"); self.expert=lax.axis_size("expert")
        bits=lambda n: n.bit_length()-1
        dp_bits=[("dp",1<<i) for i in range(bits(self.dp))]
        ex_bits=[("expert",1<<i) for i in range(bits(self.expert))]
        h=len(dp_bits)//2
        xs,ys,zs=dp_bits[:h],dp_bits[h:],ex_bits[1:]
        self.core=ex_bits[0]
        self.orders=[xs+ys+zs,ys+xs+zs,zs+xs+ys]
        self.all_bits=[self.core]+zs+xs+ys
    def here(self): self.at={"dp":lax.axis_index("dp"),"expert":lax.axis_index("expert")}
    def flip(self,k): return (1-2*(self.at[k[0]]//k[1]%2))*k[1]
    def partner(self,k): return {k[0]:self.at[k[0]]+self.flip(k)}
    def block(self,place):
        dp,ex=self.at["dp"],self.at["expert"]
        for k in place:
            if k[0]=="dp": dp=dp+self.flip(k)
            else: ex=ex+self.flip(k)
        return dp*self.expert+ex
    def greet(self):
        barrier=pltpu.get_barrier_semaphore()
        for k in self.all_bits: pl.semaphore_signal(barrier,inc=1,device_id=self.partner(k),device_id_type=MESH)
        pl.semaphore_wait(barrier,len(self.all_bits))

def place_of(order,code):
    m=len(order)
    return frozenset(order[i] for i in range(m) if code>>(m-1-i)&1)

class SmallSum:
    def __init__(self,g,small_ref,sum_ref,buf,arrive,ssem,rsem):
        self.g,self.sum_ref,self.buf,self.arrive,self.ssem,self.rsem=g,sum_ref,buf,arrive,ssem,rsem
        self.i=0
        buf[0]=small_ref[...]
    def start(self):
        i=self.i
        self.copy=pltpu.make_async_remote_copy(self.buf.at[i],self.arrive.at[i],self.ssem.at[i],self.rsem.at[i],device_id=self.g.partner(self.g.all_bits[i]),device_id_type=MESH)
        self.copy.start()
    def step(self):
        i=self.i
        if i>=len(self.g.all_bits): return
        self.copy.wait()
        v=self.buf[i]+self.arrive[i]
        self.i=i+1
        if self.i<len(self.g.all_bits): self.buf[i+1]=v; self.start()
        else: self.sum_ref[...]=v

def gather_kernel(w_ref,small_ref,out_ref,sum_ref,s_buf,s_in,ssem,rsem,cs,cr,sssem,srsem):
    g=Grid(); g.here(); g.greet()
    small=SmallSum(g,small_ref,sum_ref,s_buf,s_in,sssem,srsem)
    D=w_ref.shape[1]; n=len(g.orders); L=D//n
    chip=g.orders[0]; number={place_of(chip,c):c for c in range(1<<len(chip))}
    out_ref[g.block(())]=w_ref[...]
    sends=[]; core_in=[]
    def view(o,place): return out_ref.at[g.block(place),:,o*L:(o+1)*L]
    def source(o,place): return view(o,place) if place else w_ref.at[:,o*L:(o+1)*L]
    def send(o,place,k):
        to=number[place^{k}]
        c=pltpu.make_async_remote_copy(source(o,place),view(o,place),ssem.at[o,to],rsem.at[o,to],device_id=g.partner(k),device_id_type=MESH)
        c.start(); sends.append(c)
    def arrived(o,place,k):
        i=number[place]
        pltpu.make_async_remote_copy(view(o,place),view(o,place),ssem.at[o,i],rsem.at[o,i],device_id=g.partner(k),device_id_type=MESH).wait_recv()
    def across(o,place):
        i=number[place]
        c=pltpu.make_async_remote_copy(source(o,place),view(o,place),cs.at[o,i],cr.at[o,i],device_id=g.partner(g.core),device_id_type=MESH)
        c.start(); sends.append(c)
        v=view(o,place|{g.core})
        core_in.append(pltpu.make_async_remote_copy(v,v,cs.at[o,i],cr.at[o,i],device_id=g.partner(g.core),device_id_type=MESH))
    m=len(chip)
    held=[[frozenset()] for _ in g.orders]
    fresh=[[] for _ in g.orders]
    for j in range(m):
        for o,order in enumerate(g.orders):
            k=order[m-1-j]
            for p in held[o]: send(o,p,k)
            if j==0: across(o,frozenset())
        if j==0: small.start()
        else: small.step()
        for o,order in enumerate(g.orders):
            k=order[m-1-j]
            for p in fresh[o]:
                arrived(o,p,order[m-j]); send(o,p,k); across(o,p)
            held[o]=held[o]+fresh[o]
            fresh[o]=[p|{k} for p in held[o]]
    for i in range(len(fresh[0])):
        for o,order in enumerate(g.orders):
            arrived(o,fresh[o][i],order[0]); across(o,fresh[o][i])
    for _ in g.all_bits: small.step()
    for c in core_in: c.wait_recv()
    for c in sends: c.wait_send()

def gather_mixer(w,small):
    g=Grid(); n=g.dp*g.expert; half=n//2; k=len(g.orders); nb=len(g.all_bits)
    V=pl.BlockSpec(memory_space=pltpu.VMEM); S=pltpu.SemaphoreType.DMA
    D=w.shape[1]
    return pl.pallas_call(gather_kernel,
        in_specs=[V,V],out_specs=[V,V],
        out_shape=[jax.ShapeDtypeStruct((n,)+w.shape,w.dtype),jax.ShapeDtypeStruct(small.shape,F32)],
        scratch_shapes=[pltpu.VMEM((nb,)+small.shape,F32)]*2+[S((k,half))]*4+[S((nb,))]*2,
        compiler_params=pltpu.CompilerParams(collective_id=0,has_side_effects=True,vmem_limit_bytes=60<<20),
        cost_estimate=pl.CostEstimate(flops=0,bytes_accessed=n*w.size*2,transcendentals=0),
        name="gather_mixer")(w,small)

def scatter_kernel(g_ref,small_ref,out_ref,sum_ref,c_in,acc,out_buf,in_buf,s_buf,s_in,csem,crem,ssem,rsem,sssem,srsem):
    g=Grid(); g.here(); g.greet()
    D=g_ref.shape[2]; n=len(g.orders); L=D//n
    chip=g.orders[0]; m=len(chip); full=1<<m
    number={place_of(chip,c):c for c in range(full)}
    sends=[]; here=set(); pending=[]
    def flush():
        for c in pending: c.start(); sends.append(c)
        pending.clear()
    small=SmallSum(g,small_ref,sum_ref,s_buf,s_in,sssem,srsem)
    cross=[]
    for s in range(full-1,-1,-1):
        for order in g.orders:
            p=place_of(order,s)
            if p in cross: continue
            cross.append(p)
    for p in cross:
        i=number[p]
        c=pltpu.make_async_remote_copy(g_ref.at[g.block(p|{g.core})],c_in.at[i],csem.at[i],crem.at[i],device_id=g.partner(g.core),device_id_type=MESH)
        c.start(); sends.append(c)
    small.start()
    def first(o,s):
        p=place_of(g.orders[o],s); i=number[p]
        if p not in here:
            here.add(p)
            pltpu.make_async_remote_copy(c_in.at[i],c_in.at[i],csem.at[i],crem.at[i],device_id=g.partner(g.core),device_id_type=MESH).wait_recv()
        lanes=slice(o*L,(o+1)*L)
        return g_ref[g.block(p),:,lanes].astype(F32)+c_in[i,:,lanes].astype(F32)
    def send(o,s,j,v):
        out_buf[o,s]=v.astype(BF)
        flush()
        pending.append(pltpu.make_async_remote_copy(out_buf.at[o,s],in_buf.at[o,s],ssem.at[o,s],rsem.at[o,s],device_id=g.partner(g.orders[o][j]),device_id_type=MESH))
    def arrived(o,s,j):
        pltpu.make_async_remote_copy(out_buf.at[o,s],in_buf.at[o,s],ssem.at[o,s],rsem.at[o,s],device_id=g.partner(g.orders[o][j]),device_id_type=MESH).wait_recv()
        return in_buf[o,s].astype(F32)
    half=full//2
    for s in range(full-1,half-1,-1):
        for o in range(n): send(o,s,0,first(o,s))
    flush()
    for s in range(half-1,-1,-1):
        for o in range(n): acc[o,s]=first(o,s)
    small.step()
    for j in range(1,m):
        half=full>>(j+1)
        for s in range(2*half-1,half-1,-1):
            for o in range(n): send(o,s,j,acc[o,s]+arrived(o,s+2*half,j-1))
        flush()
        for s in range(half-1,-1,-1):
            for o in range(n): acc[o,s]+=arrived(o,s+2*half,j-1)
        small.step()
    for o in range(n): out_ref[:,o*L:(o+1)*L]=acc[o,0]+arrived(o,1,m-1)
    for _ in g.all_bits: small.step()
    for c in sends: c.wait_send()

def scatter_mixer(grad,small):
    g=Grid(); n=len(g.orders); full=1<<len(g.orders[0]); nb=len(g.all_bits)
    _,w,D=grad.shape; L=D//n
    V=pl.BlockSpec(memory_space=pltpu.VMEM); S=pltpu.SemaphoreType.DMA
    return pl.pallas_call(scatter_kernel,in_specs=[V,V],out_specs=[V,V],
        out_shape=[jax.ShapeDtypeStruct((w,D),F32),jax.ShapeDtypeStruct(small.shape,F32)],
        scratch_shapes=[pltpu.VMEM((full,w,D),BF),pltpu.VMEM((n,full//2,w,L),F32),pltpu.VMEM((n,full,w,L),BF),pltpu.VMEM((n,full,w,L),BF),
          pltpu.VMEM((nb,)+small.shape,F32),pltpu.VMEM((nb,)+small.shape,F32),
          S((full,)),S((full,)),S((n,full)),S((n,full)),S((nb,)),S((nb,))],
        compiler_params=pltpu.CompilerParams(collective_id=1,has_side_effects=True,vmem_limit_bytes=60<<20),
        cost_estimate=pl.CostEstimate(flops=0,bytes_accessed=grad.size*4,transcendentals=0),
        name="scatter_mixer")(grad,small)

def tie(*xs): return lax.optimization_barrier(xs)

def low_shift(n,nx,k): return [(i,i//nx*nx+(i%nx+k)%nx) for i in range(n)]
def high_shift(n,nx,k): return [(i,(i+k*nx)%n) for i in range(n)]


def on_device(
    tokens,
    routes,
    slot_order,
    prefix_len,
    ln1_gain,
    ln1_bias,
    mixer_weight,
    ln2_gain,
    ln2_bias,
    router_weight,
    expert_in,
    expert_out,
    cotangent,
):
    model_width = tokens.shape[1]
    token_count = tokens.shape[0]
    expert_total = router_weight.shape[1]
    local_experts = expert_in.shape[0]
    capacity = token_count // expert_total
    owner_count = lax.axis_size("expert")
    dp_count = lax.axis_size("dp")
    low = max(d for d in range(1, dp_count + 1) if dp_count % d == 0 and d * d <= dp_count)
    high = dp_count // low
    to_low = lambda a, k: lax.ppermute(a, "dp", low_shift(dp_count, low, k))
    to_high = lambda a, k: lax.ppermute(a, "dp", high_shift(dp_count, low, k))
    swap_owner = lambda a: lax.all_to_all(a, "expert", split_axis=0, concat_axis=0, tiled=True)
    route_flat = routes[:, 0]
    route_hot = route_flat[:, None] == jnp.arange(expert_total)[None, :]
    route_float = route_hot.astype(jnp.float32)
    count_pad = jnp.pad(jnp.sum(route_float, axis=0)[None, :], ((0, 7), (0, 128 - expert_total)))
    gathered, count_sum = gather_mixer(mixer_weight.T, count_pad)
    counts = count_sum[0, :expert_total]
    full_mixer = gathered.reshape(4 * model_width, model_width)
    earlier = (slot_order[None, :] < slot_order[:, None]).astype(jnp.bfloat16)
    ahead_count = jnp.dot(
        earlier, route_hot.astype(jnp.bfloat16), preferred_element_type=jnp.float32
    )
    slot_rank = jnp.sum(ahead_count * route_float, axis=1).astype(jnp.int32)
    part_rows = owner_count * capacity
    slot_index = (
        route_flat % local_experts * part_rows + route_flat // local_experts * capacity + slot_rank
    )
    is_kept = slot_rank < capacity
    slot_hot = (
        (slot_index[:, None] == jnp.arange(expert_total * capacity)[None, :]) & is_kept[:, None]
    ).astype(jnp.bfloat16)
    experts = range(local_experts)
    outgoing = contract_rows(slot_hot, cotangent).astype(jnp.bfloat16)
    outgoing, *shards, full_mixer = tie(
        outgoing,
        *[expert_in[e] for e in experts],
        *[expert_out[e] for e in experts],
        full_mixer,
    )
    cot_home = swap_owner(
        outgoing.reshape(local_experts, owner_count, capacity, model_width)
        .transpose(1, 0, 2, 3)
        .reshape(owner_count, local_experts * capacity, model_width)
    )
    ins = [[a] + [to_low(a, k) for k in range(1, low)] for a in shards[:local_experts]]
    outs = [[a] + [to_low(a, k) for k in range(1, low)] for a in shards[local_experts:]]
    inner_weight = full_mixer[: 3 * model_width]
    outer_weight = full_mixer[3 * model_width :]
    inputs = tokens.astype(jnp.float32)
    normed, norm_pull = jax.vjp(layer_norm, inputs, ln1_gain, ln1_bias)
    normed_low = normed.astype(jnp.bfloat16)
    projected = times_transposed(normed_low, inner_weight).astype(jnp.bfloat16)
    attended, head_lse = attn_fwd(prefix_len, projected)
    attended, *ins[0] = tie(attended, *ins[0])
    middle = inputs + times_transposed(attended, outer_weight)
    normed2, norm2_pull = jax.vjp(layer_norm, middle, ln2_gain, ln2_bias)
    normed2_low = normed2.astype(jnp.bfloat16)
    chosen = jnp.sum(
        jnp.dot(normed2_low, router_weight, preferred_element_type=jnp.float32) * route_float, axis=1
    )
    gate_value = jax.nn.sigmoid(chosen)
    first_expert = lax.axis_index("expert") * local_experts
    grad_rows, produced_parts, moved, in_grads, out_grads = [], [], [], [], []
    router_part = jnp.zeros((model_width, expert_total), jnp.float32)
    normed2_low, cot_home = tie(normed2_low, cot_home)
    cot_rows = [cot_home] + [to_high(cot_home, k) for k in range(1, high)]
    cot_sets = [
        [
            a.reshape(owner_count, local_experts, capacity, model_width)
            for a in cot_rows
        ]
        for e in experts
    ]
    home = []
    for e in experts:
        hot = slot_hot[:, e * part_rows : (e + 1) * part_rows]
        source = normed2_low
        if e == 1:
            source, *outs[0] = tie(normed2_low, *outs[0])
        outgoing = contract_rows(hot, source).astype(jnp.bfloat16)
        home.append(swap_owner(outgoing.reshape(owner_count, capacity, model_width)))
    row_sets = [[a] + [to_high(a, k) for k in range(1, high)] for a in home]
    tied = tie(*row_sets[0], *home[1:], *[a for e in experts[1:] for a in ins[e]])
    row_sets[0], tied = list(tied[:high]), tied[high:]
    for e in range(1, local_experts):
        row_sets[e][0] = tied[e - 1]
        ins[e] = list(tied[local_experts - 1 + (e - 1) * low :][:low])
    for e in experts:
        column = (jnp.arange(expert_total) == first_expert + e).astype(jnp.float32)
        router_column = jnp.sum(router_weight.astype(jnp.float32) * column[None, :], axis=1)
        produced, slot_grad, in_part, out_part, router_row = run_expert(
            e, router_column[None, :], row_sets[e], cot_sets[e], ins[e], outs[e]
        )
        grad_rows.append(slot_grad)
        produced_parts.append(produced)
        moved.append([to_high(slot_grad[k], -k) for k in range(1, high)])
        for parts, sums in ((in_part, in_grads), (out_part, out_grads)):
            sums.append([parts[0]] + [to_low(parts[k], -k) for k in range(1, low)])
        router_part = router_part + router_row[0][:, None] * column[None, :]
    router_part, *held = tie(router_part, *[a for e in experts[:-1] for a in moved[e]])
    moved[:-1] = [held[e * (high - 1) : (e + 1) * (high - 1)] for e in experts[:-1]]
    back_rows = []
    for e in experts:
        total = grad_rows[e][0]
        for a in moved[e]:
            total = total + a.astype(jnp.float32)
        back_rows.append(swap_owner(total.astype(jnp.bfloat16)))
    tied = tie(*[a for p in produced_parts for a in p[1:]], *moved[-1])
    totals = []
    for e in experts:
        total = produced_parts[e][0]
        for k in range(1, high):
            total = total + to_high(tied[e * (high - 1) + k - 1], -k).astype(jnp.float32)
        totals.append(total.astype(jnp.bfloat16))
    produced_home = swap_owner(jnp.concatenate(totals, axis=1))
    produced_home = produced_home.reshape(owner_count, local_experts, capacity, model_width)
    out_grad = cotangent.astype(jnp.float32)
    mean_load = jnp.sum(counts) / expert_total
    load_weight = (
        (jnp.sum(route_float * counts[None, :], axis=1) - mean_load) / mean_load / jnp.sum(counts)
    )
    balance_part = jnp.sum(load_weight * gate_value)
    load_grad = load_weight * gate_value * (1.0 - gate_value)
    load_full = (load_grad[:, None] * route_float).astype(jnp.bfloat16)
    router_part = router_part + contract_rows(normed2_low, load_full)
    normed2_grad = times_transposed(load_full, router_weight) + jnp.dot(
        slot_hot,
        jnp.concatenate([r.reshape(part_rows, model_width) for r in back_rows]),
        preferred_element_type=jnp.float32,
    )
    returned = jnp.dot(
        slot_hot,
        produced_home.transpose(1, 0, 2, 3).reshape(expert_total * capacity, model_width),
        preferred_element_type=jnp.float32,
    )
    mixed_out = (middle + gate_value[:, None] * returned).astype(jnp.bfloat16)
    middle_part, ln2_gain_part, ln2_bias_part = norm2_pull(normed2_grad)
    middle_grad = out_grad + middle_part
    attn_grad = middle_grad.astype(jnp.bfloat16)
    outer_grad = contract_rows(attn_grad, attended).astype(jnp.bfloat16)
    attended_grad = nn(attn_grad, outer_weight).astype(jnp.bfloat16)
    parts = attn_bwd(prefix_len, projected, attended, attended_grad, head_lse)
    grad_blocks = jnp.concatenate(
        [contract_rows(part, normed_low).astype(jnp.bfloat16) for part in parts] + [outer_grad]
    ).reshape(dp_count * owner_count, -1, model_width)
    normed_grad = sum(
        nn(part, inner_weight[c * model_width : (c + 1) * model_width])
        for c, part in enumerate(parts)
    )
    flat = [a for group in in_grads + out_grads for a in group[1:]]
    normed_grad, *flat = tie(normed_grad, *flat)
    join = lambda groups: jnp.stack(
        [sum((flat.pop(0).astype(jnp.float32) for _ in g[1:]), g[0]) for g in groups]
    )
    expert_in_grad = join(in_grads)
    expert_out_grad = join(out_grads)
    input_part, ln1_gain_part, ln1_bias_part = norm_pull(normed_grad)
    tokens_grad = middle_grad + input_part
    small = jnp.concatenate(
        [
            jnp.stack([ln1_gain_part, ln1_bias_part, ln2_gain_part, ln2_bias_part]),
            jnp.full((4, model_width), balance_part),
            router_part.T,
        ]
    )
    mixer_grad, summed = scatter_mixer(grad_blocks, small)
    return (
        mixed_out,
        tokens_grad,
        summed[0],
        summed[1],
        mixer_grad.T,
        summed[2],
        summed[3],
        summed[8:].T,
        expert_in_grad,
        expert_out_grad,
        summed[4, 0],
    )


def solution(mesh):
    in_specs = (
        P(("dp", "expert"), None),
        P(("dp", "expert"), None),
        P(("dp", "expert")),
        P(("dp", "expert")),
        P(),
        P(),
        P(None, ("dp", "expert")),
        P(),
        P(),
        P(),
        P("expert", "dp", None),
        P("expert", "dp", None),
        P(("dp", "expert"), None),
    )
    out_specs = (
        P(("dp", "expert"), None),
        P(("dp", "expert"), None),
        P(),
        P(),
        P(None, ("dp", "expert")),
        P(),
        P(),
        P(),
        P("expert", "dp", None),
        P("expert", "dp", None),
        P(),
    )
    return jax.shard_map(
        on_device, mesh=mesh, in_specs=in_specs, out_specs=out_specs, check_vma=False
    )
```

```python
import functools

import jax
import jax.numpy as jnp
from jax import lax
from jax.experimental import pallas as pl
from jax.experimental.pallas import tpu as pltpu
from jax.sharding import PartitionSpec as P


epsilon = 1e-05


def layer_norm(values, gain_vec, offset):
    center = values - jnp.mean(values, axis=-1, keepdims=True)
    spread = jnp.mean(center * center, axis=-1, keepdims=True)
    return center * lax.rsqrt(spread + epsilon) * gain_vec + offset


def contract_rows(first_op, second_op):
    return lax.dot_general(
        first_op, second_op, (((0,), (0,)), ((), ())), preferred_element_type=jnp.float32
    )


def times_transposed(first_op, second_op):
    return lax.dot_general(
        first_op, second_op, (((1,), (1,)), ((), ())), preferred_element_type=jnp.float32
    )


BF=jnp.bfloat16; F32=jnp.float32
NEG=-1e9
QB=256
def key_extent(i, n):
    return max((i+1)*QB, 512)

def nt(a,b): return lax.dot_general(a,b,(((1,),(1,)),((),())),preferred_element_type=F32)
def nn(a,b): return lax.dot_general(a,b,(((1,),(0,)),((),())),preferred_element_type=F32)

def fill_bias(bias_ref, prefix):
    kp=lax.broadcasted_iota(jnp.int32,(QB,QB),0); qp=lax.broadcasted_iota(jnp.int32,(QB,QB),1)
    causal=kp<=qp
    bias_ref[0]=jnp.where(causal|(kp<prefix),0.0,NEG)
    bias_ref[1]=jnp.where(kp+QB<prefix,0.0,NEG)+jnp.zeros((QB,QB),F32)
    bias_ref[2]=jnp.where(causal|(kp+QB<prefix),0.0,NEG)
    bias_ref[3]=jnp.where(causal,0.0,NEG)

def block_bias(j,i):
    if j==0 and i==0: return 0
    if j==1 and i==0: return 1
    if j==1 and i==1: return 2
    if j==i: return 3
    return None

def fwd_kernel(pre_ref,q_ref,k_ref,v_ref,o_ref,lse_ref,bias_ref):
    @pl.when(pl.program_id(0)==0)
    def _(): fill_bias(bias_ref,pre_ref[0])
    T=q_ref.shape[0]
    lane=lax.broadcasted_iota(jnp.int32,(1,128),1)
    vT=v_ref[...].T
    ones=jnp.ones((16,T),BF)
    for i in range(T//QB):
        K=key_extent(i,T)
        q=q_ref[i*QB:(i+1)*QB,:]*jnp.asarray(0.125,BF)
        outs=[]
        for h in range(2):
            qh=jnp.where((lane<64) if h==0 else (lane>=64), q, jnp.zeros_like(q))
            parts=[]
            for j in range(K//QB):
                s=nt(k_ref[j*QB:(j+1)*QB,:],qh)
                b=block_bias(j,i)
                if b is not None: s=s+bias_ref[b]
                parts.append(s)
            m=functools.reduce(jnp.maximum,[jnp.max(s,axis=0,keepdims=True) for s in parts])
            vh=jnp.concatenate([vT[h*64:(h+1)*64],ones],axis=0)
            acc=None
            for j,s in enumerate(parts):
                p=jnp.exp(s-m).astype(BF)
                c=nn(vh[:,j*QB:(j+1)*QB],p)
                acc=c if acc is None else acc+c
            l=acc[64:65]
            outs.append(acc[:64]*(1.0/l))
            lse_ref[0,h:h+1,i*QB:(i+1)*QB]=m+jnp.log(l)
        o_ref[i*QB:(i+1)*QB,:]=jnp.concatenate(outs,axis=0).T.astype(BF)

def attn_fwd(prefix,proj):
    T=proj.shape[0]; W=proj.shape[1]//3; n=W//128
    return pl.pallas_call(fwd_kernel,grid=(n,),
        in_specs=[pl.BlockSpec(memory_space=pltpu.SMEM)]+[pl.BlockSpec((T,128),functools.partial(lambda c,j:(0,c*n+j),c)) for c in range(3)],
        out_specs=[pl.BlockSpec((T,128),lambda j:(0,j)),pl.BlockSpec((1,2,T),lambda j:(j,0,0))],
        out_shape=[jax.ShapeDtypeStruct((T,W),BF),jax.ShapeDtypeStruct((n,2,T),F32)],
        scratch_shapes=[pltpu.VMEM((4,QB,QB),F32)],
        compiler_params=pltpu.CompilerParams(vmem_limit_bytes=60<<20),
        name="attn_fwd")(prefix,proj,proj,proj)

def bwd_kernel(pre_ref,q_ref,k_ref,v_ref,o_ref,g_ref,lse_ref,dq_ref,dk_ref,dv_ref,bias_ref,dk_acc,dv_acc):
    @pl.when(pl.program_id(0)==0)
    def _(): fill_bias(bias_ref,pre_ref[0])
    T=q_ref.shape[0]; nb=T//QB
    lane=lax.broadcasted_iota(jnp.int32,(1,128),1)
    kT=k_ref[...].T
    started=[False]*nb
    for i in range(nb-1,-1,-1):
        K=key_extent(i,T)
        rows=slice(i*QB,(i+1)*QB)
        q=q_ref[rows,:]*jnp.asarray(0.125,BF)
        g=g_ref[rows,:]
        dT=(g.astype(F32)*o_ref[rows,:].astype(F32)).T
        outs=[]
        for h in range(2):
            sel=(lane<64) if h==0 else (lane>=64)
            qh=jnp.where(sel,q,jnp.zeros_like(q)); gh=jnp.where(sel,g,jnp.zeros_like(g))
            lse=lse_ref[0,h:h+1,rows]
            delta=jnp.sum(dT[h*64:(h+1)*64],axis=0,keepdims=True)
            dq=None
            for j in range(K//QB):
                kr=slice(j*QB,(j+1)*QB)
                s=nt(k_ref[kr,:],qh)
                b=block_bias(j,i)
                if b is not None: s=s+bias_ref[b]
                p=jnp.exp(s-lse)
                dp=nt(v_ref[kr,:],gh)
                ds=(p*(dp-delta)).astype(BF)
                dv=nn(p.astype(BF),gh)
                dk=nn(ds,qh)
                first=(i==nb-1 and h==0)
                if first: dv_acc[kr,:]=dv; dk_acc[kr,:]=dk
                else:
                    dv_acc[kr,:]+=dv; dk_acc[kr,:]+=dk
                c=nn(kT[h*64:(h+1)*64,kr],ds)
                dq=c if dq is None else dq+c
            outs.append(dq)
        dq_ref[rows,:]=(jnp.concatenate(outs,axis=0).T*0.125).astype(BF)
    dk_ref[...]=dk_acc[...].astype(BF)
    dv_ref[...]=dv_acc[...].astype(BF)

def attn_bwd(prefix,proj,att,grad,lse):
    T=proj.shape[0]; W=proj.shape[1]//3; n=W//128
    cb=lambda: pl.BlockSpec((T,128),lambda j:(0,j))
    return pl.pallas_call(bwd_kernel,grid=(n,),
        in_specs=[pl.BlockSpec(memory_space=pltpu.SMEM)]+[pl.BlockSpec((T,128),functools.partial(lambda c,j:(0,c*n+j),c)) for c in range(3)]
          +[cb(),cb(),pl.BlockSpec((1,2,T),lambda j:(j,0,0))],
        out_specs=[cb()]*3,
        out_shape=[jax.ShapeDtypeStruct((T,W),BF)]*3,
        scratch_shapes=[pltpu.VMEM((4,QB,QB),F32),pltpu.VMEM((T,128),F32),pltpu.VMEM((T,128),F32)],
        compiler_params=pltpu.CompilerParams(vmem_limit_bytes=60<<20),
        name="attn_bwd")(prefix,proj,proj,proj,att,grad,lse)

def tn(a,b): return lax.dot_general(a,b,(((0,),(0,)),((),())),preferred_element_type=F32)

ERF_TOP=3.832506856900711
ERF_NUM=(0.00022905065861350646,0.0034082910107109506,0.050955695062380861,0.18520832239976145,1.128379143519084)
ERF_DEN=(-1.1791602954361697e-7,0.000023547966471313185,0.0010179625278914885,0.014070470171167667,0.11098505178285362,0.49746925110067538,1.0)

def erf32(x):
    x=jnp.clip(x,-ERF_TOP,ERF_TOP); y=x*x
    n=ERF_NUM[0]
    for c in ERF_NUM[1:]: n=n*y+c
    d=ERF_DEN[0]
    for c in ERF_DEN[1:]: d=d*y+c
    return x*n/d

def rows_kernel(nw,tiles,rw_ref,x_ref,c_ref,*refs):
    wi_refs,wo_refs=refs[:nw],refs[nw:2*nw]
    p_ref,d_ref,act_ref,dp_ref,g_ref,rg_ref,gate_s,p_acc,d_acc=refs[2*nw:]
    step=pl.program_id(0)
    S,C,D=x_ref.shape; R=S*C
    @pl.when(step==0)
    def _():
        gate=jax.nn.sigmoid(jnp.sum(x_ref[...].reshape(R,D).astype(F32)*rw_ref[...],axis=1,keepdims=True))
        g_ref[...]=(gate*c_ref[...].reshape(R,D).astype(F32)).astype(BF)
        gate_s[...]=gate
    for w in range(nw):
        @pl.when(step//tiles==w)
        def _(w=w):
            wi=wi_refs[w][...]; wo=wo_refs[w][...]
            F=wi.shape[0]; sub=256 if F%256==0 else F
            x=x_ref[...].reshape(R,D); g=g_ref[...]
            for i in range(0,F,sub):
                pre=nt(x,wi[i:i+sub])
                da=nt(g,wo[i:i+sub])
                phi=0.5+0.5*erf32(pre*0.7071067811865476)
                act_ref[:,i:i+sub]=(pre*phi).astype(BF)
                dens=0.3989422804014327*jnp.exp(-0.5*pre*pre)
                dp_ref[:,i:i+sub]=(da*(phi+pre*dens)).astype(BF)
            p=nn(act_ref[...],wo); d=nn(dp_ref[...],wi)
            if w==0:
                @pl.when(step==0)
                def _(): p_acc[...]=p; d_acc[...]=d
                @pl.when(step>0)
                def _(): p_acc[...]+=p; d_acc[...]+=d
            else: p_acc[...]+=p; d_acc[...]+=d
    @pl.when(step==nw*tiles-1)
    def _():
        p=p_acc[...]; gate=gate_s[...]
        dot=jnp.sum(p*c_ref[...].reshape(R,D).astype(F32),axis=1,keepdims=True)
        lg=dot*(gate*(1.0-gate))
        p_ref[...]=p.reshape(S,C,D).astype(p_ref.dtype)
        d_ref[...]=(d_acc[...]+lg*rw_ref[...]).reshape(S,C,D).astype(d_ref.dtype)
        rg_ref[...]=jnp.sum(lg*x_ref[...].reshape(R,D).astype(F32),axis=0,keepdims=True)

def tile_of(Q):
    return Q

def run_rows(kind,rw,x,c,wis,wos):
    nw=len(wis); S,C,D=x.shape; Q=wis[0].shape[0]; R=S*C; tile=tile_of(Q); tiles=Q//tile
    whole=lambda shape: pl.BlockSpec(shape,lambda i:(0,)*len(shape))
    at=lambda w: (lambda i: jnp.clip(i-w*tiles,0,tiles-1))
    wspec=lambda w: pl.BlockSpec((tile,D),lambda i,f=at(w):(f(i),0))
    wide=pl.BlockSpec((None,R,tile),lambda i:(i,0,0))
    return pl.pallas_call(functools.partial(rows_kernel,nw,tiles),grid=(nw*tiles,),
        in_specs=[whole((1,D)),whole((S,C,D)),whole((S,C,D))]+[wspec(w) for w in range(nw)]*2,
        out_specs=[whole((S,C,D))]*2+[wide,wide,whole((R,D)),whole((1,D))],
        out_shape=[jax.ShapeDtypeStruct((S,C,D),kind)]*2+[jax.ShapeDtypeStruct((nw*tiles,R,tile),BF)]*2
          +[jax.ShapeDtypeStruct((R,D),BF),jax.ShapeDtypeStruct((1,D),F32)],
        scratch_shapes=[pltpu.VMEM((R,1),F32),pltpu.VMEM((R,D),F32),pltpu.VMEM((R,D),F32)],
        compiler_params=pltpu.CompilerParams(vmem_limit_bytes=60<<20),
        cost_estimate=pl.CostEstimate(flops=8*R*nw*Q*D,bytes_accessed=nw*Q*(4*D+4*R)+R*D*10,transcendentals=R*nw*Q),
        name="expert_rows")(rw,x,c,*wis,*wos)

def grads_kernel(nr,nw,tiles,*refs):
    x_refs,g_refs,act_refs,dp_refs=(refs[i*nr:(i+1)*nr] for i in range(4))
    gi_refs,go_refs=refs[4*nr:4*nr+nw],refs[4*nr+nw:]
    step=pl.program_id(0)
    S,C,D=x_refs[0].shape
    gi=sum(tn(d[...],x[...].reshape(S*C,D)) for d,x in zip(dp_refs,x_refs)).astype(BF)
    go=sum(tn(a[...],g[...]) for a,g in zip(act_refs,g_refs)).astype(BF)
    for w in range(nw):
        @pl.when(step//tiles==w)
        def _(w=w):
            gi_refs[w][...]=gi; go_refs[w][...]=go

def run_grads(nw,xs,gs,acts,dps):
    nr=len(xs); S,C,D=xs[0].shape; R=S*C; tile=acts[0].shape[2]; tiles=acts[0].shape[0]//nw; Q=tiles*tile
    whole=lambda shape: pl.BlockSpec(shape,lambda i:(0,)*len(shape))
    gspec=lambda w: pl.BlockSpec((tile,D),lambda i:(jnp.clip(i-w*tiles,0,tiles-1),0))
    outs=pl.pallas_call(functools.partial(grads_kernel,nr,nw,tiles),grid=(nw*tiles,),
        in_specs=[whole((S,C,D))]*nr+[whole((R,D))]*nr+[pl.BlockSpec((None,R,tile),lambda i:(i,0,0))]*(2*nr),
        out_specs=[gspec(w) for w in range(nw)]*2,
        out_shape=[jax.ShapeDtypeStruct((Q,D),BF)]*(2*nw),
        compiler_params=pltpu.CompilerParams(vmem_limit_bytes=60<<20),
        cost_estimate=pl.CostEstimate(flops=4*nr*R*nw*Q*D,bytes_accessed=nw*Q*D*4+nr*R*(4*D+4*nw*Q),transcendentals=0),
        name="expert_grads")(*xs,*gs,*acts,*dps)
    return list(outs[:nw]),list(outs[nw:])

MESH=pl.DeviceIdType.MESH

class Grid:
    def __init__(self):
        self.dp=lax.axis_size("dp"); self.expert=lax.axis_size("expert")
        bits=lambda n: n.bit_length()-1
        dp_bits=[("dp",1<<i) for i in range(bits(self.dp))]
        ex_bits=[("expert",1<<i) for i in range(bits(self.expert))]
        h=len(dp_bits)//2
        xs,ys,zs=dp_bits[:h],dp_bits[h:],ex_bits[1:]
        self.core=ex_bits[0]
        self.orders=[xs+ys+zs,ys+xs+zs,zs+xs+ys]
        self.all_bits=[self.core]+zs+xs+ys
    def here(self): self.at={"dp":lax.axis_index("dp"),"expert":lax.axis_index("expert")}
    def flip(self,k): return (1-2*(self.at[k[0]]//k[1]%2))*k[1]
    def partner(self,k): return {k[0]:self.at[k[0]]+self.flip(k)}
    def block(self,place):
        dp,ex=self.at["dp"],self.at["expert"]
        for k in place:
            if k[0]=="dp": dp=dp+self.flip(k)
            else: ex=ex+self.flip(k)
        return dp*self.expert+ex
    def greet(self):
        barrier=pltpu.get_barrier_semaphore()
        for k in self.all_bits: pl.semaphore_signal(barrier,inc=1,device_id=self.partner(k),device_id_type=MESH)
        pl.semaphore_wait(barrier,len(self.all_bits))

def place_of(order,code):
    m=len(order)
    return frozenset(order[i] for i in range(m) if code>>(m-1-i)&1)

class SmallSum:
    def __init__(self,g,small_ref,sum_ref,buf,arrive,ssem,rsem):
        self.g,self.sum_ref,self.buf,self.arrive,self.ssem,self.rsem=g,sum_ref,buf,arrive,ssem,rsem
        self.i=0
        buf[0]=small_ref[...]
    def start(self):
        i=self.i
        self.copy=pltpu.make_async_remote_copy(self.buf.at[i],self.arrive.at[i],self.ssem.at[i],self.rsem.at[i],device_id=self.g.partner(self.g.all_bits[i]),device_id_type=MESH)
        self.copy.start()
    def step(self):
        i=self.i
        if i>=len(self.g.all_bits): return
        self.copy.wait()
        v=self.buf[i]+self.arrive[i]
        self.i=i+1
        if self.i<len(self.g.all_bits): self.buf[i+1]=v; self.start()
        else: self.sum_ref[...]=v

def gather_kernel(nx,w_ref,small_ref,*refs):
    x_refs=refs[:nx]; out_ref,sum_ref=refs[nx:nx+2]; count=x_refs[0].shape[0]
    y_refs=refs[nx+2:nx+2+nx*count]
    s_buf,s_in,hold,ssem,rsem,cs,cr,sssem,srsem,isem,osem=refs[nx+2+nx*count:]
    g=Grid(); g.here(); g.greet()
    loads=[pltpu.make_async_copy(x_refs[i//count].at[i%count],hold.at[i],isem.at[i]) for i in range(nx*count)]
    stores=[pltpu.make_async_copy(hold.at[i],y_refs[i],osem.at[i]) for i in range(nx*count)]
    small=SmallSum(g,small_ref,sum_ref,s_buf,s_in,sssem,srsem)
    D=w_ref.shape[1]; n=len(g.orders); L=D//n
    chip=g.orders[0]; number={place_of(chip,c):c for c in range(1<<len(chip))}
    out_ref[g.block(())]=w_ref[...]
    sends=[]; core_in=[]
    def view(o,place): return out_ref.at[g.block(place),:,o*L:(o+1)*L]
    def source(o,place): return view(o,place) if place else w_ref.at[:,o*L:(o+1)*L]
    def send(o,place,k):
        to=number[place^{k}]
        c=pltpu.make_async_remote_copy(source(o,place),view(o,place),ssem.at[o,to],rsem.at[o,to],device_id=g.partner(k),device_id_type=MESH)
        c.start(); sends.append(c)
    def arrived(o,place,k):
        i=number[place]
        pltpu.make_async_remote_copy(view(o,place),view(o,place),ssem.at[o,i],rsem.at[o,i],device_id=g.partner(k),device_id_type=MESH).wait_recv()
    def across(o,place):
        i=number[place]
        c=pltpu.make_async_remote_copy(source(o,place),view(o,place),cs.at[o,i],cr.at[o,i],device_id=g.partner(g.core),device_id_type=MESH)
        c.start(); sends.append(c)
        v=view(o,place|{g.core})
        core_in.append(pltpu.make_async_remote_copy(v,v,cs.at[o,i],cr.at[o,i],device_id=g.partner(g.core),device_id_type=MESH))
    m=len(chip)
    held=[[frozenset()] for _ in g.orders]
    fresh=[[] for _ in g.orders]
    for j in range(m):
        for o,order in enumerate(g.orders):
            k=order[m-1-j]
            for p in held[o]: send(o,p,k)
            if j==0: across(o,frozenset())
        if j==0:
            small.start()
            for c in loads: c.start()
        else: small.step()
        for o,order in enumerate(g.orders):
            k=order[m-1-j]
            for p in fresh[o]:
                arrived(o,p,order[m-j]); send(o,p,k); across(o,p)
            held[o]=held[o]+fresh[o]
            fresh[o]=[p|{k} for p in held[o]]
        if j==1:
            for a,b in zip(loads,stores): a.wait(); b.start()
    for i in range(len(fresh[0])):
        for o,order in enumerate(g.orders):
            arrived(o,fresh[o][i],order[0]); across(o,fresh[o][i])
    for _ in g.all_bits: small.step()
    for c in core_in: c.wait_recv()
    for c in sends: c.wait_send()
    for c in stores: c.wait()

def gather_mixer(w,small,stacks):
    g=Grid(); n=g.dp*g.expert; half=n//2; k=len(g.orders); nb=len(g.all_bits)
    V=pl.BlockSpec(memory_space=pltpu.VMEM); S=pltpu.SemaphoreType.DMA
    D=w.shape[1]
    nx=len(stacks); count,Q,_=stacks[0].shape; A=pl.BlockSpec(memory_space=pl.ANY)
    outs=pl.pallas_call(functools.partial(gather_kernel,nx),
        in_specs=[V,V]+[A]*nx,out_specs=[V,V]+[A]*(nx*count),
        out_shape=[jax.ShapeDtypeStruct((n,)+w.shape,w.dtype),jax.ShapeDtypeStruct(small.shape,F32)]
          +[jax.ShapeDtypeStruct((Q,D),w.dtype)]*(nx*count),
        scratch_shapes=[pltpu.VMEM((nb,)+small.shape,F32)]*2+[pltpu.VMEM((nx*count,Q,D),w.dtype)]+[S((k,half))]*4+[S((nb,))]*2+[S((nx*count,))]*2,
        compiler_params=pltpu.CompilerParams(collective_id=0,has_side_effects=True,vmem_limit_bytes=60<<20),
        cost_estimate=pl.CostEstimate(flops=0,bytes_accessed=n*w.size*2,transcendentals=0),
        name="gather_mixer")(w,small,*stacks)
    return outs[0],outs[1],[list(outs[2+i*count:2+(i+1)*count]) for i in range(nx)]

def scatter_kernel(g_ref,small_ref,out_ref,sum_ref,c_in,acc,out_buf,in_buf,s_buf,s_in,csem,crem,ssem,rsem,sssem,srsem):
    g=Grid(); g.here(); g.greet()
    D=g_ref.shape[2]; n=len(g.orders); L=D//n
    chip=g.orders[0]; m=len(chip); full=1<<m
    number={place_of(chip,c):c for c in range(full)}
    sends=[]; here=set(); pending=[]
    def flush():
        for c in pending: c.start(); sends.append(c)
        pending.clear()
    small=SmallSum(g,small_ref,sum_ref,s_buf,s_in,sssem,srsem)
    cross=[]
    for s in range(full-1,-1,-1):
        for order in g.orders:
            p=place_of(order,s)
            if p in cross: continue
            cross.append(p)
    for p in cross:
        i=number[p]
        c=pltpu.make_async_remote_copy(g_ref.at[g.block(p|{g.core})],c_in.at[i],csem.at[i],crem.at[i],device_id=g.partner(g.core),device_id_type=MESH)
        c.start(); sends.append(c)
    small.start()
    def first(o,s):
        p=place_of(g.orders[o],s); i=number[p]
        if p not in here:
            here.add(p)
            pltpu.make_async_remote_copy(c_in.at[i],c_in.at[i],csem.at[i],crem.at[i],device_id=g.partner(g.core),device_id_type=MESH).wait_recv()
        lanes=slice(o*L,(o+1)*L)
        return g_ref[g.block(p),:,lanes].astype(F32)+c_in[i,:,lanes].astype(F32)
    def send(o,s,j,v):
        out_buf[o,s]=v.astype(BF)
        flush()
        pending.append(pltpu.make_async_remote_copy(out_buf.at[o,s],in_buf.at[o,s],ssem.at[o,s],rsem.at[o,s],device_id=g.partner(g.orders[o][j]),device_id_type=MESH))
    def arrived(o,s,j):
        pltpu.make_async_remote_copy(out_buf.at[o,s],in_buf.at[o,s],ssem.at[o,s],rsem.at[o,s],device_id=g.partner(g.orders[o][j]),device_id_type=MESH).wait_recv()
        return in_buf[o,s].astype(F32)
    half=full//2
    for s in range(full-1,half-1,-1):
        for o in range(n): send(o,s,0,first(o,s))
    flush()
    for s in range(half-1,-1,-1):
        for o in range(n): acc[o,s]=first(o,s)
    small.step()
    for j in range(1,m):
        half=full>>(j+1)
        for s in range(2*half-1,half-1,-1):
            for o in range(n): send(o,s,j,acc[o,s]+arrived(o,s+2*half,j-1))
        flush()
        for s in range(half-1,-1,-1):
            for o in range(n): acc[o,s]+=arrived(o,s+2*half,j-1)
        small.step()
    for o in range(n): out_ref[:,o*L:(o+1)*L]=acc[o,0]+arrived(o,1,m-1)
    for _ in g.all_bits: small.step()
    for c in sends: c.wait_send()

def scatter_mixer(grad,small):
    g=Grid(); n=len(g.orders); full=1<<len(g.orders[0]); nb=len(g.all_bits)
    _,w,D=grad.shape; L=D//n
    V=pl.BlockSpec(memory_space=pltpu.VMEM); S=pltpu.SemaphoreType.DMA
    return pl.pallas_call(scatter_kernel,in_specs=[V,V],out_specs=[V,V],
        out_shape=[jax.ShapeDtypeStruct((w,D),F32),jax.ShapeDtypeStruct(small.shape,F32)],
        scratch_shapes=[pltpu.VMEM((full,w,D),BF),pltpu.VMEM((n,full//2,w,L),F32),pltpu.VMEM((n,full,w,L),BF),pltpu.VMEM((n,full,w,L),BF),
          pltpu.VMEM((nb,)+small.shape,F32),pltpu.VMEM((nb,)+small.shape,F32),
          S((full,)),S((full,)),S((n,full)),S((n,full)),S((nb,)),S((nb,))],
        compiler_params=pltpu.CompilerParams(collective_id=1,has_side_effects=True,vmem_limit_bytes=60<<20),
        cost_estimate=pl.CostEstimate(flops=0,bytes_accessed=grad.size*4,transcendentals=0),
        name="scatter_mixer")(grad,small)

def join_kernel(count,sizes,*refs):
    outs=refs[sum(sizes):]; refs=list(refs[:sum(sizes)])
    for i,n in enumerate(sizes):
        parts=[refs.pop(0) for _ in range(n)]
        total=parts[0][...].astype(F32)
        for p in parts[1:]: total=total+p[...].astype(F32)
        outs[i//count][i%count]=total

def join_grads(groups,count):
    sizes=tuple(len(g) for g in groups); Q,D=groups[0][0].shape; tile=Q//4
    return pl.pallas_call(functools.partial(join_kernel,count,sizes),grid=(4,),
        in_specs=[pl.BlockSpec((tile,D),lambda i:(i,0))]*sum(sizes),
        out_specs=[pl.BlockSpec((count,tile,D),lambda i:(0,i,0))]*2,
        out_shape=[jax.ShapeDtypeStruct((count,Q,D),F32)]*2,
        compiler_params=pltpu.CompilerParams(vmem_limit_bytes=60<<20),
        cost_estimate=pl.CostEstimate(flops=0,bytes_accessed=Q*D*(8*count+2*sum(sizes)),transcendentals=0),
        name="join_grads")(*[p for g in groups for p in g])

def tie(*xs): return lax.optimization_barrier(xs)

def low_shift(n,nx,k): return [(i,i//nx*nx+(i%nx+k)%nx) for i in range(n)]
def high_shift(n,nx,k): return [(i,(i+k*nx)%n) for i in range(n)]


def on_device(
    tokens,
    routes,
    slot_order,
    prefix_len,
    ln1_gain,
    ln1_bias,
    mixer_weight,
    ln2_gain,
    ln2_bias,
    router_weight,
    expert_in,
    expert_out,
    cotangent,
):
    model_width = tokens.shape[1]
    token_count = tokens.shape[0]
    expert_total = router_weight.shape[1]
    local_experts = expert_in.shape[0]
    capacity = token_count // expert_total
    owner_count = lax.axis_size("expert")
    dp_count = lax.axis_size("dp")
    low = max(d for d in range(1, dp_count + 1) if dp_count % d == 0 and d * d <= dp_count)
    high = dp_count // low
    to_low = lambda a, k: lax.ppermute(a, "dp", low_shift(dp_count, low, k))
    to_high = lambda a, k: lax.ppermute(a, "dp", high_shift(dp_count, low, k))
    swap_owner = lambda a: lax.all_to_all(a, "expert", split_axis=0, concat_axis=0, tiled=True)
    route_flat = routes[:, 0]
    route_hot = route_flat[:, None] == jnp.arange(expert_total)[None, :]
    route_float = route_hot.astype(jnp.float32)
    count_pad = jnp.pad(jnp.sum(route_float, axis=0)[None, :], ((0, 7), (0, 128 - expert_total)))
    gathered, count_sum, (own_in, own_out) = gather_mixer(
        mixer_weight.T, count_pad, [expert_in, expert_out]
    )
    counts = count_sum[0, :expert_total]
    full_mixer = gathered.reshape(4 * model_width, model_width)
    earlier = (slot_order[None, :] < slot_order[:, None]).astype(jnp.bfloat16)
    ahead_count = jnp.dot(
        earlier, route_hot.astype(jnp.bfloat16), preferred_element_type=jnp.float32
    )
    slot_rank = jnp.sum(ahead_count * route_float, axis=1).astype(jnp.int32)
    part_rows = owner_count * capacity
    slot_index = (
        route_flat % local_experts * part_rows + route_flat // local_experts * capacity + slot_rank
    )
    is_kept = slot_rank < capacity
    slot_hot = (
        (slot_index[:, None] == jnp.arange(expert_total * capacity)[None, :]) & is_kept[:, None]
    ).astype(jnp.bfloat16)
    experts = range(local_experts)
    outgoing = contract_rows(slot_hot, cotangent).astype(jnp.bfloat16)
    outgoing, full_mixer = tie(outgoing, full_mixer)
    cot_home = swap_owner(
        outgoing.reshape(local_experts, owner_count, capacity, model_width)
        .transpose(1, 0, 2, 3)
        .reshape(owner_count, local_experts * capacity, model_width)
    )
    row_move = [(to_high, high) if e % 2 == 0 else (to_low, low) for e in experts]
    weight_move = [(to_low, low) if e % 2 == 0 else (to_high, high) for e in experts]
    spread = lambda a, move: [a] + [move[0](a, k) for k in range(1, move[1])]
    gather_back = lambda parts, move: [parts[0]] + [move[0](parts[k], -k) for k in range(1, move[1])]
    ins = [spread(own_in[e], weight_move[e]) for e in experts]
    outs = [spread(own_out[e], weight_move[e]) for e in experts]
    inner_weight = full_mixer[: 3 * model_width]
    outer_weight = full_mixer[3 * model_width :]
    inputs = tokens.astype(jnp.float32)
    normed, norm_pull = jax.vjp(layer_norm, inputs, ln1_gain, ln1_bias)
    normed_low = normed.astype(jnp.bfloat16)
    projected = times_transposed(normed_low, inner_weight).astype(jnp.bfloat16)
    attended, head_lse = attn_fwd(prefix_len, projected)
    middle = inputs + times_transposed(attended, outer_weight)
    normed2, norm2_pull = jax.vjp(layer_norm, middle, ln2_gain, ln2_bias)
    normed2_low = normed2.astype(jnp.bfloat16)
    chosen = jnp.sum(
        jnp.dot(normed2_low, router_weight, preferred_element_type=jnp.float32) * route_float, axis=1
    )
    gate_value = jax.nn.sigmoid(chosen)
    first_expert = lax.axis_index("expert") * local_experts
    in_grads, out_grads = [], []
    router_part = jnp.zeros((model_width, expert_total), jnp.float32)
    normed2_low, cot_home = tie(normed2_low, cot_home)
    cot_home = cot_home.reshape(owner_count, local_experts, capacity, model_width)
    cot_rows = [spread(cot_home[:, e], row_move[e]) for e in experts]
    home = []
    for e in experts:
        hot = slot_hot[:, e * part_rows : (e + 1) * part_rows]
        source = normed2_low
        if e == 1:
            source, *tied = tie(normed2_low, *[a for g in ins + outs for a in g])
            tied = [[tied.pop(0) for _ in g] for g in ins + outs]
            ins, outs = tied[:local_experts], tied[local_experts:]
        outgoing = contract_rows(hot, source).astype(jnp.bfloat16)
        home.append(swap_owner(outgoing.reshape(owner_count, capacity, model_width)))
    home[0], *cot_rows[0] = tie(home[0], *cot_rows[0])
    first_rows = spread(home[0], row_move[0])
    row_sets = [first_rows] + [spread(home[e], row_move[e]) for e in experts[1:]]
    tied = tie(*first_rows, *ins[0], *outs[0], *home[1:])
    row_sets[0], tied = list(tied[: len(first_rows)]), tied[len(first_rows) + 2 * len(ins[0]) :]
    for e in experts[1:]:
        row_sets[e][0] = tied[e - 1]
    done = {}
    before = []
    for e in experts:
        column = (jnp.arange(expert_total) == first_expert + e).astype(jnp.float32)
        router_column = jnp.sum(router_weight.astype(jnp.float32) * column[None, :], axis=1)
        for r in [*range(1, row_move[e][1]), 0]:
            rows = row_sets[e][r]
            if before:
                rows = tie(rows, *before)[0]
            kind = F32 if r == 0 else BF
            done[e, r] = run_rows(
                kind, router_column[None, :], rows, cot_rows[e][r], ins[e], outs[e]
            )
            before = [done[e, r][5]]
            router_part = router_part + done[e, r][5][0][:, None] * column[None, :]
        parts = [done[e, r] for r in range(row_move[e][1])]
        tied = tie(*before, *[p[i] for p in parts for i in (4, 2, 3)])
        in_part, out_part = run_grads(weight_move[e][1], row_sets[e], tied[1::3], tied[2::3], tied[3::3])
        before = [in_part[0]]
        for own, sums in ((in_part, in_grads), (out_part, out_grads)):
            sums.append(gather_back(own, weight_move[e]))
    returning = lambda e, i: gather_back(
        [done[e, r][i] for r in range(row_move[e][1])], row_move[e]
    )
    moved = [returning(e, 1) for e in experts]
    gate_row = done[local_experts - 1, row_move[-1][1] - 1][5]
    moved[:-1] = [tie(*moved[e], gate_row)[:-1] for e in experts[:-1]]
    back_rows = []
    for e in experts:
        total = moved[e][0]
        for a in moved[e][1:]:
            total = total + a.astype(jnp.float32)
        back_rows.append(swap_owner(total.astype(jnp.bfloat16)))
    for e in experts:
        for r in range(1, row_move[e][1]):
            done[e, r] = [tie(done[e, r][0], *moved[-1])[0]] + list(done[e, r][1:])
    produced_moved = [returning(e, 0) for e in experts]
    out_grad = cotangent.astype(jnp.float32)
    mean_load = jnp.sum(counts) / expert_total
    load_weight = (
        (jnp.sum(route_float * counts[None, :], axis=1) - mean_load) / mean_load / jnp.sum(counts)
    )
    balance_part = jnp.sum(load_weight * gate_value)
    load_grad = load_weight * gate_value * (1.0 - gate_value)
    load_full = (load_grad[:, None] * route_float).astype(jnp.bfloat16)
    router_part = router_part + contract_rows(normed2_low, load_full)
    normed2_grad = times_transposed(load_full, router_weight) + jnp.dot(
        slot_hot,
        jnp.concatenate([r.reshape(part_rows, model_width) for r in back_rows]),
        preferred_element_type=jnp.float32,
    )
    middle_part, ln2_gain_part, ln2_bias_part = norm2_pull(normed2_grad)
    middle_grad = out_grad + middle_part
    attn_grad = middle_grad.astype(jnp.bfloat16)
    outer_grad = contract_rows(attn_grad, attended).astype(jnp.bfloat16)
    attended_grad = nn(attn_grad, outer_weight).astype(jnp.bfloat16)
    parts = attn_bwd(prefix_len, projected, attended, attended_grad, head_lse)
    grad_blocks = jnp.concatenate(
        [contract_rows(part, normed_low).astype(jnp.bfloat16) for part in parts] + [outer_grad]
    ).reshape(dp_count * owner_count, -1, model_width)
    normed_grad = sum(
        nn(part, inner_weight[c * model_width : (c + 1) * model_width])
        for c, part in enumerate(parts)
    )
    normed_grad, *tied = tie(normed_grad, *[a for p in produced_moved for a in p[1:]])
    totals = []
    for e in experts:
        total = produced_moved[e][0]
        for _ in produced_moved[e][1:]:
            total = total + tied.pop(0).astype(jnp.float32)
        totals.append(total.astype(jnp.bfloat16))
    produced_home = swap_owner(jnp.concatenate(totals, axis=1))
    produced_home = produced_home.reshape(owner_count, local_experts, capacity, model_width)
    returned = jnp.dot(
        slot_hot,
        produced_home.transpose(1, 0, 2, 3).reshape(expert_total * capacity, model_width),
        preferred_element_type=jnp.float32,
    )
    mixed_out = (middle + gate_value[:, None] * returned).astype(jnp.bfloat16)
    input_part, ln1_gain_part, ln1_bias_part = norm_pull(normed_grad)
    tokens_grad = middle_grad + input_part
    small = jnp.concatenate(
        [
            jnp.stack([ln1_gain_part, ln1_bias_part, ln2_gain_part, ln2_bias_part]),
            jnp.full((4, model_width), balance_part),
            router_part.T,
        ]
    )
    mixer_grad, summed = scatter_mixer(grad_blocks, small)
    mixer_grad, *late = tie(mixer_grad, *[a for g in in_grads + out_grads for a in g])
    late = [[late.pop(0) for _ in g] for g in in_grads + out_grads]
    expert_in_grad, expert_out_grad = join_grads(late, local_experts)
    return (
        mixed_out,
        tokens_grad,
        summed[0],
        summed[1],
        mixer_grad.T,
        summed[2],
        summed[3],
        summed[8:].T,
        expert_in_grad,
        expert_out_grad,
        summed[4, 0],
    )


def solution(mesh):
    in_specs = (
        P(("dp", "expert"), None),
        P(("dp", "expert"), None),
        P(("dp", "expert")),
        P(("dp", "expert")),
        P(),
        P(),
        P(None, ("dp", "expert")),
        P(),
        P(),
        P(),
        P("expert", "dp", None),
        P("expert", "dp", None),
        P(("dp", "expert"), None),
    )
    out_specs = (
        P(("dp", "expert"), None),
        P(("dp", "expert"), None),
        P(),
        P(),
        P(None, ("dp", "expert")),
        P(),
        P(),
        P(),
        P("expert", "dp", None),
        P("expert", "dp", None),
        P(),
    )
    return jax.shard_map(
        on_device, mesh=mesh, in_specs=in_specs, out_specs=out_specs, check_vma=False
    )
```

```python
import functools

import jax
import jax.numpy as jnp
from jax import lax
from jax.experimental import pallas as pl
from jax.experimental.pallas import tpu as pltpu
from jax.sharding import PartitionSpec as P


epsilon = 1e-05


def contract_rows(first_op, second_op):
    return lax.dot_general(
        first_op, second_op, (((0,), (0,)), ((), ())), preferred_element_type=jnp.float32
    )


def times_transposed(first_op, second_op):
    return lax.dot_general(
        first_op, second_op, (((1,), (1,)), ((), ())), preferred_element_type=jnp.float32
    )


BF=jnp.bfloat16; F32=jnp.float32
NEG=-1e9
QB=256
def key_extent(i, n):
    return max((i+1)*QB, 512)

def nt(a,b): return lax.dot_general(a,b,(((1,),(1,)),((),())),preferred_element_type=F32)
def nn(a,b): return lax.dot_general(a,b,(((1,),(0,)),((),())),preferred_element_type=F32)

def fill_bias(bias_ref, prefix):
    kp=lax.broadcasted_iota(jnp.int32,(QB,QB),0); qp=lax.broadcasted_iota(jnp.int32,(QB,QB),1)
    causal=kp<=qp
    bias_ref[0]=jnp.where(causal|(kp<prefix),0.0,NEG)
    bias_ref[1]=jnp.where(kp+QB<prefix,0.0,NEG)+jnp.zeros((QB,QB),F32)
    bias_ref[2]=jnp.where(causal|(kp+QB<prefix),0.0,NEG)
    bias_ref[3]=jnp.where(causal,0.0,NEG)

def block_bias(j,i):
    if j==0 and i==0: return 0
    if j==1 and i==0: return 1
    if j==1 and i==1: return 2
    if j==i: return 3
    return None

def fwd_kernel(pre_ref,q_ref,k_ref,v_ref,o_ref,lse_ref,bias_ref):
    @pl.when(pl.program_id(0)==0)
    def _(): fill_bias(bias_ref,pre_ref[0])
    T=q_ref.shape[0]
    lane=lax.broadcasted_iota(jnp.int32,(1,128),1)
    vT=v_ref[...].T
    ones=jnp.ones((16,T),BF)
    for i in range(T//QB):
        K=key_extent(i,T)
        q=q_ref[i*QB:(i+1)*QB,:]*jnp.asarray(0.125,BF)
        outs=[]
        for h in range(2):
            qh=jnp.where((lane<64) if h==0 else (lane>=64), q, jnp.zeros_like(q))
            parts=[]
            for j in range(K//QB):
                s=nt(k_ref[j*QB:(j+1)*QB,:],qh)
                b=block_bias(j,i)
                if b is not None: s=s+bias_ref[b]
                parts.append(s)
            m=functools.reduce(jnp.maximum,[jnp.max(s,axis=0,keepdims=True) for s in parts])
            vh=jnp.concatenate([vT[h*64:(h+1)*64],ones],axis=0)
            acc=None
            for j,s in enumerate(parts):
                p=jnp.exp(s-m).astype(BF)
                c=nn(vh[:,j*QB:(j+1)*QB],p)
                acc=c if acc is None else acc+c
            l=acc[64:65]
            outs.append(acc[:64]*(1.0/l))
            lse_ref[0,h:h+1,i*QB:(i+1)*QB]=m+jnp.log(l)
        o_ref[i*QB:(i+1)*QB,:]=jnp.concatenate(outs,axis=0).T.astype(BF)

def attn_fwd(prefix,proj):
    T=proj.shape[0]; W=proj.shape[1]//3; n=W//128
    return pl.pallas_call(fwd_kernel,grid=(n,),
        in_specs=[pl.BlockSpec(memory_space=pltpu.SMEM)]+[pl.BlockSpec((T,128),functools.partial(lambda c,j:(0,c*n+j),c)) for c in range(3)],
        out_specs=[pl.BlockSpec((T,128),lambda j:(0,j)),pl.BlockSpec((1,2,T),lambda j:(j,0,0))],
        out_shape=[jax.ShapeDtypeStruct((T,W),BF),jax.ShapeDtypeStruct((n,2,T),F32)],
        scratch_shapes=[pltpu.VMEM((4,QB,QB),F32)],
        compiler_params=pltpu.CompilerParams(vmem_limit_bytes=60<<20),
        name="attn_fwd")(prefix,proj,proj,proj)

def bwd_kernel(pre_ref,q_ref,k_ref,v_ref,o_ref,g_ref,lse_ref,dq_ref,dk_ref,dv_ref,bias_ref,dk_acc,dv_acc):
    @pl.when(pl.program_id(0)==0)
    def _(): fill_bias(bias_ref,pre_ref[0])
    T=q_ref.shape[0]; nb=T//QB
    lane=lax.broadcasted_iota(jnp.int32,(1,128),1)
    kT=k_ref[...].T
    started=[False]*nb
    for i in range(nb-1,-1,-1):
        K=key_extent(i,T)
        rows=slice(i*QB,(i+1)*QB)
        q=q_ref[rows,:]*jnp.asarray(0.125,BF)
        g=g_ref[rows,:]
        dT=(g.astype(F32)*o_ref[rows,:].astype(F32)).T
        outs=[]
        for h in range(2):
            sel=(lane<64) if h==0 else (lane>=64)
            qh=jnp.where(sel,q,jnp.zeros_like(q)); gh=jnp.where(sel,g,jnp.zeros_like(g))
            lse=lse_ref[0,h:h+1,rows]
            delta=jnp.sum(dT[h*64:(h+1)*64],axis=0,keepdims=True)
            dq=None
            for j in range(K//QB):
                kr=slice(j*QB,(j+1)*QB)
                s=nt(k_ref[kr,:],qh)
                b=block_bias(j,i)
                if b is not None: s=s+bias_ref[b]
                p=jnp.exp(s-lse)
                dp=nt(v_ref[kr,:],gh)
                ds=(p*(dp-delta)).astype(BF)
                dv=nn(p.astype(BF),gh)
                dk=nn(ds,qh)
                first=(i==nb-1 and h==0)
                if first: dv_acc[kr,:]=dv; dk_acc[kr,:]=dk
                else:
                    dv_acc[kr,:]+=dv; dk_acc[kr,:]+=dk
                c=nn(kT[h*64:(h+1)*64,kr],ds)
                dq=c if dq is None else dq+c
            outs.append(dq)
        dq_ref[rows,:]=(jnp.concatenate(outs,axis=0).T*0.125).astype(BF)
    dk_ref[...]=dk_acc[...].astype(BF)
    dv_ref[...]=dv_acc[...].astype(BF)

def attn_bwd(prefix,proj,att,grad,lse):
    T=proj.shape[0]; W=proj.shape[1]//3; n=W//128
    cb=lambda: pl.BlockSpec((T,128),lambda j:(0,j))
    return pl.pallas_call(bwd_kernel,grid=(n,),
        in_specs=[pl.BlockSpec(memory_space=pltpu.SMEM)]+[pl.BlockSpec((T,128),functools.partial(lambda c,j:(0,c*n+j),c)) for c in range(3)]
          +[cb(),cb(),pl.BlockSpec((1,2,T),lambda j:(j,0,0))],
        out_specs=[cb()]*3,
        out_shape=[jax.ShapeDtypeStruct((T,W),BF)]*3,
        scratch_shapes=[pltpu.VMEM((4,QB,QB),F32),pltpu.VMEM((T,128),F32),pltpu.VMEM((T,128),F32)],
        compiler_params=pltpu.CompilerParams(vmem_limit_bytes=60<<20),
        name="attn_bwd")(prefix,proj,proj,proj,att,grad,lse)

def tn(a,b): return lax.dot_general(a,b,(((0,),(0,)),((),())),preferred_element_type=F32)

ERF_TOP=3.832506856900711
ERF_NUM=(0.00022905065861350646,0.0034082910107109506,0.050955695062380861,0.18520832239976145,1.128379143519084)
ERF_DEN=(-1.1791602954361697e-7,0.000023547966471313185,0.0010179625278914885,0.014070470171167667,0.11098505178285362,0.49746925110067538,1.0)

def erf32(x):
    x=jnp.clip(x,-ERF_TOP,ERF_TOP); y=x*x
    n=ERF_NUM[0]
    for c in ERF_NUM[1:]: n=n*y+c
    d=ERF_DEN[0]
    for c in ERF_DEN[1:]: d=d*y+c
    return x*n/d

def rows_kernel(nw,tiles,rw_ref,x_ref,c_ref,*refs):
    wi_refs,wo_refs=refs[:nw],refs[nw:2*nw]
    p_ref,d_ref,act_ref,dp_ref,g_ref,rg_ref,gate_s,p_acc,d_acc=refs[2*nw:]
    step=pl.program_id(0)
    S,C,D=x_ref.shape; R=S*C
    @pl.when(step==0)
    def _():
        gate=jax.nn.sigmoid(jnp.sum(x_ref[...].reshape(R,D).astype(F32)*rw_ref[...],axis=1,keepdims=True))
        g_ref[...]=(gate*c_ref[...].reshape(R,D).astype(F32)).astype(BF)
        gate_s[...]=gate
    for w in range(nw):
        @pl.when(step//tiles==w)
        def _(w=w):
            wi=wi_refs[w][...]; wo=wo_refs[w][...]
            F=wi.shape[0]; sub=256 if F%256==0 else F
            x=x_ref[...].reshape(R,D); g=g_ref[...]
            for i in range(0,F,sub):
                pre=nt(x,wi[i:i+sub])
                da=nt(g,wo[i:i+sub])
                phi=0.5+0.5*erf32(pre*0.7071067811865476)
                act_ref[:,i:i+sub]=(pre*phi).astype(BF)
                dens=0.3989422804014327*jnp.exp(-0.5*pre*pre)
                dp_ref[:,i:i+sub]=(da*(phi+pre*dens)).astype(BF)
            p=nn(act_ref[...],wo); d=nn(dp_ref[...],wi)
            if w==0:
                @pl.when(step==0)
                def _(): p_acc[...]=p; d_acc[...]=d
                @pl.when(step>0)
                def _(): p_acc[...]+=p; d_acc[...]+=d
            else: p_acc[...]+=p; d_acc[...]+=d
    @pl.when(step==nw*tiles-1)
    def _():
        p=p_acc[...]; gate=gate_s[...]
        dot=jnp.sum(p*c_ref[...].reshape(R,D).astype(F32),axis=1,keepdims=True)
        lg=dot*(gate*(1.0-gate))
        p_ref[...]=p.reshape(S,C,D).astype(p_ref.dtype)
        d_ref[...]=(d_acc[...]+lg*rw_ref[...]).reshape(S,C,D).astype(d_ref.dtype)
        rg_ref[...]=jnp.sum(lg*x_ref[...].reshape(R,D).astype(F32),axis=0,keepdims=True)

def tile_of(Q):
    return Q

def run_rows(kind,rw,x,c,wis,wos):
    nw=len(wis); S,C,D=x.shape; Q=wis[0].shape[0]; R=S*C; tile=tile_of(Q); tiles=Q//tile
    whole=lambda shape: pl.BlockSpec(shape,lambda i:(0,)*len(shape))
    at=lambda w: (lambda i: jnp.clip(i-w*tiles,0,tiles-1))
    wspec=lambda w: pl.BlockSpec((tile,D),lambda i,f=at(w):(f(i),0))
    wide=pl.BlockSpec((None,R,tile),lambda i:(i,0,0))
    return pl.pallas_call(functools.partial(rows_kernel,nw,tiles),grid=(nw*tiles,),
        in_specs=[whole((1,D)),whole((S,C,D)),whole((S,C,D))]+[wspec(w) for w in range(nw)]*2,
        out_specs=[whole((S,C,D))]*2+[wide,wide,whole((R,D)),whole((1,D))],
        out_shape=[jax.ShapeDtypeStruct((S,C,D),kind)]*2+[jax.ShapeDtypeStruct((nw*tiles,R,tile),BF)]*2
          +[jax.ShapeDtypeStruct((R,D),BF),jax.ShapeDtypeStruct((1,D),F32)],
        scratch_shapes=[pltpu.VMEM((R,1),F32),pltpu.VMEM((R,D),F32),pltpu.VMEM((R,D),F32)],
        compiler_params=pltpu.CompilerParams(vmem_limit_bytes=60<<20),
        cost_estimate=pl.CostEstimate(flops=8*R*nw*Q*D,bytes_accessed=nw*Q*(4*D+4*R)+R*D*10,transcendentals=R*nw*Q),
        name="expert_rows")(rw,x,c,*wis,*wos)

def grads_kernel(nr,nw,tiles,*refs):
    x_refs,g_refs,act_refs,dp_refs=(refs[i*nr:(i+1)*nr] for i in range(4))
    gi_refs,go_refs=refs[4*nr:4*nr+nw],refs[4*nr+nw:]
    step=pl.program_id(0)
    S,C,D=x_refs[0].shape
    gi=sum(tn(d[...],x[...].reshape(S*C,D)) for d,x in zip(dp_refs,x_refs)).astype(BF)
    go=sum(tn(a[...],g[...]) for a,g in zip(act_refs,g_refs)).astype(BF)
    for w in range(nw):
        @pl.when(step//tiles==w)
        def _(w=w):
            gi_refs[w][...]=gi; go_refs[w][...]=go

def run_grads(nw,xs,gs,acts,dps):
    nr=len(xs); S,C,D=xs[0].shape; R=S*C; tile=acts[0].shape[2]; tiles=acts[0].shape[0]//nw; Q=tiles*tile
    whole=lambda shape: pl.BlockSpec(shape,lambda i:(0,)*len(shape))
    gspec=lambda w: pl.BlockSpec((tile,D),lambda i:(jnp.clip(i-w*tiles,0,tiles-1),0))
    outs=pl.pallas_call(functools.partial(grads_kernel,nr,nw,tiles),grid=(nw*tiles,),
        in_specs=[whole((S,C,D))]*nr+[whole((R,D))]*nr+[pl.BlockSpec((None,R,tile),lambda i:(i,0,0))]*(2*nr),
        out_specs=[gspec(w) for w in range(nw)]*2,
        out_shape=[jax.ShapeDtypeStruct((Q,D),BF)]*(2*nw),
        compiler_params=pltpu.CompilerParams(vmem_limit_bytes=60<<20),
        cost_estimate=pl.CostEstimate(flops=4*nr*R*nw*Q*D,bytes_accessed=nw*Q*D*4+nr*R*(4*D+4*nw*Q),transcendentals=0),
        name="expert_grads")(*xs,*gs,*acts,*dps)
    return list(outs[:nw]),list(outs[nw:])

MESH=pl.DeviceIdType.MESH

class Grid:
    def __init__(self):
        self.dp=lax.axis_size("dp"); self.expert=lax.axis_size("expert")
        bits=lambda n: n.bit_length()-1
        dp_bits=[("dp",1<<i) for i in range(bits(self.dp))]
        ex_bits=[("expert",1<<i) for i in range(bits(self.expert))]
        h=len(dp_bits)//2
        xs,ys,zs=dp_bits[:h],dp_bits[h:],ex_bits[1:]
        self.core=ex_bits[0]
        self.orders=[xs+ys+zs,ys+xs+zs,zs+xs+ys]
        self.all_bits=[self.core]+zs+xs+ys
    def here(self): self.at={"dp":lax.axis_index("dp"),"expert":lax.axis_index("expert")}
    def flip(self,k): return (1-2*(self.at[k[0]]//k[1]%2))*k[1]
    def partner(self,k): return {k[0]:self.at[k[0]]+self.flip(k)}
    def block(self,place):
        dp,ex=self.at["dp"],self.at["expert"]
        for k in place:
            if k[0]=="dp": dp=dp+self.flip(k)
            else: ex=ex+self.flip(k)
        return dp*self.expert+ex
    def greet(self):
        barrier=pltpu.get_barrier_semaphore()
        for k in self.all_bits: pl.semaphore_signal(barrier,inc=1,device_id=self.partner(k),device_id_type=MESH)
        pl.semaphore_wait(barrier,len(self.all_bits))

def place_of(order,code):
    m=len(order)
    return frozenset(order[i] for i in range(m) if code>>(m-1-i)&1)

class SmallSum:
    def __init__(self,g,small_ref,sum_ref,buf,arrive,ssem,rsem):
        self.g,self.sum_ref,self.buf,self.arrive,self.ssem,self.rsem=g,sum_ref,buf,arrive,ssem,rsem
        self.i=0
        buf[0]=small_ref[...]
    def start(self):
        i=self.i
        self.copy=pltpu.make_async_remote_copy(self.buf.at[i],self.arrive.at[i],self.ssem.at[i],self.rsem.at[i],device_id=self.g.partner(self.g.all_bits[i]),device_id_type=MESH)
        self.copy.start()
    def step(self):
        i=self.i
        if i>=len(self.g.all_bits): return
        self.copy.wait()
        v=self.buf[i]+self.arrive[i]
        self.i=i+1
        if self.i<len(self.g.all_bits): self.buf[i+1]=v; self.start()
        else: self.sum_ref[...]=v

def gather_kernel(nx,w_ref,small_ref,*refs):
    x_refs=refs[:nx]; out_ref,sum_ref=refs[nx:nx+2]; count=x_refs[0].shape[0]
    y_refs=refs[nx+2:nx+2+nx*count]
    s_buf,s_in,hold,ssem,rsem,cs,cr,sssem,srsem,isem,osem=refs[nx+2+nx*count:]
    g=Grid(); g.here(); g.greet()
    loads=[pltpu.make_async_copy(x_refs[i//count].at[i%count],hold.at[i],isem.at[i]) for i in range(nx*count)]
    stores=[pltpu.make_async_copy(hold.at[i],y_refs[i],osem.at[i]) for i in range(nx*count)]
    small=SmallSum(g,small_ref,sum_ref,s_buf,s_in,sssem,srsem)
    D=w_ref.shape[1]; n=len(g.orders); L=D//n
    chip=g.orders[0]; number={place_of(chip,c):c for c in range(1<<len(chip))}
    out_ref[g.block(())]=w_ref[...]
    sends=[]; core_in=[]
    def view(o,place): return out_ref.at[g.block(place),:,o*L:(o+1)*L]
    def source(o,place): return view(o,place) if place else w_ref.at[:,o*L:(o+1)*L]
    def send(o,place,k):
        to=number[place^{k}]
        c=pltpu.make_async_remote_copy(source(o,place),view(o,place),ssem.at[o,to],rsem.at[o,to],device_id=g.partner(k),device_id_type=MESH)
        c.start(); sends.append(c)
    def arrived(o,place,k):
        i=number[place]
        pltpu.make_async_remote_copy(view(o,place),view(o,place),ssem.at[o,i],rsem.at[o,i],device_id=g.partner(k),device_id_type=MESH).wait_recv()
    def across(o,place):
        i=number[place]
        c=pltpu.make_async_remote_copy(source(o,place),view(o,place),cs.at[o,i],cr.at[o,i],device_id=g.partner(g.core),device_id_type=MESH)
        c.start(); sends.append(c)
        v=view(o,place|{g.core})
        core_in.append(pltpu.make_async_remote_copy(v,v,cs.at[o,i],cr.at[o,i],device_id=g.partner(g.core),device_id_type=MESH))
    m=len(chip)
    held=[[frozenset()] for _ in g.orders]
    fresh=[[] for _ in g.orders]
    for j in range(m):
        for o,order in enumerate(g.orders):
            k=order[m-1-j]
            for p in held[o]: send(o,p,k)
            if j==0: across(o,frozenset())
        if j==0:
            small.start()
            for c in loads: c.start()
        else: small.step()
        for o,order in enumerate(g.orders):
            k=order[m-1-j]
            for p in fresh[o]:
                arrived(o,p,order[m-j]); send(o,p,k); across(o,p)
            held[o]=held[o]+fresh[o]
            fresh[o]=[p|{k} for p in held[o]]
        if j==1:
            for a,b in zip(loads,stores): a.wait(); b.start()
    for i in range(len(fresh[0])):
        for o,order in enumerate(g.orders):
            arrived(o,fresh[o][i],order[0]); across(o,fresh[o][i])
    for _ in g.all_bits: small.step()
    for c in core_in: c.wait_recv()
    for c in sends: c.wait_send()
    for c in stores: c.wait()

def gather_mixer(w,small,stacks):
    g=Grid(); n=g.dp*g.expert; half=n//2; k=len(g.orders); nb=len(g.all_bits)
    V=pl.BlockSpec(memory_space=pltpu.VMEM); S=pltpu.SemaphoreType.DMA
    D=w.shape[1]
    nx=len(stacks); count,Q,_=stacks[0].shape; A=pl.BlockSpec(memory_space=pl.ANY)
    outs=pl.pallas_call(functools.partial(gather_kernel,nx),
        in_specs=[V,V]+[A]*nx,out_specs=[V,V]+[A]*(nx*count),
        out_shape=[jax.ShapeDtypeStruct((n,)+w.shape,w.dtype),jax.ShapeDtypeStruct(small.shape,F32)]
          +[jax.ShapeDtypeStruct((Q,D),w.dtype)]*(nx*count),
        scratch_shapes=[pltpu.VMEM((nb,)+small.shape,F32)]*2+[pltpu.VMEM((nx*count,Q,D),w.dtype)]+[S((k,half))]*4+[S((nb,))]*2+[S((nx*count,))]*2,
        compiler_params=pltpu.CompilerParams(collective_id=0,has_side_effects=True,vmem_limit_bytes=60<<20),
        cost_estimate=pl.CostEstimate(flops=0,bytes_accessed=n*w.size*2,transcendentals=0),
        name="gather_mixer")(w,small,*stacks)
    return outs[0],outs[1],[list(outs[2+i*count:2+(i+1)*count]) for i in range(nx)]

def scatter_kernel(g_ref,small_ref,out_ref,sum_ref,c_in,acc,out_buf,in_buf,s_buf,s_in,csem,crem,ssem,rsem,sssem,srsem):
    g=Grid(); g.here(); g.greet()
    D=g_ref.shape[2]; n=len(g.orders); L=D//n
    chip=g.orders[0]; m=len(chip); full=1<<m
    number={place_of(chip,c):c for c in range(full)}
    sends=[]; here=set(); pending=[]
    def flush():
        for c in pending: c.start(); sends.append(c)
        pending.clear()
    small=SmallSum(g,small_ref,sum_ref,s_buf,s_in,sssem,srsem)
    cross=[]
    for s in range(full-1,-1,-1):
        for order in g.orders:
            p=place_of(order,s)
            if p in cross: continue
            cross.append(p)
    for p in cross:
        i=number[p]
        c=pltpu.make_async_remote_copy(g_ref.at[g.block(p|{g.core})],c_in.at[i],csem.at[i],crem.at[i],device_id=g.partner(g.core),device_id_type=MESH)
        c.start(); sends.append(c)
    small.start()
    def first(o,s):
        p=place_of(g.orders[o],s); i=number[p]
        if p not in here:
            here.add(p)
            pltpu.make_async_remote_copy(c_in.at[i],c_in.at[i],csem.at[i],crem.at[i],device_id=g.partner(g.core),device_id_type=MESH).wait_recv()
        lanes=slice(o*L,(o+1)*L)
        return g_ref[g.block(p),:,lanes].astype(F32)+c_in[i,:,lanes].astype(F32)
    def send(o,s,j,v):
        out_buf[o,s]=v.astype(BF)
        flush()
        pending.append(pltpu.make_async_remote_copy(out_buf.at[o,s],in_buf.at[o,s],ssem.at[o,s],rsem.at[o,s],device_id=g.partner(g.orders[o][j]),device_id_type=MESH))
    def arrived(o,s,j):
        pltpu.make_async_remote_copy(out_buf.at[o,s],in_buf.at[o,s],ssem.at[o,s],rsem.at[o,s],device_id=g.partner(g.orders[o][j]),device_id_type=MESH).wait_recv()
        return in_buf[o,s].astype(F32)
    half=full//2
    for s in range(full-1,half-1,-1):
        for o in range(n): send(o,s,0,first(o,s))
    flush()
    for s in range(half-1,-1,-1):
        for o in range(n): acc[o,s]=first(o,s)
    small.step()
    for j in range(1,m):
        half=full>>(j+1)
        for s in range(2*half-1,half-1,-1):
            for o in range(n): send(o,s,j,acc[o,s]+arrived(o,s+2*half,j-1))
        flush()
        for s in range(half-1,-1,-1):
            for o in range(n): acc[o,s]+=arrived(o,s+2*half,j-1)
        small.step()
    for o in range(n): out_ref[:,o*L:(o+1)*L]=acc[o,0]+arrived(o,1,m-1)
    for _ in g.all_bits: small.step()
    for c in sends: c.wait_send()

def scatter_mixer(grad,small):
    g=Grid(); n=len(g.orders); full=1<<len(g.orders[0]); nb=len(g.all_bits)
    _,w,D=grad.shape; L=D//n
    V=pl.BlockSpec(memory_space=pltpu.VMEM); S=pltpu.SemaphoreType.DMA
    return pl.pallas_call(scatter_kernel,in_specs=[V,V],out_specs=[V,V],
        out_shape=[jax.ShapeDtypeStruct((w,D),F32),jax.ShapeDtypeStruct(small.shape,F32)],
        scratch_shapes=[pltpu.VMEM((full,w,D),BF),pltpu.VMEM((n,full//2,w,L),F32),pltpu.VMEM((n,full,w,L),BF),pltpu.VMEM((n,full,w,L),BF),
          pltpu.VMEM((nb,)+small.shape,F32),pltpu.VMEM((nb,)+small.shape,F32),
          S((full,)),S((full,)),S((n,full)),S((n,full)),S((nb,)),S((nb,))],
        compiler_params=pltpu.CompilerParams(collective_id=1,has_side_effects=True,vmem_limit_bytes=60<<20),
        cost_estimate=pl.CostEstimate(flops=0,bytes_accessed=grad.size*4,transcendentals=0),
        name="scatter_mixer")(grad,small)

def join_kernel(count,sizes,*refs):
    outs=refs[sum(sizes):]; refs=list(refs[:sum(sizes)])
    for i,n in enumerate(sizes):
        parts=[refs.pop(0) for _ in range(n)]
        total=parts[0][...].astype(F32)
        for p in parts[1:]: total=total+p[...].astype(F32)
        outs[i//count][i%count]=total

def join_grads(groups,count):
    sizes=tuple(len(g) for g in groups); Q,D=groups[0][0].shape; tile=Q//4
    return pl.pallas_call(functools.partial(join_kernel,count,sizes),grid=(4,),
        in_specs=[pl.BlockSpec((tile,D),lambda i:(i,0))]*sum(sizes),
        out_specs=[pl.BlockSpec((count,tile,D),lambda i:(0,i,0))]*2,
        out_shape=[jax.ShapeDtypeStruct((count,Q,D),F32)]*2,
        compiler_params=pltpu.CompilerParams(vmem_limit_bytes=60<<20),
        cost_estimate=pl.CostEstimate(flops=0,bytes_accessed=Q*D*(8*count+2*sum(sizes)),transcendentals=0),
        name="join_grads")(*[p for g in groups for p in g])

ROWS=256

def stats(x):
    c=x-jnp.mean(x,axis=1,keepdims=True)
    r=lax.rsqrt(jnp.mean(c*c,axis=1,keepdims=True)+epsilon)
    return c*r,r

def norm_back(g,n,r):
    return (g-jnp.mean(g,axis=1,keepdims=True)-n*jnp.mean(g*n,axis=1,keepdims=True))*r

def one_hot(ids,start,count):
    return jnp.where(ids==start+lax.broadcasted_iota(jnp.int32,(ids.shape[0],count),1),1.0,0.0).astype(BF)

def row_call(kernel,name,T,blocked,resident,outs,sums=0):
    D=outs[0][0]
    by_rows=lambda a: pl.BlockSpec((ROWS,a),lambda i:(i,0))
    flat=[pl.BlockSpec(a.shape,lambda i,n=a.ndim:(0,)*n) if not isinstance(a,tuple) else pl.BlockSpec(a[1],a[2]) for a in resident]
    arrays=[a[0] if isinstance(a,tuple) else a for a in resident]
    return pl.pallas_call(kernel,grid=(T//ROWS,),
        in_specs=[by_rows(a.shape[1]) for a in blocked]+flat,
        out_specs=[by_rows(w) for w,_ in outs]+[pl.BlockSpec((1,D),lambda i:(0,0))]*sums,
        out_shape=[jax.ShapeDtypeStruct((T,w),d) for w,d in outs]+[jax.ShapeDtypeStruct((1,D),F32)]*sums,
        compiler_params=pltpu.CompilerParams(vmem_limit_bytes=60<<20),
        name=name)(*blocked,*arrays)

def add_sums(refs,values):
    @pl.when(pl.program_id(0)==0)
    def _():
        for r,v in zip(refs,values): r[...]=v
    @pl.when(pl.program_id(0)>0)
    def _():
        for r,v in zip(refs,values): r[...]+=v

def norm_kernel(x_ref,gain_ref,bias_ref,o_ref):
    n,_=stats(x_ref[...].astype(F32))
    o_ref[...]=(n*gain_ref[...]+bias_ref[...]).astype(BF)

def middle_kernel(a_ref,x_ref,w_ref,gain_ref,bias_ref,m_ref,o_ref):
    m=x_ref[...].astype(F32)+nt(a_ref[...],w_ref[...])
    m_ref[...]=m
    n,_=stats(m)
    o_ref[...]=(n*gain_ref[...]+bias_ref[...]).astype(BF)

def slot_kernel(base,ids_ref,x_ref,o_ref):
    B=o_ref.shape[0]; T=x_ref.shape[0]
    start=base+pl.program_id(0)*B
    hot=jnp.where(ids_ref[...]==start+lax.broadcasted_iota(jnp.int32,(B,T),0),1.0,0.0).astype(BF)
    o_ref[...]=nn(hot,x_ref[...]).astype(BF)

def slot_rows(ids,x,base,count):
    T,D=x.shape
    return pl.pallas_call(functools.partial(slot_kernel,base),grid=(count//ROWS,),
        in_specs=[pl.BlockSpec((1,T),lambda i:(0,0)),pl.BlockSpec((T,D),lambda i:(0,0))],
        out_specs=pl.BlockSpec((ROWS,D),lambda i:(i,0)),
        out_shape=jax.ShapeDtypeStruct((count,D),BF),
        compiler_params=pltpu.CompilerParams(vmem_limit_bytes=60<<20),
        cost_estimate=pl.CostEstimate(flops=2*T*D*count,bytes_accessed=8*(T+count)*D,transcendentals=0),
        name="slot_rows")(ids,x)

def norm2_back_kernel(count,ids_ref,load_ref,m_ref,c_ref,gain_ref,rw_ref,*refs):
    backs,(mg_ref,ag_ref,sg_ref,sb_ref)=refs[:count],refs[count:]
    ids=ids_ref[...]; d=nt(load_ref[...],rw_ref[...]); start=0
    for b in backs:
        d=d+nn(one_hot(ids,start,b.shape[0]),b[...]); start+=b.shape[0]
    n,r=stats(m_ref[...])
    mg=c_ref[...].astype(F32)+norm_back(d*gain_ref[...],n,r)
    mg_ref[...]=mg; ag_ref[...]=mg.astype(BF)
    add_sums((sg_ref,sb_ref),(jnp.sum(d*n,axis=0,keepdims=True),jnp.sum(d,axis=0,keepdims=True)))

def norm1_back_kernel(dq_ref,dk_ref,dv_ref,x_ref,mg_ref,gain_ref,w_ref,t_ref,sg_ref,sb_ref):
    D=x_ref.shape[1]
    d=nn(dq_ref[...],w_ref[:D])+nn(dk_ref[...],w_ref[D:2*D])+nn(dv_ref[...],w_ref[2*D:])
    n,r=stats(x_ref[...].astype(F32))
    t_ref[...]=mg_ref[...]+norm_back(d*gain_ref[...],n,r)
    add_sums((sg_ref,sb_ref),(jnp.sum(d*n,axis=0,keepdims=True),jnp.sum(d,axis=0,keepdims=True)))

def mix_kernel(ids_ref,gate_ref,m_ref,p_ref,o_ref):
    hot=one_hot(ids_ref[...],0,p_ref.shape[0])
    o_ref[...]=(m_ref[...]+gate_ref[...]*nn(hot,p_ref[...])).astype(BF)

def tie(*xs): return lax.optimization_barrier(xs)

def low_shift(n,nx,k): return [(i,i//nx*nx+(i%nx+k)%nx) for i in range(n)]
def high_shift(n,nx,k): return [(i,(i+k*nx)%n) for i in range(n)]


def on_device(
    tokens,
    routes,
    slot_order,
    prefix_len,
    ln1_gain,
    ln1_bias,
    mixer_weight,
    ln2_gain,
    ln2_bias,
    router_weight,
    expert_in,
    expert_out,
    cotangent,
):
    model_width = tokens.shape[1]
    token_count = tokens.shape[0]
    expert_total = router_weight.shape[1]
    local_experts = expert_in.shape[0]
    capacity = token_count // expert_total
    owner_count = lax.axis_size("expert")
    dp_count = lax.axis_size("dp")
    low = max(d for d in range(1, dp_count + 1) if dp_count % d == 0 and d * d <= dp_count)
    high = dp_count // low
    to_low = lambda a, k: lax.ppermute(a, "dp", low_shift(dp_count, low, k))
    to_high = lambda a, k: lax.ppermute(a, "dp", high_shift(dp_count, low, k))
    swap_owner = lambda a: lax.all_to_all(a, "expert", split_axis=0, concat_axis=0, tiled=True)
    route_flat = routes[:, 0]
    route_hot = route_flat[:, None] == jnp.arange(expert_total)[None, :]
    route_float = route_hot.astype(jnp.float32)
    count_pad = jnp.pad(jnp.sum(route_float, axis=0)[None, :], ((0, 7), (0, 128 - expert_total)))
    gathered, count_sum, (own_in, own_out) = gather_mixer(
        mixer_weight.T, count_pad, [expert_in, expert_out]
    )
    counts = count_sum[0, :expert_total]
    full_mixer = gathered.reshape(4 * model_width, model_width)
    earlier = (slot_order[None, :] < slot_order[:, None]).astype(jnp.bfloat16)
    ahead_count = jnp.dot(
        earlier, route_hot.astype(jnp.bfloat16), preferred_element_type=jnp.float32
    )
    slot_rank = jnp.sum(ahead_count * route_float, axis=1).astype(jnp.int32)
    part_rows = owner_count * capacity
    slot_index = (
        route_flat % local_experts * part_rows + route_flat // local_experts * capacity + slot_rank
    )
    is_kept = slot_rank < capacity
    slot_index = jnp.where(is_kept, slot_index, -1)
    home_index = jnp.where(is_kept, route_flat * capacity + slot_rank, -1)
    experts = range(local_experts)
    outgoing = slot_rows(home_index[None, :], cotangent, 0, expert_total * capacity)
    outgoing, full_mixer = tie(outgoing, full_mixer)
    cot_home = swap_owner(
        outgoing.reshape(owner_count, local_experts * capacity, model_width)
    )
    row_move = [(to_high, high) if e % 2 == 0 else (to_low, low) for e in experts]
    weight_move = [(to_low, low) if e % 2 == 0 else (to_high, high) for e in experts]
    spread = lambda a, move: [a] + [move[0](a, k) for k in range(1, move[1])]
    gather_back = lambda parts, move: [parts[0]] + [move[0](parts[k], -k) for k in range(1, move[1])]
    ins = [spread(own_in[e], weight_move[e]) for e in experts]
    outs = [spread(own_out[e], weight_move[e]) for e in experts]
    inner_weight = full_mixer[: 3 * model_width]
    outer_weight = full_mixer[3 * model_width :]
    (normed_low,) = row_call(
        norm_kernel, "norm1", token_count, [tokens], [ln1_gain[None, :], ln1_bias[None, :]],
        [(model_width, BF)],
    )
    projected = times_transposed(normed_low, inner_weight).astype(jnp.bfloat16)
    attended, head_lse = attn_fwd(prefix_len, projected)
    width = (model_width, model_width)
    middle, normed2_low = row_call(
        middle_kernel, "middle", token_count, [attended, tokens],
        [(full_mixer, width, lambda i: (3, 0)), ln2_gain[None, :], ln2_bias[None, :]],
        [(model_width, F32), (model_width, BF)],
    )
    chosen = jnp.sum(
        jnp.dot(normed2_low, router_weight, preferred_element_type=jnp.float32) * route_float, axis=1
    )
    gate_value = jax.nn.sigmoid(chosen)
    first_expert = lax.axis_index("expert") * local_experts
    in_grads, out_grads = [], []
    router_part = jnp.zeros((model_width, expert_total), jnp.float32)
    normed2_low, cot_home = tie(normed2_low, cot_home)
    cot_home = cot_home.reshape(owner_count, local_experts, capacity, model_width)
    cot_rows = [spread(cot_home[:, e], row_move[e]) for e in experts]
    home = []
    for e in experts:
        source = normed2_low
        if e == 1:
            source, *tied = tie(normed2_low, *[a for g in ins + outs for a in g])
            tied = [[tied.pop(0) for _ in g] for g in ins + outs]
            ins, outs = tied[:local_experts], tied[local_experts:]
        if e == 0:
            outgoing = slot_rows(slot_index[None, :], source, 0, part_rows)
        else:
            hot = slot_index[:, None] == e * part_rows + jnp.arange(part_rows)[None, :]
            outgoing = contract_rows(hot.astype(jnp.bfloat16), source).astype(jnp.bfloat16)
        home.append(swap_owner(outgoing.reshape(owner_count, capacity, model_width)))
    home[0], *cot_rows[0] = tie(home[0], *cot_rows[0])
    first_rows = spread(home[0], row_move[0])
    row_sets = [first_rows] + [spread(home[e], row_move[e]) for e in experts[1:]]
    tied = tie(*first_rows, *ins[0], *outs[0], *home[1:])
    row_sets[0], tied = list(tied[: len(first_rows)]), tied[len(first_rows) + 2 * len(ins[0]) :]
    for e in experts[1:]:
        row_sets[e][0] = tied[e - 1]
    done = {}
    before = []
    for e in experts:
        column = (jnp.arange(expert_total) == first_expert + e).astype(jnp.float32)
        router_column = jnp.sum(router_weight.astype(jnp.float32) * column[None, :], axis=1)
        for r in [*range(1, row_move[e][1]), 0]:
            rows = row_sets[e][r]
            if before:
                rows = tie(rows, *before)[0]
            kind = F32 if r == 0 else BF
            done[e, r] = run_rows(
                kind, router_column[None, :], rows, cot_rows[e][r], ins[e], outs[e]
            )
            before = [done[e, r][5]]
            router_part = router_part + done[e, r][5][0][:, None] * column[None, :]
        parts = [done[e, r] for r in range(row_move[e][1])]
        tied = tie(*before, *[p[i] for p in parts for i in (4, 2, 3)])
        in_part, out_part = run_grads(weight_move[e][1], row_sets[e], tied[1::3], tied[2::3], tied[3::3])
        before = [in_part[0]]
        for own, sums in ((in_part, in_grads), (out_part, out_grads)):
            sums.append(gather_back(own, weight_move[e]))
    returning = lambda e, i: gather_back(
        [done[e, r][i] for r in range(row_move[e][1])], row_move[e]
    )
    moved = [returning(e, 1) for e in experts]
    gate_row = done[local_experts - 1, row_move[-1][1] - 1][5]
    moved[:-1] = [tie(*moved[e], gate_row)[:-1] for e in experts[:-1]]
    back_rows = []
    for e in experts:
        total = moved[e][0]
        for a in moved[e][1:]:
            total = total + a.astype(jnp.float32)
        back_rows.append(swap_owner(total.astype(jnp.bfloat16)))
    for e in experts:
        for r in range(1, row_move[e][1]):
            done[e, r] = [tie(done[e, r][0], *moved[-1])[0]] + list(done[e, r][1:])
    produced_moved = [returning(e, 0) for e in experts]
    mean_load = jnp.sum(counts) / expert_total
    load_weight = (
        (jnp.sum(route_float * counts[None, :], axis=1) - mean_load) / mean_load / jnp.sum(counts)
    )
    balance_part = jnp.sum(load_weight * gate_value)
    load_grad = load_weight * gate_value * (1.0 - gate_value)
    load_full = (load_grad[:, None] * route_float).astype(jnp.bfloat16)
    router_part = router_part + contract_rows(normed2_low, load_full)
    load_full = tie(load_full, before[0])[0]
    middle_grad, attn_grad, ln2_gain_part, ln2_bias_part = row_call(
        functools.partial(norm2_back_kernel, local_experts), "norm2_back", token_count,
        [slot_index[:, None], load_full, middle, cotangent],
        [ln2_gain[None, :], router_weight]
        + [r.reshape(part_rows, model_width) for r in back_rows],
        [(model_width, F32), (model_width, BF)], 2,
    )
    outer_grad = contract_rows(attn_grad, attended).astype(jnp.bfloat16)
    attended_grad = nn(attn_grad, outer_weight).astype(jnp.bfloat16)
    totals = []
    for e in experts:
        total = produced_moved[e][0]
        for a in produced_moved[e][1:]:
            total = total + a.astype(jnp.float32)
        totals.append(total.astype(jnp.bfloat16))
    attended_grad, *totals = tie(attended_grad, *totals)
    produced_home = swap_owner(jnp.concatenate(totals, axis=1))
    parts = attn_bwd(prefix_len, projected, attended, attended_grad, head_lse)
    grad_blocks = jnp.concatenate(
        [contract_rows(part, normed_low).astype(jnp.bfloat16) for part in parts] + [outer_grad]
    ).reshape(dp_count * owner_count, -1, model_width)
    tokens_grad, ln1_gain_part, ln1_bias_part = row_call(
        norm1_back_kernel, "norm1_back", token_count, [*parts, tokens, middle_grad],
        [ln1_gain[None, :], (full_mixer, (3 * model_width, model_width), lambda i: (0, 0))],
        [(model_width, F32)], 2,
    )
    (mixed_out,) = row_call(
        mix_kernel, "mix", token_count, [home_index[:, None], gate_value[:, None], middle],
        [produced_home.reshape(expert_total * capacity, model_width)],
        [(model_width, BF)],
    )
    small = jnp.concatenate(
        [
            ln1_gain_part,
            ln1_bias_part,
            ln2_gain_part,
            ln2_bias_part,
            jnp.full((4, model_width), balance_part),
            router_part.T,
        ]
    )
    mixer_grad, summed = scatter_mixer(grad_blocks, small)
    mixer_grad, *late = tie(mixer_grad, *[a for g in in_grads + out_grads for a in g])
    late = [[late.pop(0) for _ in g] for g in in_grads + out_grads]
    expert_in_grad, expert_out_grad = join_grads(late, local_experts)
    return (
        mixed_out,
        tokens_grad,
        summed[0],
        summed[1],
        mixer_grad.T,
        summed[2],
        summed[3],
        summed[8:].T,
        expert_in_grad,
        expert_out_grad,
        summed[4, 0],
    )


def solution(mesh):
    in_specs = (
        P(("dp", "expert"), None),
        P(("dp", "expert"), None),
        P(("dp", "expert")),
        P(("dp", "expert")),
        P(),
        P(),
        P(None, ("dp", "expert")),
        P(),
        P(),
        P(),
        P("expert", "dp", None),
        P("expert", "dp", None),
        P(("dp", "expert"), None),
    )
    out_specs = (
        P(("dp", "expert"), None),
        P(("dp", "expert"), None),
        P(),
        P(),
        P(None, ("dp", "expert")),
        P(),
        P(),
        P(),
        P("expert", "dp", None),
        P("expert", "dp", None),
        P(),
    )
    return jax.shard_map(
        on_device, mesh=mesh, in_specs=in_specs, out_specs=out_specs, check_vma=False
    )
```

```python
import functools

import jax
import jax.numpy as jnp
from jax import lax
from jax.experimental import pallas as pl
from jax.experimental.pallas import tpu as pltpu
from jax.sharding import PartitionSpec as P


epsilon = 1e-05


def contract_rows(first_op, second_op):
    return lax.dot_general(
        first_op, second_op, (((0,), (0,)), ((), ())), preferred_element_type=jnp.float32
    )


def times_transposed(first_op, second_op):
    return lax.dot_general(
        first_op, second_op, (((1,), (1,)), ((), ())), preferred_element_type=jnp.float32
    )


BF=jnp.bfloat16; F32=jnp.float32
NEG=-1e9
QB=256
def key_extent(i, n):
    return max((i+1)*QB, 512)

def nt(a,b): return lax.dot_general(a,b,(((1,),(1,)),((),())),preferred_element_type=F32)
def nn(a,b): return lax.dot_general(a,b,(((1,),(0,)),((),())),preferred_element_type=F32)

def fill_bias(bias_ref, prefix):
    kp=lax.broadcasted_iota(jnp.int32,(QB,QB),0); qp=lax.broadcasted_iota(jnp.int32,(QB,QB),1)
    causal=kp<=qp
    bias_ref[0]=jnp.where(causal|(kp<prefix),0.0,NEG)
    bias_ref[1]=jnp.where(kp+QB<prefix,0.0,NEG)+jnp.zeros((QB,QB),F32)
    bias_ref[2]=jnp.where(causal|(kp+QB<prefix),0.0,NEG)
    bias_ref[3]=jnp.where(causal,0.0,NEG)

def block_bias(j,i):
    if j==0 and i==0: return 0
    if j==1 and i==0: return 1
    if j==1 and i==1: return 2
    if j==i: return 3
    return None

def fwd_kernel(pre_ref,q_ref,k_ref,v_ref,o_ref,lse_ref,bias_ref):
    @pl.when(pl.program_id(0)==0)
    def _(): fill_bias(bias_ref,pre_ref[0])
    T=q_ref.shape[0]
    lane=lax.broadcasted_iota(jnp.int32,(1,128),1)
    vT=v_ref[...].T
    ones=jnp.ones((16,T),BF)
    for i in range(T//QB):
        K=key_extent(i,T)
        q=q_ref[i*QB:(i+1)*QB,:]*jnp.asarray(0.125,BF)
        outs=[]
        for h in range(2):
            qh=jnp.where((lane<64) if h==0 else (lane>=64), q, jnp.zeros_like(q))
            parts=[]
            for j in range(K//QB):
                s=nt(k_ref[j*QB:(j+1)*QB,:],qh)
                b=block_bias(j,i)
                if b is not None: s=s+bias_ref[b]
                parts.append(s)
            m=functools.reduce(jnp.maximum,[jnp.max(s,axis=0,keepdims=True) for s in parts])
            vh=jnp.concatenate([vT[h*64:(h+1)*64],ones],axis=0)
            acc=None
            for j,s in enumerate(parts):
                p=jnp.exp(s-m).astype(BF)
                c=nn(vh[:,j*QB:(j+1)*QB],p)
                acc=c if acc is None else acc+c
            l=acc[64:65]
            outs.append(acc[:64]*(1.0/l))
            lse_ref[0,h:h+1,i*QB:(i+1)*QB]=m+jnp.log(l)
        o_ref[i*QB:(i+1)*QB,:]=jnp.concatenate(outs,axis=0).T.astype(BF)

def attn_fwd(prefix,proj):
    T=proj.shape[0]; W=proj.shape[1]//3; n=W//128
    return pl.pallas_call(fwd_kernel,grid=(n,),
        in_specs=[pl.BlockSpec(memory_space=pltpu.SMEM)]+[pl.BlockSpec((T,128),functools.partial(lambda c,j:(0,c*n+j),c)) for c in range(3)],
        out_specs=[pl.BlockSpec((T,128),lambda j:(0,j)),pl.BlockSpec((1,2,T),lambda j:(j,0,0))],
        out_shape=[jax.ShapeDtypeStruct((T,W),BF),jax.ShapeDtypeStruct((n,2,T),F32)],
        scratch_shapes=[pltpu.VMEM((4,QB,QB),F32)],
        compiler_params=pltpu.CompilerParams(vmem_limit_bytes=60<<20),
        name="attn_fwd")(prefix,proj,proj,proj)

def bwd_kernel(pre_ref,q_ref,k_ref,v_ref,o_ref,g_ref,lse_ref,dq_ref,dk_ref,dv_ref,bias_ref,dk_acc,dv_acc):
    @pl.when(pl.program_id(0)==0)
    def _(): fill_bias(bias_ref,pre_ref[0])
    T=q_ref.shape[0]; nb=T//QB
    lane=lax.broadcasted_iota(jnp.int32,(1,128),1)
    kT=k_ref[...].T
    started=[False]*nb
    for i in range(nb-1,-1,-1):
        K=key_extent(i,T)
        rows=slice(i*QB,(i+1)*QB)
        q=q_ref[rows,:]*jnp.asarray(0.125,BF)
        g=g_ref[rows,:]
        dT=(g.astype(F32)*o_ref[rows,:].astype(F32)).T
        outs=[]
        for h in range(2):
            sel=(lane<64) if h==0 else (lane>=64)
            qh=jnp.where(sel,q,jnp.zeros_like(q)); gh=jnp.where(sel,g,jnp.zeros_like(g))
            lse=lse_ref[0,h:h+1,rows]
            delta=jnp.sum(dT[h*64:(h+1)*64],axis=0,keepdims=True)
            dq=None
            for j in range(K//QB):
                kr=slice(j*QB,(j+1)*QB)
                s=nt(k_ref[kr,:],qh)
                b=block_bias(j,i)
                if b is not None: s=s+bias_ref[b]
                p=jnp.exp(s-lse)
                dp=nt(v_ref[kr,:],gh)
                ds=(p*(dp-delta)).astype(BF)
                dv=nn(p.astype(BF),gh)
                dk=nn(ds,qh)
                first=(i==nb-1 and h==0)
                if first: dv_acc[kr,:]=dv; dk_acc[kr,:]=dk
                else:
                    dv_acc[kr,:]+=dv; dk_acc[kr,:]+=dk
                c=nn(kT[h*64:(h+1)*64,kr],ds)
                dq=c if dq is None else dq+c
            outs.append(dq)
        dq_ref[rows,:]=(jnp.concatenate(outs,axis=0).T*0.125).astype(BF)
    dk_ref[...]=dk_acc[...].astype(BF)
    dv_ref[...]=dv_acc[...].astype(BF)

def attn_bwd(prefix,proj,att,grad,lse):
    T=proj.shape[0]; W=proj.shape[1]//3; n=W//128
    cb=lambda: pl.BlockSpec((T,128),lambda j:(0,j))
    return pl.pallas_call(bwd_kernel,grid=(n,),
        in_specs=[pl.BlockSpec(memory_space=pltpu.SMEM)]+[pl.BlockSpec((T,128),functools.partial(lambda c,j:(0,c*n+j),c)) for c in range(3)]
          +[cb(),cb(),pl.BlockSpec((1,2,T),lambda j:(j,0,0))],
        out_specs=[cb()]*3,
        out_shape=[jax.ShapeDtypeStruct((T,W),BF)]*3,
        scratch_shapes=[pltpu.VMEM((4,QB,QB),F32),pltpu.VMEM((T,128),F32),pltpu.VMEM((T,128),F32)],
        compiler_params=pltpu.CompilerParams(vmem_limit_bytes=60<<20),
        name="attn_bwd")(prefix,proj,proj,proj,att,grad,lse)

def tn(a,b): return lax.dot_general(a,b,(((0,),(0,)),((),())),preferred_element_type=F32)

ERF_TOP=3.832506856900711
ERF_NUM=(0.00022905065861350646,0.0034082910107109506,0.050955695062380861,0.18520832239976145,1.128379143519084)
ERF_DEN=(-1.1791602954361697e-7,0.000023547966471313185,0.0010179625278914885,0.014070470171167667,0.11098505178285362,0.49746925110067538,1.0)

def erf32(x):
    x=jnp.clip(x,-ERF_TOP,ERF_TOP); y=x*x
    n=ERF_NUM[0]
    for c in ERF_NUM[1:]: n=n*y+c
    d=ERF_DEN[0]
    for c in ERF_DEN[1:]: d=d*y+c
    return x*n/d

def rows_kernel(nw,tiles,rw_ref,x_ref,c_ref,*refs):
    wi_refs,wo_refs=refs[:nw],refs[nw:2*nw]
    p_ref,d_ref,act_ref,dp_ref,g_ref,rg_ref,gate_s,p_acc,d_acc=refs[2*nw:]
    step=pl.program_id(0)
    S,C,D=x_ref.shape; R=S*C
    @pl.when(step==0)
    def _():
        gate=jax.nn.sigmoid(jnp.sum(x_ref[...].reshape(R,D).astype(F32)*rw_ref[...],axis=1,keepdims=True))
        g_ref[...]=(gate*c_ref[...].reshape(R,D).astype(F32)).astype(BF)
        gate_s[...]=gate
    for w in range(nw):
        @pl.when(step//tiles==w)
        def _(w=w):
            wi=wi_refs[w][...]; wo=wo_refs[w][...]
            F=wi.shape[0]; sub=256 if F%256==0 else F
            x=x_ref[...].reshape(R,D); g=g_ref[...]
            for i in range(0,F,sub):
                pre=nt(x,wi[i:i+sub])
                da=nt(g,wo[i:i+sub])
                phi=0.5+0.5*erf32(pre*0.7071067811865476)
                act_ref[:,i:i+sub]=(pre*phi).astype(BF)
                dens=0.3989422804014327*jnp.exp(-0.5*pre*pre)
                dp_ref[:,i:i+sub]=(da*(phi+pre*dens)).astype(BF)
            p=nn(act_ref[...],wo); d=nn(dp_ref[...],wi)
            if w==0:
                @pl.when(step==0)
                def _(): p_acc[...]=p; d_acc[...]=d
                @pl.when(step>0)
                def _(): p_acc[...]+=p; d_acc[...]+=d
            else: p_acc[...]+=p; d_acc[...]+=d
    @pl.when(step==nw*tiles-1)
    def _():
        p=p_acc[...]; gate=gate_s[...]
        dot=jnp.sum(p*c_ref[...].reshape(R,D).astype(F32),axis=1,keepdims=True)
        lg=dot*(gate*(1.0-gate))
        p_ref[...]=p.reshape(S,C,D).astype(p_ref.dtype)
        d_ref[...]=(d_acc[...]+lg*rw_ref[...]).reshape(S,C,D).astype(d_ref.dtype)
        rg_ref[...]=jnp.sum(lg*x_ref[...].reshape(R,D).astype(F32),axis=0,keepdims=True)

def tile_of(Q):
    return Q

def run_rows(kind,rw,x,c,wis,wos):
    nw=len(wis); S,C,D=x.shape; Q=wis[0].shape[0]; R=S*C; tile=tile_of(Q); tiles=Q//tile
    whole=lambda shape: pl.BlockSpec(shape,lambda i:(0,)*len(shape))
    at=lambda w: (lambda i: jnp.clip(i-w*tiles,0,tiles-1))
    wspec=lambda w: pl.BlockSpec((tile,D),lambda i,f=at(w):(f(i),0))
    wide=pl.BlockSpec((None,R,tile),lambda i:(i,0,0))
    return pl.pallas_call(functools.partial(rows_kernel,nw,tiles),grid=(nw*tiles,),
        in_specs=[whole((1,D)),whole((S,C,D)),whole((S,C,D))]+[wspec(w) for w in range(nw)]*2,
        out_specs=[whole((S,C,D))]*2+[wide,wide,whole((R,D)),whole((1,D))],
        out_shape=[jax.ShapeDtypeStruct((S,C,D),kind)]*2+[jax.ShapeDtypeStruct((nw*tiles,R,tile),BF)]*2
          +[jax.ShapeDtypeStruct((R,D),BF),jax.ShapeDtypeStruct((1,D),F32)],
        scratch_shapes=[pltpu.VMEM((R,1),F32),pltpu.VMEM((R,D),F32),pltpu.VMEM((R,D),F32)],
        compiler_params=pltpu.CompilerParams(vmem_limit_bytes=60<<20),
        cost_estimate=pl.CostEstimate(flops=8*R*nw*Q*D,bytes_accessed=nw*Q*(4*D+4*R)+R*D*10,transcendentals=R*nw*Q),
        name="expert_rows")(rw,x,c,*wis,*wos)

def grads_kernel(nr,nw,tiles,*refs):
    x_refs,g_refs,act_refs,dp_refs=(refs[i*nr:(i+1)*nr] for i in range(4))
    gi_refs,go_refs=refs[4*nr:4*nr+nw],refs[4*nr+nw:]
    step=pl.program_id(0)
    S,C,D=x_refs[0].shape
    gi=sum(tn(d[...],x[...].reshape(S*C,D)) for d,x in zip(dp_refs,x_refs)).astype(BF)
    go=sum(tn(a[...],g[...]) for a,g in zip(act_refs,g_refs)).astype(BF)
    for w in range(nw):
        @pl.when(step//tiles==w)
        def _(w=w):
            gi_refs[w][...]=gi; go_refs[w][...]=go

def run_grads(nw,xs,gs,acts,dps):
    nr=len(xs); S,C,D=xs[0].shape; R=S*C; tile=acts[0].shape[2]; tiles=acts[0].shape[0]//nw; Q=tiles*tile
    whole=lambda shape: pl.BlockSpec(shape,lambda i:(0,)*len(shape))
    gspec=lambda w: pl.BlockSpec((tile,D),lambda i:(jnp.clip(i-w*tiles,0,tiles-1),0))
    outs=pl.pallas_call(functools.partial(grads_kernel,nr,nw,tiles),grid=(nw*tiles,),
        in_specs=[whole((S,C,D))]*nr+[whole((R,D))]*nr+[pl.BlockSpec((None,R,tile),lambda i:(i,0,0))]*(2*nr),
        out_specs=[gspec(w) for w in range(nw)]*2,
        out_shape=[jax.ShapeDtypeStruct((Q,D),BF)]*(2*nw),
        compiler_params=pltpu.CompilerParams(vmem_limit_bytes=60<<20),
        cost_estimate=pl.CostEstimate(flops=4*nr*R*nw*Q*D,bytes_accessed=nw*Q*D*4+nr*R*(4*D+4*nw*Q),transcendentals=0),
        name="expert_grads")(*xs,*gs,*acts,*dps)
    return list(outs[:nw]),list(outs[nw:])

MESH=pl.DeviceIdType.MESH

class Grid:
    def __init__(self):
        self.dp=lax.axis_size("dp"); self.expert=lax.axis_size("expert")
        bits=lambda n: n.bit_length()-1
        dp_bits=[("dp",1<<i) for i in range(bits(self.dp))]
        ex_bits=[("expert",1<<i) for i in range(bits(self.expert))]
        h=len(dp_bits)//2
        xs,ys,zs=dp_bits[:h],dp_bits[h:],ex_bits[1:]
        self.core=ex_bits[0]
        self.orders=[xs+ys+zs,ys+xs+zs,zs+xs+ys]
        self.all_bits=[self.core]+zs+xs+ys
    def here(self): self.at={"dp":lax.axis_index("dp"),"expert":lax.axis_index("expert")}
    def flip(self,k): return (1-2*(self.at[k[0]]//k[1]%2))*k[1]
    def partner(self,k): return {k[0]:self.at[k[0]]+self.flip(k)}
    def block(self,place):
        dp,ex=self.at["dp"],self.at["expert"]
        for k in place:
            if k[0]=="dp": dp=dp+self.flip(k)
            else: ex=ex+self.flip(k)
        return dp*self.expert+ex
    def greet(self):
        barrier=pltpu.get_barrier_semaphore()
        for k in self.all_bits: pl.semaphore_signal(barrier,inc=1,device_id=self.partner(k),device_id_type=MESH)
        pl.semaphore_wait(barrier,len(self.all_bits))

def place_of(order,code):
    m=len(order)
    return frozenset(order[i] for i in range(m) if code>>(m-1-i)&1)

class SmallSum:
    def __init__(self,g,small_ref,sum_ref,buf,arrive,ssem,rsem):
        self.g,self.sum_ref,self.buf,self.arrive,self.ssem,self.rsem=g,sum_ref,buf,arrive,ssem,rsem
        self.i=0
        buf[0]=small_ref[...]
    def start(self):
        i=self.i
        self.copy=pltpu.make_async_remote_copy(self.buf.at[i],self.arrive.at[i],self.ssem.at[i],self.rsem.at[i],device_id=self.g.partner(self.g.all_bits[i]),device_id_type=MESH)
        self.copy.start()
    def step(self):
        i=self.i
        if i>=len(self.g.all_bits): return
        self.copy.wait()
        v=self.buf[i]+self.arrive[i]
        self.i=i+1
        if self.i<len(self.g.all_bits): self.buf[i+1]=v; self.start()
        else: self.sum_ref[...]=v

def gather_kernel(nx,w_ref,small_ref,t_ref,gain_ref,bias_ref,*refs):
    x_refs=refs[:nx]; out_ref,sum_ref,normed_ref=refs[nx:nx+3]; count=x_refs[0].shape[0]
    y_refs=refs[nx+3:nx+3+nx*count]
    s_buf,s_in,hold,ssem,rsem,cs,cr,sssem,srsem,isem,osem=refs[nx+3+nx*count:]
    g=Grid(); g.here(); g.greet()
    loads=[pltpu.make_async_copy(x_refs[i//count].at[i%count],hold.at[i],isem.at[i]) for i in range(nx*count)]
    stores=[pltpu.make_async_copy(hold.at[i],y_refs[i],osem.at[i]) for i in range(nx*count)]
    small=SmallSum(g,small_ref,sum_ref,s_buf,s_in,sssem,srsem)
    D=w_ref.shape[1]; n=len(g.orders); L=D//n
    chip=g.orders[0]; number={place_of(chip,c):c for c in range(1<<len(chip))}
    out_ref[g.block(())]=w_ref[...]
    sends=[]; core_in=[]
    T=t_ref.shape[0]; waiting=[slice(i*T//8,(i+1)*T//8) for i in range(8)]
    def fill():
        if not waiting: return
        rows=waiting.pop(0)
        n,_=stats(t_ref[rows,:].astype(F32))
        normed_ref[rows,:]=(n*gain_ref[...]+bias_ref[...]).astype(BF)
    def view(o,place): return out_ref.at[g.block(place),:,o*L:(o+1)*L]
    def source(o,place): return view(o,place) if place else w_ref.at[:,o*L:(o+1)*L]
    def send(o,place,k):
        to=number[place^{k}]
        c=pltpu.make_async_remote_copy(source(o,place),view(o,place),ssem.at[o,to],rsem.at[o,to],device_id=g.partner(k),device_id_type=MESH)
        c.start(); sends.append(c)
    def arrived(o,place,k):
        i=number[place]
        pltpu.make_async_remote_copy(view(o,place),view(o,place),ssem.at[o,i],rsem.at[o,i],device_id=g.partner(k),device_id_type=MESH).wait_recv()
    def across(o,place):
        i=number[place]
        c=pltpu.make_async_remote_copy(source(o,place),view(o,place),cs.at[o,i],cr.at[o,i],device_id=g.partner(g.core),device_id_type=MESH)
        c.start(); sends.append(c)
        v=view(o,place|{g.core})
        core_in.append(pltpu.make_async_remote_copy(v,v,cs.at[o,i],cr.at[o,i],device_id=g.partner(g.core),device_id_type=MESH))
    m=len(chip)
    held=[[frozenset()] for _ in g.orders]
    fresh=[[] for _ in g.orders]
    for j in range(m):
        for o,order in enumerate(g.orders):
            k=order[m-1-j]
            for p in held[o]: send(o,p,k)
            if j==0: across(o,frozenset())
        if j==0:
            small.start()
            for c in loads: c.start()
            fill(); fill()
        else: small.step()
        for o,order in enumerate(g.orders):
            k=order[m-1-j]
            for p in fresh[o]:
                arrived(o,p,order[m-j]); send(o,p,k); across(o,p); fill()
            held[o]=held[o]+fresh[o]
            fresh[o]=[p|{k} for p in held[o]]
        if j==1:
            for a,b in zip(loads,stores): a.wait(); b.start()
    for i in range(len(fresh[0])):
        for o,order in enumerate(g.orders):
            arrived(o,fresh[o][i],order[0]); across(o,fresh[o][i])
    while waiting: fill()
    for _ in g.all_bits: small.step()
    for c in core_in: c.wait_recv()
    for c in sends: c.wait_send()
    for c in stores: c.wait()

def gather_mixer(w,small,tokens,gain,bias,stacks):
    g=Grid(); n=g.dp*g.expert; half=n//2; k=len(g.orders); nb=len(g.all_bits)
    V=pl.BlockSpec(memory_space=pltpu.VMEM); S=pltpu.SemaphoreType.DMA
    D=w.shape[1]
    nx=len(stacks); count,Q,_=stacks[0].shape; A=pl.BlockSpec(memory_space=pl.ANY)
    outs=pl.pallas_call(functools.partial(gather_kernel,nx),
        in_specs=[V]*5+[A]*nx,out_specs=[V]*3+[A]*(nx*count),
        out_shape=[jax.ShapeDtypeStruct((n,)+w.shape,w.dtype),jax.ShapeDtypeStruct(small.shape,F32),jax.ShapeDtypeStruct(tokens.shape,BF)]
          +[jax.ShapeDtypeStruct((Q,D),w.dtype)]*(nx*count),
        scratch_shapes=[pltpu.VMEM((nb,)+small.shape,F32)]*2+[pltpu.VMEM((nx*count,Q,D),w.dtype)]+[S((k,half))]*4+[S((nb,))]*2+[S((nx*count,))]*2,
        compiler_params=pltpu.CompilerParams(collective_id=0,has_side_effects=True,vmem_limit_bytes=60<<20),
        cost_estimate=pl.CostEstimate(flops=0,bytes_accessed=n*w.size*2,transcendentals=0),
        name="gather_mixer")(w,small,tokens,gain,bias,*stacks)
    return outs[:3],[list(outs[3+i*count:3+(i+1)*count]) for i in range(nx)]

def scatter_kernel(g_ref,small_ref,out_ref,sum_ref,c_in,acc,out_buf,in_buf,s_buf,s_in,csem,crem,ssem,rsem,sssem,srsem):
    g=Grid(); g.here(); g.greet()
    D=g_ref.shape[2]; n=len(g.orders); L=D//n
    chip=g.orders[0]; m=len(chip); full=1<<m
    number={place_of(chip,c):c for c in range(full)}
    sends=[]; here=set(); pending=[]
    def flush():
        for c in pending: c.start(); sends.append(c)
        pending.clear()
    small=SmallSum(g,small_ref,sum_ref,s_buf,s_in,sssem,srsem)
    cross=[]
    for s in range(full-1,-1,-1):
        for order in g.orders:
            p=place_of(order,s)
            if p in cross: continue
            cross.append(p)
    for p in cross:
        i=number[p]
        c=pltpu.make_async_remote_copy(g_ref.at[g.block(p|{g.core})],c_in.at[i],csem.at[i],crem.at[i],device_id=g.partner(g.core),device_id_type=MESH)
        c.start(); sends.append(c)
    small.start()
    def first(o,s):
        p=place_of(g.orders[o],s); i=number[p]
        if p not in here:
            here.add(p)
            pltpu.make_async_remote_copy(c_in.at[i],c_in.at[i],csem.at[i],crem.at[i],device_id=g.partner(g.core),device_id_type=MESH).wait_recv()
        lanes=slice(o*L,(o+1)*L)
        return g_ref[g.block(p),:,lanes].astype(F32)+c_in[i,:,lanes].astype(F32)
    def send(o,s,j,v):
        out_buf[o,s]=v.astype(BF)
        flush()
        pending.append(pltpu.make_async_remote_copy(out_buf.at[o,s],in_buf.at[o,s],ssem.at[o,s],rsem.at[o,s],device_id=g.partner(g.orders[o][j]),device_id_type=MESH))
    def arrived(o,s,j):
        pltpu.make_async_remote_copy(out_buf.at[o,s],in_buf.at[o,s],ssem.at[o,s],rsem.at[o,s],device_id=g.partner(g.orders[o][j]),device_id_type=MESH).wait_recv()
        return in_buf[o,s].astype(F32)
    half=full//2
    for s in range(full-1,half-1,-1):
        for o in range(n): send(o,s,0,first(o,s))
    flush()
    for s in range(half-1,-1,-1):
        for o in range(n): acc[o,s]=first(o,s)
    small.step()
    for j in range(1,m):
        half=full>>(j+1)
        for s in range(2*half-1,half-1,-1):
            for o in range(n): send(o,s,j,acc[o,s]+arrived(o,s+2*half,j-1))
        flush()
        for s in range(half-1,-1,-1):
            for o in range(n): acc[o,s]+=arrived(o,s+2*half,j-1)
        small.step()
    for o in range(n): out_ref[:,o*L:(o+1)*L]=acc[o,0]+arrived(o,1,m-1)
    for _ in g.all_bits: small.step()
    for c in sends: c.wait_send()

def scatter_mixer(grad,small):
    g=Grid(); n=len(g.orders); full=1<<len(g.orders[0]); nb=len(g.all_bits)
    _,w,D=grad.shape; L=D//n
    V=pl.BlockSpec(memory_space=pltpu.VMEM); S=pltpu.SemaphoreType.DMA
    return pl.pallas_call(scatter_kernel,in_specs=[V,V],out_specs=[V,V],
        out_shape=[jax.ShapeDtypeStruct((w,D),F32),jax.ShapeDtypeStruct(small.shape,F32)],
        scratch_shapes=[pltpu.VMEM((full,w,D),BF),pltpu.VMEM((n,full//2,w,L),F32),pltpu.VMEM((n,full,w,L),BF),pltpu.VMEM((n,full,w,L),BF),
          pltpu.VMEM((nb,)+small.shape,F32),pltpu.VMEM((nb,)+small.shape,F32),
          S((full,)),S((full,)),S((n,full)),S((n,full)),S((nb,)),S((nb,))],
        compiler_params=pltpu.CompilerParams(collective_id=1,has_side_effects=True,vmem_limit_bytes=60<<20),
        cost_estimate=pl.CostEstimate(flops=0,bytes_accessed=grad.size*4,transcendentals=0),
        name="scatter_mixer")(grad,small)

def join_kernel(count,sizes,*refs):
    outs=refs[sum(sizes):]; refs=list(refs[:sum(sizes)])
    for i,n in enumerate(sizes):
        parts=[refs.pop(0) for _ in range(n)]
        total=parts[0][...].astype(F32)
        for p in parts[1:]: total=total+p[...].astype(F32)
        outs[i//count][i%count]=total

def join_grads(groups,count):
    sizes=tuple(len(g) for g in groups); Q,D=groups[0][0].shape; tile=Q//4
    return pl.pallas_call(functools.partial(join_kernel,count,sizes),grid=(4,),
        in_specs=[pl.BlockSpec((tile,D),lambda i:(i,0))]*sum(sizes),
        out_specs=[pl.BlockSpec((count,tile,D),lambda i:(0,i,0))]*2,
        out_shape=[jax.ShapeDtypeStruct((count,Q,D),F32)]*2,
        compiler_params=pltpu.CompilerParams(vmem_limit_bytes=60<<20),
        cost_estimate=pl.CostEstimate(flops=0,bytes_accessed=Q*D*(8*count+2*sum(sizes)),transcendentals=0),
        name="join_grads")(*[p for g in groups for p in g])

ROWS=256

def stats(x):
    c=x-jnp.mean(x,axis=1,keepdims=True)
    r=lax.rsqrt(jnp.mean(c*c,axis=1,keepdims=True)+epsilon)
    return c*r,r

def norm_back(g,n,r):
    return (g-jnp.mean(g,axis=1,keepdims=True)-n*jnp.mean(g*n,axis=1,keepdims=True))*r

def one_hot(ids,start,count):
    return jnp.where(ids==start+lax.broadcasted_iota(jnp.int32,(ids.shape[0],count),1),1.0,0.0).astype(BF)

def row_call(kernel,name,T,blocked,resident,outs,sums=0):
    D=outs[0][0]
    by_rows=lambda a: pl.BlockSpec((ROWS,a),lambda i:(i,0))
    flat=[pl.BlockSpec(a.shape,lambda i,n=a.ndim:(0,)*n) if not isinstance(a,tuple) else pl.BlockSpec(a[1],a[2]) for a in resident]
    arrays=[a[0] if isinstance(a,tuple) else a for a in resident]
    return pl.pallas_call(kernel,grid=(T//ROWS,),
        in_specs=[by_rows(a.shape[1]) for a in blocked]+flat,
        out_specs=[by_rows(w) for w,_ in outs]+[pl.BlockSpec((1,D),lambda i:(0,0))]*sums,
        out_shape=[jax.ShapeDtypeStruct((T,w),d) for w,d in outs]+[jax.ShapeDtypeStruct((1,D),F32)]*sums,
        compiler_params=pltpu.CompilerParams(vmem_limit_bytes=60<<20),
        name=name)(*blocked,*arrays)

def add_sums(refs,values):
    @pl.when(pl.program_id(0)==0)
    def _():
        for r,v in zip(refs,values): r[...]=v
    @pl.when(pl.program_id(0)>0)
    def _():
        for r,v in zip(refs,values): r[...]+=v

def middle_kernel(a_ref,x_ref,w_ref,gain_ref,bias_ref,m_ref,o_ref):
    m=x_ref[...].astype(F32)+nt(a_ref[...],w_ref[...])
    m_ref[...]=m
    n,_=stats(m)
    o_ref[...]=(n*gain_ref[...]+bias_ref[...]).astype(BF)

def slot_kernel(base,ids_ref,x_ref,o_ref):
    B=o_ref.shape[0]; T=x_ref.shape[0]
    start=base+pl.program_id(0)*B
    hot=jnp.where(ids_ref[...]==start+lax.broadcasted_iota(jnp.int32,(B,T),0),1.0,0.0).astype(BF)
    o_ref[...]=nn(hot,x_ref[...]).astype(BF)

def slot_rows(ids,x,base,count):
    T,D=x.shape
    return pl.pallas_call(functools.partial(slot_kernel,base),grid=(count//ROWS,),
        in_specs=[pl.BlockSpec((1,T),lambda i:(0,0)),pl.BlockSpec((T,D),lambda i:(0,0))],
        out_specs=pl.BlockSpec((ROWS,D),lambda i:(i,0)),
        out_shape=jax.ShapeDtypeStruct((count,D),BF),
        compiler_params=pltpu.CompilerParams(vmem_limit_bytes=60<<20),
        cost_estimate=pl.CostEstimate(flops=2*T*D*count,bytes_accessed=8*(T+count)*D,transcendentals=0),
        name="slot_rows")(ids,x)

def norm2_back_kernel(count,ids_ref,load_ref,m_ref,c_ref,gain_ref,rw_ref,*refs):
    backs,(mg_ref,ag_ref,sg_ref,sb_ref)=refs[:count],refs[count:]
    ids=ids_ref[...]; d=nt(load_ref[...],rw_ref[...]); start=0
    for b in backs:
        d=d+nn(one_hot(ids,start,b.shape[0]),b[...]); start+=b.shape[0]
    n,r=stats(m_ref[...])
    mg=c_ref[...].astype(F32)+norm_back(d*gain_ref[...],n,r)
    mg_ref[...]=mg; ag_ref[...]=mg.astype(BF)
    add_sums((sg_ref,sb_ref),(jnp.sum(d*n,axis=0,keepdims=True),jnp.sum(d,axis=0,keepdims=True)))

def norm1_back_kernel(dq_ref,dk_ref,dv_ref,x_ref,mg_ref,gain_ref,w_ref,t_ref,sg_ref,sb_ref):
    D=x_ref.shape[1]
    d=nn(dq_ref[...],w_ref[:D])+nn(dk_ref[...],w_ref[D:2*D])+nn(dv_ref[...],w_ref[2*D:])
    n,r=stats(x_ref[...].astype(F32))
    t_ref[...]=mg_ref[...]+norm_back(d*gain_ref[...],n,r)
    add_sums((sg_ref,sb_ref),(jnp.sum(d*n,axis=0,keepdims=True),jnp.sum(d,axis=0,keepdims=True)))

def mix_kernel(ids_ref,gate_ref,m_ref,p_ref,o_ref):
    hot=one_hot(ids_ref[...],0,p_ref.shape[0])
    o_ref[...]=(m_ref[...]+gate_ref[...]*nn(hot,p_ref[...])).astype(BF)

def tie(*xs): return lax.optimization_barrier(xs)

def low_shift(n,nx,k): return [(i,i//nx*nx+(i%nx+k)%nx) for i in range(n)]
def high_shift(n,nx,k): return [(i,(i+k*nx)%n) for i in range(n)]


def on_device(
    tokens,
    routes,
    slot_order,
    prefix_len,
    ln1_gain,
    ln1_bias,
    mixer_weight,
    ln2_gain,
    ln2_bias,
    router_weight,
    expert_in,
    expert_out,
    cotangent,
):
    model_width = tokens.shape[1]
    token_count = tokens.shape[0]
    expert_total = router_weight.shape[1]
    local_experts = expert_in.shape[0]
    capacity = token_count // expert_total
    owner_count = lax.axis_size("expert")
    dp_count = lax.axis_size("dp")
    low = max(d for d in range(1, dp_count + 1) if dp_count % d == 0 and d * d <= dp_count)
    high = dp_count // low
    to_low = lambda a, k: lax.ppermute(a, "dp", low_shift(dp_count, low, k))
    to_high = lambda a, k: lax.ppermute(a, "dp", high_shift(dp_count, low, k))
    swap_owner = lambda a: lax.all_to_all(a, "expert", split_axis=0, concat_axis=0, tiled=True)
    route_flat = routes[:, 0]
    route_hot = route_flat[:, None] == jnp.arange(expert_total)[None, :]
    route_float = route_hot.astype(jnp.float32)
    count_pad = jnp.pad(jnp.sum(route_float, axis=0)[None, :], ((0, 7), (0, 128 - expert_total)))
    (gathered, count_sum, normed_low), (own_in, own_out) = gather_mixer(
        mixer_weight.T, count_pad, tokens, ln1_gain[None, :], ln1_bias[None, :], [expert_in, expert_out]
    )
    counts = count_sum[0, :expert_total]
    full_mixer = gathered.reshape(4 * model_width, model_width)
    earlier = (slot_order[None, :] < slot_order[:, None]).astype(jnp.bfloat16)
    ahead_count = jnp.dot(
        earlier, route_hot.astype(jnp.bfloat16), preferred_element_type=jnp.float32
    )
    slot_rank = jnp.sum(ahead_count * route_float, axis=1).astype(jnp.int32)
    part_rows = owner_count * capacity
    slot_index = (
        route_flat % local_experts * part_rows + route_flat // local_experts * capacity + slot_rank
    )
    is_kept = slot_rank < capacity
    slot_index = jnp.where(is_kept, slot_index, -1)
    home_index = jnp.where(is_kept, route_flat * capacity + slot_rank, -1)
    experts = range(local_experts)
    outgoing = slot_rows(home_index[None, :], cotangent, 0, expert_total * capacity)
    outgoing, full_mixer = tie(outgoing, full_mixer)
    cot_home = swap_owner(
        outgoing.reshape(owner_count, local_experts * capacity, model_width)
    )
    row_move = [(to_high, high) if e % 2 == 0 else (to_low, low) for e in experts]
    weight_move = [(to_low, low) if e % 2 == 0 else (to_high, high) for e in experts]
    spread = lambda a, move: [a] + [move[0](a, k) for k in range(1, move[1])]
    gather_back = lambda parts, move: [parts[0]] + [move[0](parts[k], -k) for k in range(1, move[1])]
    ins = [spread(own_in[e], weight_move[e]) for e in experts]
    outs = [spread(own_out[e], weight_move[e]) for e in experts]
    inner_weight = full_mixer[: 3 * model_width]
    outer_weight = full_mixer[3 * model_width :]
    projected = times_transposed(normed_low, inner_weight).astype(jnp.bfloat16)
    attended, head_lse = attn_fwd(prefix_len, projected)
    width = (model_width, model_width)
    middle, normed2_low = row_call(
        middle_kernel, "middle", token_count, [attended, tokens],
        [(full_mixer, width, lambda i: (3, 0)), ln2_gain[None, :], ln2_bias[None, :]],
        [(model_width, F32), (model_width, BF)],
    )
    chosen = jnp.sum(
        jnp.dot(normed2_low, router_weight, preferred_element_type=jnp.float32) * route_float, axis=1
    )
    gate_value = jax.nn.sigmoid(chosen)
    first_expert = lax.axis_index("expert") * local_experts
    in_grads, out_grads = [], []
    router_part = jnp.zeros((model_width, expert_total), jnp.float32)
    normed2_low, cot_home = tie(normed2_low, cot_home)
    cot_home = cot_home.reshape(owner_count, local_experts, capacity, model_width)
    cot_rows = [spread(cot_home[:, e], row_move[e]) for e in experts]
    home = []
    for e in experts:
        source = normed2_low
        if e == 1:
            groups = ins + outs + [cot_rows[0]]
            source, *tied = tie(normed2_low, *[a for g in groups for a in g])
            tied = [[tied.pop(0) for _ in g] for g in groups]
            ins, outs, cot_rows[0] = tied[:local_experts], tied[local_experts:-1], tied[-1]
        if e == 0:
            outgoing = slot_rows(slot_index[None, :], source, 0, part_rows)
        else:
            hot = slot_index[:, None] == e * part_rows + jnp.arange(part_rows)[None, :]
            outgoing = contract_rows(hot.astype(jnp.bfloat16), source).astype(jnp.bfloat16)
        home.append(swap_owner(outgoing.reshape(owner_count, capacity, model_width)))
    columns = [
        (jnp.arange(expert_total) == first_expert + e).astype(jnp.float32) for e in experts
    ]
    done = {}

    def rows_of(e, r, rows):
        router_column = jnp.sum(router_weight.astype(jnp.float32) * columns[e][None, :], axis=1)
        done[e, r] = run_rows(
            F32 if r == 0 else BF, router_column[None, :], rows, cot_rows[e][r], ins[e], outs[e]
        )
        return [done[e, r][5]]

    row_sets = [spread(home[0], row_move[0])]
    before = rows_of(0, 0, home[0])
    home[1:] = tie(*home[1:], *before)[:-1]
    row_sets += [spread(home[e], row_move[e]) for e in experts[1:]]
    tied = tie(*row_sets[0][1:], *home[1:])
    row_sets[0][1:], tied = list(tied[: row_move[0][1] - 1]), tied[row_move[0][1] - 1 :]
    for e in experts[1:]:
        row_sets[e][0] = tied[e - 1]
    for e in experts:
        for r in [*range(1, row_move[e][1]), 0]:
            if (e, r) not in done:
                before = rows_of(e, r, tie(row_sets[e][r], *before)[0])
            router_part = router_part + done[e, r][5][0][:, None] * columns[e][None, :]
        parts = [done[e, r] for r in range(row_move[e][1])]
        tied = tie(*before, *[p[i] for p in parts for i in (4, 2, 3)])
        in_part, out_part = run_grads(weight_move[e][1], row_sets[e], tied[1::3], tied[2::3], tied[3::3])
        before = [in_part[0]]
        for own, sums in ((in_part, in_grads), (out_part, out_grads)):
            sums.append(gather_back(own, weight_move[e]))
    returning = lambda e, i: gather_back(
        [done[e, r][i] for r in range(row_move[e][1])], row_move[e]
    )
    moved = [returning(e, 1) for e in experts]
    gate_row = done[local_experts - 1, row_move[-1][1] - 1][5]
    moved[:-1] = [tie(*moved[e], gate_row)[:-1] for e in experts[:-1]]
    back_rows = []
    for e in experts:
        total = moved[e][0]
        for a in moved[e][1:]:
            total = total + a.astype(jnp.float32)
        back_rows.append(swap_owner(total.astype(jnp.bfloat16)))
    for e in experts:
        for r in range(1, row_move[e][1]):
            done[e, r] = [tie(done[e, r][0], *moved[-1])[0]] + list(done[e, r][1:])
    produced_moved = [returning(e, 0) for e in experts]
    mean_load = jnp.sum(counts) / expert_total
    load_weight = (
        (jnp.sum(route_float * counts[None, :], axis=1) - mean_load) / mean_load / jnp.sum(counts)
    )
    balance_part = jnp.sum(load_weight * gate_value)
    load_grad = load_weight * gate_value * (1.0 - gate_value)
    load_full = (load_grad[:, None] * route_float).astype(jnp.bfloat16)
    router_part = router_part + contract_rows(normed2_low, load_full)
    load_full = tie(load_full, before[0])[0]
    middle_grad, attn_grad, ln2_gain_part, ln2_bias_part = row_call(
        functools.partial(norm2_back_kernel, local_experts), "norm2_back", token_count,
        [slot_index[:, None], load_full, middle, cotangent],
        [ln2_gain[None, :], router_weight]
        + [r.reshape(part_rows, model_width) for r in back_rows],
        [(model_width, F32), (model_width, BF)], 2,
    )
    outer_grad = contract_rows(attn_grad, attended).astype(jnp.bfloat16)
    attended_grad = nn(attn_grad, outer_weight).astype(jnp.bfloat16)
    totals = []
    for e in experts:
        total = produced_moved[e][0]
        for a in produced_moved[e][1:]:
            total = total + a.astype(jnp.float32)
        totals.append(total.astype(jnp.bfloat16))
    attended_grad, *totals = tie(attended_grad, *totals)
    produced_home = swap_owner(jnp.concatenate(totals, axis=1))
    parts = attn_bwd(prefix_len, projected, attended, attended_grad, head_lse)
    grad_blocks = jnp.concatenate(
        [contract_rows(part, normed_low).astype(jnp.bfloat16) for part in parts] + [outer_grad]
    ).reshape(dp_count * owner_count, -1, model_width)
    tokens_grad, ln1_gain_part, ln1_bias_part = row_call(
        norm1_back_kernel, "norm1_back", token_count, [*parts, tokens, middle_grad],
        [ln1_gain[None, :], (full_mixer, (3 * model_width, model_width), lambda i: (0, 0))],
        [(model_width, F32)], 2,
    )
    (mixed_out,) = row_call(
        mix_kernel, "mix", token_count, [home_index[:, None], gate_value[:, None], middle],
        [produced_home.reshape(expert_total * capacity, model_width)],
        [(model_width, BF)],
    )
    small = jnp.concatenate(
        [
            ln1_gain_part,
            ln1_bias_part,
            ln2_gain_part,
            ln2_bias_part,
            jnp.full((4, model_width), balance_part),
            router_part.T,
        ]
    )
    mixer_grad, summed = scatter_mixer(grad_blocks, small)
    mixer_grad, *late = tie(mixer_grad, *[a for g in in_grads + out_grads for a in g])
    late = [[late.pop(0) for _ in g] for g in in_grads + out_grads]
    expert_in_grad, expert_out_grad = join_grads(late, local_experts)
    return (
        mixed_out,
        tokens_grad,
        summed[0],
        summed[1],
        mixer_grad.T,
        summed[2],
        summed[3],
        summed[8:].T,
        expert_in_grad,
        expert_out_grad,
        summed[4, 0],
    )


def solution(mesh):
    in_specs = (
        P(("dp", "expert"), None),
        P(("dp", "expert"), None),
        P(("dp", "expert")),
        P(("dp", "expert")),
        P(),
        P(),
        P(None, ("dp", "expert")),
        P(),
        P(),
        P(),
        P("expert", "dp", None),
        P("expert", "dp", None),
        P(("dp", "expert"), None),
    )
    out_specs = (
        P(("dp", "expert"), None),
        P(("dp", "expert"), None),
        P(),
        P(),
        P(None, ("dp", "expert")),
        P(),
        P(),
        P(),
        P("expert", "dp", None),
        P("expert", "dp", None),
        P(),
    )
    return jax.shard_map(
        on_device, mesh=mesh, in_specs=in_specs, out_specs=out_specs, check_vma=False
    )
```

```python
import functools

import jax
import jax.numpy as jnp
from jax import lax
from jax.experimental import pallas as pl
from jax.experimental.pallas import tpu as pltpu
from jax.sharding import PartitionSpec as P


epsilon = 1e-05


def contract_rows(first_op, second_op):
    return lax.dot_general(
        first_op, second_op, (((0,), (0,)), ((), ())), preferred_element_type=jnp.float32
    )


def times_transposed(first_op, second_op):
    return lax.dot_general(
        first_op, second_op, (((1,), (1,)), ((), ())), preferred_element_type=jnp.float32
    )


BF=jnp.bfloat16; F32=jnp.float32
NEG=-1e9
QB=256
def key_extent(i, n):
    return max((i+1)*QB, 512)

def nt(a,b): return lax.dot_general(a,b,(((1,),(1,)),((),())),preferred_element_type=F32)
def nn(a,b): return lax.dot_general(a,b,(((1,),(0,)),((),())),preferred_element_type=F32)

def fill_bias(bias_ref, prefix):
    kp=lax.broadcasted_iota(jnp.int32,(QB,QB),0); qp=lax.broadcasted_iota(jnp.int32,(QB,QB),1)
    causal=kp<=qp
    bias_ref[0]=jnp.where(causal|(kp<prefix),0.0,NEG)
    bias_ref[1]=jnp.where(kp+QB<prefix,0.0,NEG)+jnp.zeros((QB,QB),F32)
    bias_ref[2]=jnp.where(causal|(kp+QB<prefix),0.0,NEG)
    bias_ref[3]=jnp.where(causal,0.0,NEG)

def block_bias(j,i):
    if j==0 and i==0: return 0
    if j==1 and i==0: return 1
    if j==1 and i==1: return 2
    if j==i: return 3
    return None

def fwd_kernel(pre_ref,q_ref,k_ref,v_ref,o_ref,lse_ref,bias_ref):
    @pl.when(pl.program_id(0)==0)
    def _(): fill_bias(bias_ref,pre_ref[0])
    T=q_ref.shape[0]
    lane=lax.broadcasted_iota(jnp.int32,(1,128),1)
    vT=v_ref[...].T
    ones=jnp.ones((16,T),BF)
    for i in range(T//QB):
        K=key_extent(i,T)
        q=q_ref[i*QB:(i+1)*QB,:]*jnp.asarray(0.125,BF)
        outs=[]
        for h in range(2):
            qh=jnp.where((lane<64) if h==0 else (lane>=64), q, jnp.zeros_like(q))
            parts=[]
            for j in range(K//QB):
                s=nt(k_ref[j*QB:(j+1)*QB,:],qh)
                b=block_bias(j,i)
                if b is not None: s=s+bias_ref[b]
                parts.append(s)
            m=functools.reduce(jnp.maximum,[jnp.max(s,axis=0,keepdims=True) for s in parts])
            vh=jnp.concatenate([vT[h*64:(h+1)*64],ones],axis=0)
            acc=None
            for j,s in enumerate(parts):
                p=jnp.exp(s-m).astype(BF)
                c=nn(vh[:,j*QB:(j+1)*QB],p)
                acc=c if acc is None else acc+c
            l=acc[64:65]
            outs.append(acc[:64]*(1.0/l))
            lse_ref[0,h:h+1,i*QB:(i+1)*QB]=m+jnp.log(l)
        o_ref[i*QB:(i+1)*QB,:]=jnp.concatenate(outs,axis=0).T.astype(BF)

def attn_fwd(prefix,proj):
    T=proj.shape[0]; W=proj.shape[1]//3; n=W//128
    return pl.pallas_call(fwd_kernel,grid=(n,),
        in_specs=[pl.BlockSpec(memory_space=pltpu.SMEM)]+[pl.BlockSpec((T,128),functools.partial(lambda c,j:(0,c*n+j),c)) for c in range(3)],
        out_specs=[pl.BlockSpec((T,128),lambda j:(0,j)),pl.BlockSpec((1,2,T),lambda j:(j,0,0))],
        out_shape=[jax.ShapeDtypeStruct((T,W),BF),jax.ShapeDtypeStruct((n,2,T),F32)],
        scratch_shapes=[pltpu.VMEM((4,QB,QB),F32)],
        compiler_params=pltpu.CompilerParams(vmem_limit_bytes=60<<20),
        name="attn_fwd")(prefix,proj,proj,proj)

def bwd_kernel(pre_ref,q_ref,k_ref,v_ref,o_ref,g_ref,lse_ref,dq_ref,dk_ref,dv_ref,bias_ref,dk_acc,dv_acc):
    @pl.when(pl.program_id(0)==0)
    def _(): fill_bias(bias_ref,pre_ref[0])
    T=q_ref.shape[0]; nb=T//QB
    lane=lax.broadcasted_iota(jnp.int32,(1,128),1)
    kT=k_ref[...].T
    started=[False]*nb
    for i in range(nb-1,-1,-1):
        K=key_extent(i,T)
        rows=slice(i*QB,(i+1)*QB)
        q=q_ref[rows,:]*jnp.asarray(0.125,BF)
        g=g_ref[rows,:]
        dT=(g.astype(F32)*o_ref[rows,:].astype(F32)).T
        outs=[]
        for h in range(2):
            sel=(lane<64) if h==0 else (lane>=64)
            qh=jnp.where(sel,q,jnp.zeros_like(q)); gh=jnp.where(sel,g,jnp.zeros_like(g))
            lse=lse_ref[0,h:h+1,rows]
            delta=jnp.sum(dT[h*64:(h+1)*64],axis=0,keepdims=True)
            dq=None
            for j in range(K//QB):
                kr=slice(j*QB,(j+1)*QB)
                s=nt(k_ref[kr,:],qh)
                b=block_bias(j,i)
                if b is not None: s=s+bias_ref[b]
                p=jnp.exp(s-lse)
                dp=nt(v_ref[kr,:],gh)
                ds=(p*(dp-delta)).astype(BF)
                dv=nn(p.astype(BF),gh)
                dk=nn(ds,qh)
                first=(i==nb-1 and h==0)
                if first: dv_acc[kr,:]=dv; dk_acc[kr,:]=dk
                else:
                    dv_acc[kr,:]+=dv; dk_acc[kr,:]+=dk
                c=nn(kT[h*64:(h+1)*64,kr],ds)
                dq=c if dq is None else dq+c
            outs.append(dq)
        dq_ref[rows,:]=(jnp.concatenate(outs,axis=0).T*0.125).astype(BF)
    dk_ref[...]=dk_acc[...].astype(BF)
    dv_ref[...]=dv_acc[...].astype(BF)

def attn_bwd(prefix,proj,att,grad,lse):
    T=proj.shape[0]; W=proj.shape[1]//3; n=W//128
    cb=lambda: pl.BlockSpec((T,128),lambda j:(0,j))
    return pl.pallas_call(bwd_kernel,grid=(n,),
        in_specs=[pl.BlockSpec(memory_space=pltpu.SMEM)]+[pl.BlockSpec((T,128),functools.partial(lambda c,j:(0,c*n+j),c)) for c in range(3)]
          +[cb(),cb(),pl.BlockSpec((1,2,T),lambda j:(j,0,0))],
        out_specs=[cb()]*3,
        out_shape=[jax.ShapeDtypeStruct((T,W),BF)]*3,
        scratch_shapes=[pltpu.VMEM((4,QB,QB),F32),pltpu.VMEM((T,128),F32),pltpu.VMEM((T,128),F32)],
        compiler_params=pltpu.CompilerParams(vmem_limit_bytes=60<<20),
        name="attn_bwd")(prefix,proj,proj,proj,att,grad,lse)

def tn(a,b): return lax.dot_general(a,b,(((0,),(0,)),((),())),preferred_element_type=F32)

ERF_TOP=3.832506856900711
ERF_NUM=(0.00022905065861350646,0.0034082910107109506,0.050955695062380861,0.18520832239976145,1.128379143519084)
ERF_DEN=(-1.1791602954361697e-7,0.000023547966471313185,0.0010179625278914885,0.014070470171167667,0.11098505178285362,0.49746925110067538,1.0)

def erf32(x):
    x=jnp.clip(x,-ERF_TOP,ERF_TOP); y=x*x
    n=ERF_NUM[0]
    for c in ERF_NUM[1:]: n=n*y+c
    d=ERF_DEN[0]
    for c in ERF_DEN[1:]: d=d*y+c
    return x*n/d

def rows_kernel(nw,tiles,rw_ref,x_ref,c_ref,*refs):
    wi_refs,wo_refs=refs[:nw],refs[nw:2*nw]
    p_ref,d_ref,act_ref,dp_ref,g_ref,rg_ref,gate_s,p_acc,d_acc=refs[2*nw:]
    step=pl.program_id(0)
    S,C,D=x_ref.shape; R=S*C
    @pl.when(step==0)
    def _():
        gate=jax.nn.sigmoid(jnp.sum(x_ref[...].reshape(R,D).astype(F32)*rw_ref[...],axis=1,keepdims=True))
        g_ref[...]=(gate*c_ref[...].reshape(R,D).astype(F32)).astype(BF)
        gate_s[...]=gate
    for w in range(nw):
        @pl.when(step//tiles==w)
        def _(w=w):
            wi=wi_refs[w][...]; wo=wo_refs[w][...]
            F=wi.shape[0]; sub=256 if F%256==0 else F
            x=x_ref[...].reshape(R,D); g=g_ref[...]
            for i in range(0,F,sub):
                pre=nt(wi[i:i+sub],x)
                da=nt(wo[i:i+sub],g)
                phi=0.5+0.5*erf32(pre*0.7071067811865476)
                act_ref[i:i+sub,:]=(pre*phi).astype(BF)
                dens=0.3989422804014327*jnp.exp(-0.5*pre*pre)
                dp_ref[i:i+sub,:]=(da*(phi+pre*dens)).astype(BF)
            p=tn(act_ref[...],wo); d=tn(dp_ref[...],wi)
            if w==0:
                @pl.when(step==0)
                def _(): p_acc[...]=p; d_acc[...]=d
                @pl.when(step>0)
                def _(): p_acc[...]+=p; d_acc[...]+=d
            else: p_acc[...]+=p; d_acc[...]+=d
    @pl.when(step==nw*tiles-1)
    def _():
        p=p_acc[...]; gate=gate_s[...]
        dot=jnp.sum(p*c_ref[...].reshape(R,D).astype(F32),axis=1,keepdims=True)
        lg=dot*(gate*(1.0-gate))
        p_ref[...]=p.reshape(S,C,D).astype(p_ref.dtype)
        d_ref[...]=(d_acc[...]+lg*rw_ref[...]).reshape(S,C,D).astype(d_ref.dtype)
        rg_ref[...]=jnp.sum(lg*x_ref[...].reshape(R,D).astype(F32),axis=0,keepdims=True)

def tile_of(Q):
    return Q

def run_rows(kind,rw,x,c,wis,wos):
    nw=len(wis); S,C,D=x.shape; Q=wis[0].shape[0]; R=S*C; tile=tile_of(Q); tiles=Q//tile
    whole=lambda shape: pl.BlockSpec(shape,lambda i:(0,)*len(shape))
    at=lambda w: (lambda i: jnp.clip(i-w*tiles,0,tiles-1))
    wspec=lambda w: pl.BlockSpec((tile,D),lambda i,f=at(w):(f(i),0))
    wide=pl.BlockSpec((None,tile,R),lambda i:(i,0,0))
    return pl.pallas_call(functools.partial(rows_kernel,nw,tiles),grid=(nw*tiles,),
        in_specs=[whole((1,D)),whole((S,C,D)),whole((S,C,D))]+[wspec(w) for w in range(nw)]*2,
        out_specs=[whole((S,C,D))]*2+[wide,wide,whole((R,D)),whole((1,D))],
        out_shape=[jax.ShapeDtypeStruct((S,C,D),kind)]*2+[jax.ShapeDtypeStruct((nw*tiles,tile,R),BF)]*2
          +[jax.ShapeDtypeStruct((R,D),BF),jax.ShapeDtypeStruct((1,D),F32)],
        scratch_shapes=[pltpu.VMEM((R,1),F32),pltpu.VMEM((R,D),F32),pltpu.VMEM((R,D),F32)],
        compiler_params=pltpu.CompilerParams(vmem_limit_bytes=60<<20),
        cost_estimate=pl.CostEstimate(flops=8*R*nw*Q*D,bytes_accessed=nw*Q*(4*D+4*R)+R*D*10,transcendentals=R*nw*Q),
        name="expert_rows")(rw,x,c,*wis,*wos)

def grads_kernel(nr,nw,tiles,*refs):
    x_refs,g_refs,act_refs,dp_refs=(refs[i*nr:(i+1)*nr] for i in range(4))
    gi_refs,go_refs=refs[4*nr:4*nr+nw],refs[4*nr+nw:]
    step=pl.program_id(0)
    S,C,D=x_refs[0].shape
    gi=sum(nn(d[...],x[...].reshape(S*C,D)) for d,x in zip(dp_refs,x_refs)).astype(BF)
    go=sum(nn(a[...],g[...]) for a,g in zip(act_refs,g_refs)).astype(BF)
    for w in range(nw):
        @pl.when(step//tiles==w)
        def _(w=w):
            gi_refs[w][...]=gi; go_refs[w][...]=go

def run_grads(nw,xs,gs,acts,dps):
    nr=len(xs); S,C,D=xs[0].shape; R=S*C; whole_tile=acts[0].shape[1]; cut=3 if whole_tile%48==0 else 1
    tile=whole_tile//cut; tiles=acts[0].shape[0]//nw*cut; Q=tiles*tile
    whole=lambda shape: pl.BlockSpec(shape,lambda i:(0,)*len(shape))
    gspec=lambda w: pl.BlockSpec((tile,D),lambda i:(jnp.clip(i-w*tiles,0,tiles-1),0))
    outs=pl.pallas_call(functools.partial(grads_kernel,nr,nw,tiles),grid=(nw*tiles,),
        in_specs=[whole((S,C,D))]*nr+[whole((R,D))]*nr+[pl.BlockSpec((None,tile,R),lambda i:(i//cut,i%cut,0))]*(2*nr),
        out_specs=[gspec(w) for w in range(nw)]*2,
        out_shape=[jax.ShapeDtypeStruct((Q,D),BF)]*(2*nw),
        compiler_params=pltpu.CompilerParams(vmem_limit_bytes=60<<20),
        cost_estimate=pl.CostEstimate(flops=4*nr*R*nw*Q*D,bytes_accessed=nw*Q*D*4+nr*R*(4*D+4*nw*Q),transcendentals=0),
        name="expert_grads")(*xs,*gs,*acts,*dps)
    return list(outs[:nw]),list(outs[nw:])

MESH=pl.DeviceIdType.MESH

class Grid:
    def __init__(self):
        self.dp=lax.axis_size("dp"); self.expert=lax.axis_size("expert")
        bits=lambda n: n.bit_length()-1
        dp_bits=[("dp",1<<i) for i in range(bits(self.dp))]
        ex_bits=[("expert",1<<i) for i in range(bits(self.expert))]
        h=len(dp_bits)//2
        xs,ys,zs=dp_bits[:h],dp_bits[h:],ex_bits[1:]
        self.core=ex_bits[0]
        self.orders=[xs+ys+zs,ys+xs+zs,zs+xs+ys]
        self.all_bits=[self.core]+zs+xs+ys
    def here(self): self.at={"dp":lax.axis_index("dp"),"expert":lax.axis_index("expert")}
    def flip(self,k): return (1-2*(self.at[k[0]]//k[1]%2))*k[1]
    def partner(self,k): return {k[0]:self.at[k[0]]+self.flip(k)}
    def block(self,place):
        dp,ex=self.at["dp"],self.at["expert"]
        for k in place:
            if k[0]=="dp": dp=dp+self.flip(k)
            else: ex=ex+self.flip(k)
        return dp*self.expert+ex
    def greet(self):
        barrier=pltpu.get_barrier_semaphore()
        for k in self.all_bits: pl.semaphore_signal(barrier,inc=1,device_id=self.partner(k),device_id_type=MESH)
        pl.semaphore_wait(barrier,len(self.all_bits))

def place_of(order,code):
    m=len(order)
    return frozenset(order[i] for i in range(m) if code>>(m-1-i)&1)

class SmallSum:
    def __init__(self,g,small_ref,sum_ref,buf,arrive,ssem,rsem):
        self.g,self.sum_ref,self.buf,self.arrive,self.ssem,self.rsem=g,sum_ref,buf,arrive,ssem,rsem
        self.i=0
        buf[0]=small_ref[...]
    def start(self):
        i=self.i
        self.copy=pltpu.make_async_remote_copy(self.buf.at[i],self.arrive.at[i],self.ssem.at[i],self.rsem.at[i],device_id=self.g.partner(self.g.all_bits[i]),device_id_type=MESH)
        self.copy.start()
    def step(self):
        i=self.i
        if i>=len(self.g.all_bits): return
        self.copy.wait()
        v=self.buf[i]+self.arrive[i]
        self.i=i+1
        if self.i<len(self.g.all_bits): self.buf[i+1]=v; self.start()
        else: self.sum_ref[...]=v

def gather_kernel(nx,w_ref,small_ref,t_ref,gain_ref,bias_ref,*refs):
    x_refs=refs[:nx]; out_ref,sum_ref,normed_ref=refs[nx:nx+3]; count=x_refs[0].shape[0]
    y_refs=refs[nx+3:nx+3+nx*count]
    s_buf,s_in,hold,ssem,rsem,cs,cr,sssem,srsem,isem,osem=refs[nx+3+nx*count:]
    g=Grid(); g.here(); g.greet()
    loads=[pltpu.make_async_copy(x_refs[i//count].at[i%count],hold.at[i],isem.at[i]) for i in range(nx*count)]
    stores=[pltpu.make_async_copy(hold.at[i],y_refs[i],osem.at[i]) for i in range(nx*count)]
    small=SmallSum(g,small_ref,sum_ref,s_buf,s_in,sssem,srsem)
    D=w_ref.shape[1]; n=len(g.orders); L=D//n
    chip=g.orders[0]; number={place_of(chip,c):c for c in range(1<<len(chip))}
    out_ref[g.block(())]=w_ref[...]
    sends=[]; core_in=[]
    T=t_ref.shape[0]; waiting=[slice(i*T//8,(i+1)*T//8) for i in range(8)]
    def fill():
        if not waiting: return
        rows=waiting.pop(0)
        n,_=stats(t_ref[rows,:].astype(F32))
        normed_ref[rows,:]=(n*gain_ref[...]+bias_ref[...]).astype(BF)
    def view(o,place): return out_ref.at[g.block(place),:,o*L:(o+1)*L]
    def source(o,place): return view(o,place) if place else w_ref.at[:,o*L:(o+1)*L]
    def send(o,place,k):
        to=number[place^{k}]
        c=pltpu.make_async_remote_copy(source(o,place),view(o,place),ssem.at[o,to],rsem.at[o,to],device_id=g.partner(k),device_id_type=MESH)
        c.start(); sends.append(c)
    def arrived(o,place,k):
        i=number[place]
        pltpu.make_async_remote_copy(view(o,place),view(o,place),ssem.at[o,i],rsem.at[o,i],device_id=g.partner(k),device_id_type=MESH).wait_recv()
    def across(o,place):
        i=number[place]
        c=pltpu.make_async_remote_copy(source(o,place),view(o,place),cs.at[o,i],cr.at[o,i],device_id=g.partner(g.core),device_id_type=MESH)
        c.start(); sends.append(c)
        v=view(o,place|{g.core})
        core_in.append(pltpu.make_async_remote_copy(v,v,cs.at[o,i],cr.at[o,i],device_id=g.partner(g.core),device_id_type=MESH))
    m=len(chip)
    held=[[frozenset()] for _ in g.orders]
    fresh=[[] for _ in g.orders]
    for j in range(m):
        for o,order in enumerate(g.orders):
            k=order[m-1-j]
            for p in held[o]: send(o,p,k)
            if j==0: across(o,frozenset())
        if j==0:
            small.start()
            for c in loads: c.start()
            fill(); fill()
        else: small.step()
        for o,order in enumerate(g.orders):
            k=order[m-1-j]
            for p in fresh[o]:
                arrived(o,p,order[m-j]); send(o,p,k); across(o,p); fill()
            held[o]=held[o]+fresh[o]
            fresh[o]=[p|{k} for p in held[o]]
        if j==1:
            for a,b in zip(loads,stores): a.wait(); b.start()
    for i in range(len(fresh[0])):
        for o,order in enumerate(g.orders):
            arrived(o,fresh[o][i],order[0]); across(o,fresh[o][i])
    while waiting: fill()
    for _ in g.all_bits: small.step()
    for c in core_in: c.wait_recv()
    for c in sends: c.wait_send()
    for c in stores: c.wait()

def gather_mixer(w,small,tokens,gain,bias,stacks):
    g=Grid(); n=g.dp*g.expert; half=n//2; k=len(g.orders); nb=len(g.all_bits)
    V=pl.BlockSpec(memory_space=pltpu.VMEM); S=pltpu.SemaphoreType.DMA
    D=w.shape[1]
    nx=len(stacks); count,Q,_=stacks[0].shape; A=pl.BlockSpec(memory_space=pl.ANY)
    outs=pl.pallas_call(functools.partial(gather_kernel,nx),
        in_specs=[V]*5+[A]*nx,out_specs=[V]*3+[A]*(nx*count),
        out_shape=[jax.ShapeDtypeStruct((n,)+w.shape,w.dtype),jax.ShapeDtypeStruct(small.shape,F32),jax.ShapeDtypeStruct(tokens.shape,BF)]
          +[jax.ShapeDtypeStruct((Q,D),w.dtype)]*(nx*count),
        scratch_shapes=[pltpu.VMEM((nb,)+small.shape,F32)]*2+[pltpu.VMEM((nx*count,Q,D),w.dtype)]+[S((k,half))]*4+[S((nb,))]*2+[S((nx*count,))]*2,
        compiler_params=pltpu.CompilerParams(collective_id=0,has_side_effects=True,vmem_limit_bytes=60<<20),
        cost_estimate=pl.CostEstimate(flops=0,bytes_accessed=n*w.size*2,transcendentals=0),
        name="gather_mixer")(w,small,tokens,gain,bias,*stacks)
    return outs[:3],[list(outs[3+i*count:3+(i+1)*count]) for i in range(nx)]

def scatter_kernel(g_ref,small_ref,out_ref,sum_ref,c_in,acc,out_buf,in_buf,s_buf,s_in,csem,crem,ssem,rsem,sssem,srsem):
    g=Grid(); g.here(); g.greet()
    D=g_ref.shape[2]; n=len(g.orders); L=D//n
    chip=g.orders[0]; m=len(chip); full=1<<m
    number={place_of(chip,c):c for c in range(full)}
    sends=[]; here=set(); pending=[]
    def flush():
        for c in pending: c.start(); sends.append(c)
        pending.clear()
    small=SmallSum(g,small_ref,sum_ref,s_buf,s_in,sssem,srsem)
    cross=[]
    for s in range(full-1,-1,-1):
        for order in g.orders:
            p=place_of(order,s)
            if p in cross: continue
            cross.append(p)
    for p in cross:
        i=number[p]
        c=pltpu.make_async_remote_copy(g_ref.at[g.block(p|{g.core})],c_in.at[i],csem.at[i],crem.at[i],device_id=g.partner(g.core),device_id_type=MESH)
        c.start(); sends.append(c)
    small.start()
    def first(o,s):
        p=place_of(g.orders[o],s); i=number[p]
        if p not in here:
            here.add(p)
            pltpu.make_async_remote_copy(c_in.at[i],c_in.at[i],csem.at[i],crem.at[i],device_id=g.partner(g.core),device_id_type=MESH).wait_recv()
        lanes=slice(o*L,(o+1)*L)
        return g_ref[g.block(p),:,lanes].astype(F32)+c_in[i,:,lanes].astype(F32)
    def send(o,s,j,v):
        out_buf[o,s]=v.astype(BF)
        flush()
        pending.append(pltpu.make_async_remote_copy(out_buf.at[o,s],in_buf.at[o,s],ssem.at[o,s],rsem.at[o,s],device_id=g.partner(g.orders[o][j]),device_id_type=MESH))
    def arrived(o,s,j):
        pltpu.make_async_remote_copy(out_buf.at[o,s],in_buf.at[o,s],ssem.at[o,s],rsem.at[o,s],device_id=g.partner(g.orders[o][j]),device_id_type=MESH).wait_recv()
        return in_buf[o,s].astype(F32)
    half=full//2
    for s in range(full-1,half-1,-1):
        for o in range(n): send(o,s,0,first(o,s))
    flush()
    for s in range(half-1,-1,-1):
        for o in range(n): acc[o,s]=first(o,s)
    small.step()
    for j in range(1,m):
        half=full>>(j+1)
        for s in range(2*half-1,half-1,-1):
            for o in range(n): send(o,s,j,acc[o,s]+arrived(o,s+2*half,j-1))
        flush()
        for s in range(half-1,-1,-1):
            for o in range(n): acc[o,s]+=arrived(o,s+2*half,j-1)
        small.step()
    for o in range(n): out_ref[:,o*L:(o+1)*L]=acc[o,0]+arrived(o,1,m-1)
    for _ in g.all_bits: small.step()
    for c in sends: c.wait_send()

def scatter_mixer(grad,small):
    g=Grid(); n=len(g.orders); full=1<<len(g.orders[0]); nb=len(g.all_bits)
    _,w,D=grad.shape; L=D//n
    V=pl.BlockSpec(memory_space=pltpu.VMEM); S=pltpu.SemaphoreType.DMA
    return pl.pallas_call(scatter_kernel,in_specs=[V,V],out_specs=[V,V],
        out_shape=[jax.ShapeDtypeStruct((w,D),F32),jax.ShapeDtypeStruct(small.shape,F32)],
        scratch_shapes=[pltpu.VMEM((full,w,D),BF),pltpu.VMEM((n,full//2,w,L),F32),pltpu.VMEM((n,full,w,L),BF),pltpu.VMEM((n,full,w,L),BF),
          pltpu.VMEM((nb,)+small.shape,F32),pltpu.VMEM((nb,)+small.shape,F32),
          S((full,)),S((full,)),S((n,full)),S((n,full)),S((nb,)),S((nb,))],
        compiler_params=pltpu.CompilerParams(collective_id=1,has_side_effects=True,vmem_limit_bytes=60<<20),
        cost_estimate=pl.CostEstimate(flops=0,bytes_accessed=grad.size*4,transcendentals=0),
        name="scatter_mixer")(grad,small)

def join_kernel(count,sizes,*refs):
    outs=refs[sum(sizes):]; refs=list(refs[:sum(sizes)])
    for i,n in enumerate(sizes):
        parts=[refs.pop(0) for _ in range(n)]
        total=parts[0][...].astype(F32)
        for p in parts[1:]: total=total+p[...].astype(F32)
        outs[i//count][i%count]=total

def join_grads(groups,count):
    sizes=tuple(len(g) for g in groups); Q,D=groups[0][0].shape; tile=Q//4
    return pl.pallas_call(functools.partial(join_kernel,count,sizes),grid=(4,),
        in_specs=[pl.BlockSpec((tile,D),lambda i:(i,0))]*sum(sizes),
        out_specs=[pl.BlockSpec((count,tile,D),lambda i:(0,i,0))]*2,
        out_shape=[jax.ShapeDtypeStruct((count,Q,D),F32)]*2,
        compiler_params=pltpu.CompilerParams(vmem_limit_bytes=60<<20),
        cost_estimate=pl.CostEstimate(flops=0,bytes_accessed=Q*D*(8*count+2*sum(sizes)),transcendentals=0),
        name="join_grads")(*[p for g in groups for p in g])

ROWS=256

def stats(x):
    c=x-jnp.mean(x,axis=1,keepdims=True)
    r=lax.rsqrt(jnp.mean(c*c,axis=1,keepdims=True)+epsilon)
    return c*r,r

def norm_back(g,n,r):
    return (g-jnp.mean(g,axis=1,keepdims=True)-n*jnp.mean(g*n,axis=1,keepdims=True))*r

def one_hot(ids,start,count):
    return jnp.where(ids==start+lax.broadcasted_iota(jnp.int32,(ids.shape[0],count),1),1.0,0.0).astype(BF)

def row_call(kernel,name,T,blocked,resident,outs,sums=0):
    D=outs[0][0]
    by_rows=lambda a: pl.BlockSpec((ROWS,a),lambda i:(i,0))
    flat=[pl.BlockSpec(a.shape,lambda i,n=a.ndim:(0,)*n) if not isinstance(a,tuple) else pl.BlockSpec(a[1],a[2]) for a in resident]
    arrays=[a[0] if isinstance(a,tuple) else a for a in resident]
    return pl.pallas_call(kernel,grid=(T//ROWS,),
        in_specs=[by_rows(a.shape[1]) for a in blocked]+flat,
        out_specs=[by_rows(w) for w,_ in outs]+[pl.BlockSpec((1,D),lambda i:(0,0))]*sums,
        out_shape=[jax.ShapeDtypeStruct((T,w),d) for w,d in outs]+[jax.ShapeDtypeStruct((1,D),F32)]*sums,
        compiler_params=pltpu.CompilerParams(vmem_limit_bytes=60<<20),
        name=name)(*blocked,*arrays)

def add_sums(refs,values):
    @pl.when(pl.program_id(0)==0)
    def _():
        for r,v in zip(refs,values): r[...]=v
    @pl.when(pl.program_id(0)>0)
    def _():
        for r,v in zip(refs,values): r[...]+=v

def middle_kernel(a_ref,x_ref,w_ref,gain_ref,bias_ref,m_ref,o_ref):
    m=x_ref[...].astype(F32)+nt(a_ref[...],w_ref[...])
    m_ref[...]=m
    n,_=stats(m)
    o_ref[...]=(n*gain_ref[...]+bias_ref[...]).astype(BF)

def slot_kernel(base,ids_ref,x_ref,o_ref):
    B=o_ref.shape[0]; T=x_ref.shape[0]
    start=base+pl.program_id(0)*B
    hot=jnp.where(ids_ref[...]==start+lax.broadcasted_iota(jnp.int32,(B,T),0),1.0,0.0).astype(BF)
    o_ref[...]=nn(hot,x_ref[...]).astype(BF)

def slot_rows(ids,x,base,count):
    T,D=x.shape
    return pl.pallas_call(functools.partial(slot_kernel,base),grid=(count//ROWS,),
        in_specs=[pl.BlockSpec((1,T),lambda i:(0,0)),pl.BlockSpec((T,D),lambda i:(0,0))],
        out_specs=pl.BlockSpec((ROWS,D),lambda i:(i,0)),
        out_shape=jax.ShapeDtypeStruct((count,D),BF),
        compiler_params=pltpu.CompilerParams(vmem_limit_bytes=60<<20),
        cost_estimate=pl.CostEstimate(flops=2*T*D*count,bytes_accessed=8*(T+count)*D,transcendentals=0),
        name="slot_rows")(ids,x)

def norm2_back_kernel(count,ids_ref,load_ref,m_ref,c_ref,gain_ref,rw_ref,*refs):
    backs,(mg_ref,ag_ref,sg_ref,sb_ref)=refs[:count],refs[count:]
    ids=ids_ref[...]; d=nt(load_ref[...],rw_ref[...]); start=0
    for b in backs:
        d=d+nn(one_hot(ids,start,b.shape[0]),b[...]); start+=b.shape[0]
    n,r=stats(m_ref[...])
    mg=c_ref[...].astype(F32)+norm_back(d*gain_ref[...],n,r)
    mg_ref[...]=mg; ag_ref[...]=mg.astype(BF)
    add_sums((sg_ref,sb_ref),(jnp.sum(d*n,axis=0,keepdims=True),jnp.sum(d,axis=0,keepdims=True)))

def norm1_back_kernel(dq_ref,dk_ref,dv_ref,x_ref,mg_ref,gain_ref,w_ref,t_ref,sg_ref,sb_ref):
    D=x_ref.shape[1]
    d=nn(dq_ref[...],w_ref[:D])+nn(dk_ref[...],w_ref[D:2*D])+nn(dv_ref[...],w_ref[2*D:])
    n,r=stats(x_ref[...].astype(F32))
    t_ref[...]=mg_ref[...]+norm_back(d*gain_ref[...],n,r)
    add_sums((sg_ref,sb_ref),(jnp.sum(d*n,axis=0,keepdims=True),jnp.sum(d,axis=0,keepdims=True)))

def mix_kernel(ids_ref,gate_ref,m_ref,p_ref,o_ref):
    hot=one_hot(ids_ref[...],0,p_ref.shape[0])
    o_ref[...]=(m_ref[...]+gate_ref[...]*nn(hot,p_ref[...])).astype(BF)

def tie(*xs): return lax.optimization_barrier(xs)

def low_shift(n,nx,k): return [(i,i//nx*nx+(i%nx+k)%nx) for i in range(n)]
def high_shift(n,nx,k): return [(i,(i+k*nx)%n) for i in range(n)]


def on_device(
    tokens,
    routes,
    slot_order,
    prefix_len,
    ln1_gain,
    ln1_bias,
    mixer_weight,
    ln2_gain,
    ln2_bias,
    router_weight,
    expert_in,
    expert_out,
    cotangent,
):
    model_width = tokens.shape[1]
    token_count = tokens.shape[0]
    expert_total = router_weight.shape[1]
    local_experts = expert_in.shape[0]
    capacity = token_count // expert_total
    owner_count = lax.axis_size("expert")
    dp_count = lax.axis_size("dp")
    low = max(d for d in range(1, dp_count + 1) if dp_count % d == 0 and d * d <= dp_count)
    high = dp_count // low
    to_low = lambda a, k: lax.ppermute(a, "dp", low_shift(dp_count, low, k))
    to_high = lambda a, k: lax.ppermute(a, "dp", high_shift(dp_count, low, k))
    swap_owner = lambda a: lax.all_to_all(a, "expert", split_axis=0, concat_axis=0, tiled=True)
    route_flat = routes[:, 0]
    route_hot = route_flat[:, None] == jnp.arange(expert_total)[None, :]
    route_float = route_hot.astype(jnp.float32)
    count_pad = jnp.pad(jnp.sum(route_float, axis=0)[None, :], ((0, 7), (0, 128 - expert_total)))
    (gathered, count_sum, normed_low), (own_in, own_out) = gather_mixer(
        mixer_weight.T, count_pad, tokens, ln1_gain[None, :], ln1_bias[None, :], [expert_in, expert_out]
    )
    counts = count_sum[0, :expert_total]
    full_mixer = gathered.reshape(4 * model_width, model_width)
    earlier = (slot_order[None, :] < slot_order[:, None]).astype(jnp.bfloat16)
    ahead_count = jnp.dot(
        earlier, route_hot.astype(jnp.bfloat16), preferred_element_type=jnp.float32
    )
    slot_rank = jnp.sum(ahead_count * route_float, axis=1).astype(jnp.int32)
    part_rows = owner_count * capacity
    slot_index = (
        route_flat % local_experts * part_rows + route_flat // local_experts * capacity + slot_rank
    )
    is_kept = slot_rank < capacity
    slot_index = jnp.where(is_kept, slot_index, -1)
    home_index = jnp.where(is_kept, route_flat * capacity + slot_rank, -1)
    experts = range(local_experts)
    outgoing = slot_rows(home_index[None, :], cotangent, 0, expert_total * capacity)
    outgoing, full_mixer = tie(outgoing, full_mixer)
    cot_home = swap_owner(
        outgoing.reshape(owner_count, local_experts * capacity, model_width)
    )
    row_move = [(to_high, high) if e % 2 == 0 else (to_low, low) for e in experts]
    weight_move = [(to_low, low) if e % 2 == 0 else (to_high, high) for e in experts]
    spread = lambda a, move: [a] + [move[0](a, k) for k in range(1, move[1])]
    gather_back = lambda parts, move: [parts[0]] + [move[0](parts[k], -k) for k in range(1, move[1])]
    ins = [spread(own_in[e], weight_move[e]) for e in experts]
    outs = [spread(own_out[e], weight_move[e]) for e in experts]
    inner_weight = full_mixer[: 3 * model_width]
    outer_weight = full_mixer[3 * model_width :]
    projected = times_transposed(normed_low, inner_weight).astype(jnp.bfloat16)
    attended, head_lse = attn_fwd(prefix_len, projected)
    width = (model_width, model_width)
    middle, normed2_low = row_call(
        middle_kernel, "middle", token_count, [attended, tokens],
        [(full_mixer, width, lambda i: (3, 0)), ln2_gain[None, :], ln2_bias[None, :]],
        [(model_width, F32), (model_width, BF)],
    )
    chosen = jnp.sum(
        jnp.dot(normed2_low, router_weight, preferred_element_type=jnp.float32) * route_float, axis=1
    )
    gate_value = jax.nn.sigmoid(chosen)
    first_expert = lax.axis_index("expert") * local_experts
    in_grads, out_grads = [], []
    router_part = jnp.zeros((model_width, expert_total), jnp.float32)
    normed2_low, cot_home = tie(normed2_low, cot_home)
    cot_home = cot_home.reshape(owner_count, local_experts, capacity, model_width)
    cot_rows = [spread(cot_home[:, e], row_move[e]) for e in experts]
    home = []
    for e in experts:
        source = normed2_low
        if e == 1:
            groups = ins + outs + [cot_rows[0]]
            source, *tied = tie(normed2_low, *[a for g in groups for a in g])
            tied = [[tied.pop(0) for _ in g] for g in groups]
            ins, outs, cot_rows[0] = tied[:local_experts], tied[local_experts:-1], tied[-1]
        if e == 0:
            outgoing = slot_rows(slot_index[None, :], source, 0, part_rows)
        else:
            hot = slot_index[:, None] == e * part_rows + jnp.arange(part_rows)[None, :]
            outgoing = contract_rows(hot.astype(jnp.bfloat16), source).astype(jnp.bfloat16)
        home.append(swap_owner(outgoing.reshape(owner_count, capacity, model_width)))
    columns = [
        (jnp.arange(expert_total) == first_expert + e).astype(jnp.float32) for e in experts
    ]
    done = {}

    def rows_of(e, r, rows):
        router_column = jnp.sum(router_weight.astype(jnp.float32) * columns[e][None, :], axis=1)
        done[e, r] = run_rows(
            F32 if r == 0 else BF, router_column[None, :], rows, cot_rows[e][r], ins[e], outs[e]
        )
        return [done[e, r][5]]

    row_sets = [spread(home[0], row_move[0])]
    before = rows_of(0, 0, home[0])
    home[1:] = tie(*home[1:], *before)[:-1]
    row_sets += [spread(home[e], row_move[e]) for e in experts[1:]]
    tied = tie(*row_sets[0][1:], *home[1:])
    row_sets[0][1:], tied = list(tied[: row_move[0][1] - 1]), tied[row_move[0][1] - 1 :]
    for e in experts[1:]:
        row_sets[e][0] = tied[e - 1]
    for e in experts:
        for r in [*range(1, row_move[e][1]), 0]:
            if (e, r) not in done:
                before = rows_of(e, r, tie(row_sets[e][r], *before)[0])
            router_part = router_part + done[e, r][5][0][:, None] * columns[e][None, :]
        parts = [done[e, r] for r in range(row_move[e][1])]
        tied = tie(*before, *[p[i] for p in parts for i in (4, 2, 3)])
        in_part, out_part = run_grads(weight_move[e][1], row_sets[e], tied[1::3], tied[2::3], tied[3::3])
        before = [in_part[0]]
        for own, sums in ((in_part, in_grads), (out_part, out_grads)):
            sums.append(gather_back(own, weight_move[e]))
    returning = lambda e, i: gather_back(
        [done[e, r][i] for r in range(row_move[e][1])], row_move[e]
    )
    moved = [returning(e, 1) for e in experts]
    gate_row = done[local_experts - 1, row_move[-1][1] - 1][5]
    moved[:-1] = [tie(*moved[e], gate_row)[:-1] for e in experts[:-1]]
    back_rows = []
    for e in experts:
        total = moved[e][0]
        for a in moved[e][1:]:
            total = total + a.astype(jnp.float32)
        back_rows.append(swap_owner(total.astype(jnp.bfloat16)))
    for e in experts:
        for r in range(1, row_move[e][1]):
            done[e, r] = [tie(done[e, r][0], *moved[-1])[0]] + list(done[e, r][1:])
    produced_moved = [returning(e, 0) for e in experts]
    mean_load = jnp.sum(counts) / expert_total
    load_weight = (
        (jnp.sum(route_float * counts[None, :], axis=1) - mean_load) / mean_load / jnp.sum(counts)
    )
    balance_part = jnp.sum(load_weight * gate_value)
    load_grad = load_weight * gate_value * (1.0 - gate_value)
    load_full = (load_grad[:, None] * route_float).astype(jnp.bfloat16)
    router_part = router_part + contract_rows(normed2_low, load_full)
    load_full = tie(load_full, before[0])[0]
    middle_grad, attn_grad, ln2_gain_part, ln2_bias_part = row_call(
        functools.partial(norm2_back_kernel, local_experts), "norm2_back", token_count,
        [slot_index[:, None], load_full, middle, cotangent],
        [ln2_gain[None, :], router_weight]
        + [r.reshape(part_rows, model_width) for r in back_rows],
        [(model_width, F32), (model_width, BF)], 2,
    )
    outer_grad = contract_rows(attn_grad, attended).astype(jnp.bfloat16)
    attended_grad = nn(attn_grad, outer_weight).astype(jnp.bfloat16)
    totals = []
    for e in experts:
        total = produced_moved[e][0]
        for a in produced_moved[e][1:]:
            total = total + a.astype(jnp.float32)
        totals.append(total.astype(jnp.bfloat16))
    attended_grad, *totals = tie(attended_grad, *totals)
    produced_home = swap_owner(jnp.concatenate(totals, axis=1))
    parts = attn_bwd(prefix_len, projected, attended, attended_grad, head_lse)
    grad_blocks = jnp.concatenate(
        [contract_rows(part, normed_low).astype(jnp.bfloat16) for part in parts] + [outer_grad]
    ).reshape(dp_count * owner_count, -1, model_width)
    tokens_grad, ln1_gain_part, ln1_bias_part = row_call(
        norm1_back_kernel, "norm1_back", token_count, [*parts, tokens, middle_grad],
        [ln1_gain[None, :], (full_mixer, (3 * model_width, model_width), lambda i: (0, 0))],
        [(model_width, F32)], 2,
    )
    (mixed_out,) = row_call(
        mix_kernel, "mix", token_count, [home_index[:, None], gate_value[:, None], middle],
        [produced_home.reshape(expert_total * capacity, model_width)],
        [(model_width, BF)],
    )
    small = jnp.concatenate(
        [
            ln1_gain_part,
            ln1_bias_part,
            ln2_gain_part,
            ln2_bias_part,
            jnp.full((4, model_width), balance_part),
            router_part.T,
        ]
    )
    mixer_grad, summed = scatter_mixer(grad_blocks, small)
    mixer_grad, *late = tie(mixer_grad, *[a for g in in_grads + out_grads for a in g])
    late = [[late.pop(0) for _ in g] for g in in_grads + out_grads]
    expert_in_grad, expert_out_grad = join_grads(late, local_experts)
    return (
        mixed_out,
        tokens_grad,
        summed[0],
        summed[1],
        mixer_grad.T,
        summed[2],
        summed[3],
        summed[8:].T,
        expert_in_grad,
        expert_out_grad,
        summed[4, 0],
    )


def solution(mesh):
    in_specs = (
        P(("dp", "expert"), None),
        P(("dp", "expert"), None),
        P(("dp", "expert")),
        P(("dp", "expert")),
        P(),
        P(),
        P(None, ("dp", "expert")),
        P(),
        P(),
        P(),
        P("expert", "dp", None),
        P("expert", "dp", None),
        P(("dp", "expert"), None),
    )
    out_specs = (
        P(("dp", "expert"), None),
        P(("dp", "expert"), None),
        P(),
        P(),
        P(None, ("dp", "expert")),
        P(),
        P(),
        P(),
        P("expert", "dp", None),
        P("expert", "dp", None),
        P(),
    )
    return jax.shard_map(
        on_device, mesh=mesh, in_specs=in_specs, out_specs=out_specs, check_vma=False
    )
```
